256 devices in a mesh: gx: 8 (over y_hi, x), gy: 32 (over y_lo, z, core).
Axes of the slice: x: 4, y: 4 (y_hi: 2, y_lo: 2; y = y_hi * 2 + y_lo), z: 8, core: 2. Of those that a mesh axis runs over, the one named last changes fastest.
Arguments:
- velocity: float32 [3, 8, 32, 8192], P(None, 'gx', 'gy'), may hold values from -6 to 6
- position: float32 [3, 8, 32, 8192], P(None, 'gx', 'gy'), may hold values from -0.5 to 128, as said below
- leaving: int32 [8, 32, 4], P('gx', 'gy'), may hold values from 256 to 1024, as said below
- grid_shift: int32 [3], replicated, may hold values from 1 to 3
- axis_index: int32 [8, 32, 8192], P('gx', 'gy'), may hold values from 0 to 15
Outputs:
- new_velocity: float32 [3, 8, 32, 12288], P(None, 'gx', 'gy')
- cell_flow: float32 [3, 8, 32, 8192], P(None, 'gx', 'gy')
The draws below stay inside these ranges and needn't reach their ends.
Inputs may be any that keep to these rules, and one draw needn't show every extreme that they name: leaving[i, j] counts the rows of tile (i, j) that leave across its lower x, upper x, lower y and upper y side, laid out from row 0 in that order; the y counts exclude rows that leave across an x side. Each x run holds at most 128 rows that also leave across the lower y side and at most 128 across the upper. Counting the rows that arrive from an x neighbour and go on, at most 1024 particles cross any side of a tile; in every draw some tile sends exactly 1024 across its lower x side and exactly 1024 across its lower y side, and some x runs hold exactly 128 such rows. `position`: positions are in cell units of the holding tile's frame and multiples of 1/4096, with z in [0, 128). Rows past the four runs have x in [0, 8) and y in [0, 8). A row of an x run lies less than 0.5 outside the tile on its side in x, with y inside or, for a corner row, less than 0.5 outside; a row of a y run has x inside and y less than 0.5 outside on its side.
All inputs are finite; a program needn't handle non-finite values.
Results may differ from the reference program's by a relative error of at most 0.0003.
Values sent between devices are 32-bit elements; how exact they have to be, the bound alone decides.
A program may use at most 64 MiB of HBM per device.

```python
import jax
import jax.numpy as jnp
from jax import lax

CXL = 8
CYL = 8
CZ = 128
P_SIZE = 8192
NAX = 16
MIG = 1024
CORN = 128
PCAP = 12288
CELLS = 8192
N_GX = 8
N_GY = 32


def layout(key):
    keys = [jax.random.fold_in(key, 101 + number) for number in range(14)]
    plane = (N_GX, N_GY)
    tiles_x = jnp.arange(N_GX, dtype=jnp.int32)[:, None]
    tiles_y = jnp.arange(N_GY, dtype=jnp.int32)[None, :]
    spot_x = jax.random.randint(keys[0], (), 0, N_GX)
    spot_y = jax.random.randint(keys[1], (), 0, N_GY)
    at_spot = (tiles_x == spot_x) & (tiles_y == spot_y)
    right_of = (tiles_x == (spot_x + 1) % N_GX) & (tiles_y == spot_y)
    left_of = (tiles_x == (spot_x + N_GX - 1) % N_GX) & (tiles_y == spot_y)
    low_x = jnp.where(at_spot, MIG, jax.random.randint(keys[2], plane, MIG // 4, MIG + 1))
    high_x = jax.random.randint(keys[3], plane, MIG // 4, MIG + 1)
    low_y = jnp.where(at_spot, MIG - 2 * CORN, jax.random.randint(keys[4], plane, MIG // 4, MIG - 2 * CORN + 1))
    high_y = jax.random.randint(keys[5], plane, MIG // 4, MIG - 2 * CORN + 1)
    lowx_down = jnp.where(right_of, CORN, jax.random.randint(keys[6], plane, 0, CORN + 1))
    lowx_up = jax.random.randint(keys[7], plane, 0, CORN + 1)
    highx_down = jnp.where(left_of, CORN, jax.random.randint(keys[8], plane, 0, CORN + 1))
    highx_up = jax.random.randint(keys[9], plane, 0, CORN + 1)
    lowx_start = jax.random.randint(keys[10], plane, 0, 1 << 20) % low_x
    highx_start = jax.random.randint(keys[11], plane, 0, 1 << 20) % high_x
    return (low_x, high_x, low_y, high_y, lowx_down, lowx_up, highx_down, highx_up, lowx_start, highx_start)


def draw_leaving(key, part):
    low_x, high_x, low_y, high_y = layout(key)[0:4]
    return jnp.stack([low_x, high_x, low_y, high_y], -1).astype(jnp.int32)


def draw_position(key, part):
    low_x, high_x, low_y, high_y, lowx_down, lowx_up, highx_down, highx_up, lowx_start, highx_start = [value[:, :, None] for value in layout(key)]
    keys = [jax.random.fold_in(key, 301 + number) for number in range(8)]
    shape = (N_GX, N_GY, P_SIZE)
    row_ids = jnp.arange(P_SIZE, dtype=jnp.int32)[None, None, :]
    inside_x = jax.random.randint(keys[0], shape, 0, 4096 * CXL).astype(jnp.float32) / 4096.0
    inside_y = jax.random.randint(keys[1], shape, 0, 4096 * CYL).astype(jnp.float32) / 4096.0
    step_x = jax.random.randint(keys[2], shape, 205, 2048).astype(jnp.float32) / 4096.0
    step_y = jax.random.randint(keys[3], shape, 205, 2048).astype(jnp.float32) / 4096.0
    cubed = jax.random.randint(keys[4], shape, 0, 256)
    cubed = cubed * cubed * cubed
    jitter = jax.random.randint(keys[5], shape, 0, CZ)
    depth = (cubed // 4096 * CZ + jitter).astype(jnp.float32) / 4096.0
    in_lowx = row_ids < low_x
    in_highx = (row_ids >= low_x) & (row_ids < low_x + high_x)
    in_lowy = (row_ids >= low_x + high_x) & (row_ids < low_x + high_x + low_y)
    in_highy = (row_ids >= low_x + high_x + low_y) & (row_ids < low_x + high_x + low_y + high_y)
    place_low = jnp.mod(row_ids - lowx_start, low_x)
    place_high = jnp.mod(row_ids - low_x - highx_start, high_x)
    corner_down = in_lowx & (place_low < lowx_down) | in_highx & (place_high < highx_down)
    corner_up = in_lowx & (place_low >= lowx_down) & (place_low < lowx_down + lowx_up) | in_highx & (place_high >= highx_down) & (place_high < highx_down + highx_up)
    coord_x = jnp.where(in_lowx, -step_x, jnp.where(in_highx, CXL + step_x, inside_x))
    coord_y = jnp.where(in_lowy | corner_down, -step_y, jnp.where(in_highy | corner_up, CYL + step_y, inside_y))
    return jnp.stack([coord_x, coord_y, depth]).astype(jnp.float32)


def with_ends(values, own_key, smallest, high):
    longest = values.shape.index(max(values.shape))
    spots = []
    for shift in (0, 1):
        where = [jax.random.randint(jax.random.fold_in(own_key, axis), (), 0, length) for axis, length in enumerate(values.shape)]
        where[longest] = (where[longest] + shift) % values.shape[longest]
        spots.append(tuple(where))
    return values.at[spots[0]].set(smallest).at[spots[1]].set(high)


def block_levels(rng, shape, cuts, smallest, largest):
    def one(axis_at, parts):
        steps = jax.random.uniform(jax.random.fold_in(jax.random.fold_in(rng, 6), axis_at), (parts,), jnp.float32, smallest / len(cuts), largest / len(cuts))
        return jnp.repeat(jnp.exp(steps), shape[axis_at] // parts).reshape((-1,) + (1,) * (len(shape) - axis_at - 1))

    loudness = one(*cuts[0])
    for cut in cuts[1:]:
        loudness = loudness * one(*cut)
    return loudness


def gaussian(stream_key, shape, scale, most, cuts=(), kind=jnp.bfloat16):
    array = scale * jax.random.normal(stream_key, shape, jnp.float32)
    if cuts:
        array = array * block_levels(stream_key, shape, cuts, -0.22, 0.18)
    return jnp.clip(array, -most, most).astype(kind)


def setup_inputs(seed: int = 0) -> dict:
    splits = jax.random.split(jax.random.key(seed), 6)
    velocity = gaussian(splits[0], (3, N_GX, N_GY, P_SIZE), 1.0, 6.0, ((1, 8), (2, 32)), jnp.float32)
    position = draw_position(jax.random.fold_in(splits[5], 71), 0)
    leaving = draw_leaving(jax.random.fold_in(splits[5], 71), 0)
    grid_shift = jax.random.randint(splits[3], (3,), 1, 4).astype(jnp.int32)
    axis_index = with_ends(jax.random.randint(splits[4], (N_GX, N_GY, CELLS), 0, NAX), jax.random.fold_in(splits[4], 1), 0, NAX - 1).astype(jnp.int32)
    return dict(velocity=velocity, position=position, leaving=leaving, grid_shift=grid_shift, axis_index=axis_index)


COS_TURN = -0.6427876096865393
SIN_TURN = 0.766044443118978
GOLDEN_TURN = 2.399963229728653

def axis_table():
    number = jnp.arange(NAX).astype(jnp.float32)
    height = 1.0 - (2.0 * number + 1.0) / NAX
    radius = jnp.sqrt(1.0 - height * height)
    phase = number * GOLDEN_TURN
    return jnp.stack([radius * jnp.cos(phase), radius * jnp.sin(phase), height])

def take_run(particle_rows, start, count):
    block_rows = lax.dynamic_slice_in_dim(particle_rows, start, MIG, 1)
    slot_live = jnp.arange(MIG, dtype=jnp.int32) < count
    return (jnp.where(slot_live[None, :], block_rows, 0.0), slot_live)

def forward(run_rows, run_count, arrivals, chosen):
    flags = chosen.astype(jnp.int32)
    rank_ids = (jnp.cumsum(flags) - flags).astype(jnp.int32)
    slot_ids = jnp.where(chosen, run_count + rank_ids, MIG).astype(jnp.int32)
    merged = run_rows.at[:, slot_ids].set(arrivals, mode='drop')
    filled = (run_count + jnp.sum(flags)).astype(jnp.int32)
    return (merged, jnp.arange(MIG, dtype=jnp.int32) < filled)

def neighbours(device):
    tile_x = device // N_GY
    tile_y = device % N_GY
    return ((tile_x - 1) % N_GX * N_GY + tile_y, (tile_x + 1) % N_GX * N_GY + tile_y, tile_x * N_GY + (tile_y - 1) % N_GY, tile_x * N_GY + (tile_y + 1) % N_GY)

def cell_ids(particle_rows, living, grid_shift):
    extent = (CXL + 1) * (CYL + 1) * CZ
    sub_cells = jnp.floor(4.0 * particle_rows[3:6]).astype(jnp.int32)
    cell_x = (sub_cells[0] + grid_shift[0]) // 4
    cell_y = (sub_cells[1] + grid_shift[1]) // 4
    cell_z = (sub_cells[2] + grid_shift[2]) // 4 % CZ
    flat_ids = (cell_x * (CYL + 1) + cell_y) * CZ + cell_z
    return jnp.where(living, flat_ids, extent).astype(jnp.int32)

def rotate(velocity_rows, mean_rows, axis_rows, living):
    relative = velocity_rows - mean_rows
    cross = jnp.stack([axis_rows[1] * relative[2] - axis_rows[2] * relative[1], axis_rows[2] * relative[0] - axis_rows[0] * relative[2], axis_rows[0] * relative[1] - axis_rows[1] * relative[0]])
    along = lax.optimization_barrier(jnp.sum(axis_rows * relative, axis=0))
    turned = mean_rows + COS_TURN * relative + SIN_TURN * cross + (1.0 - COS_TURN) * along[None, :] * axis_rows
    return jnp.where(living[None, :], turned, 0.0)

def reference(velocity, position, leaving, grid_shift, axis_index):
    devices = N_GX * N_GY
    extent = (CXL + 1) * (CYL + 1) * CZ
    all_rows = jnp.concatenate([velocity, position], 0).transpose(1, 2, 0, 3).reshape(devices, 6, P_SIZE)
    all_counts = leaving.reshape(devices, 4)
    device_ids = jnp.arange(devices, dtype=jnp.int32)

    def runs(device):
        particle_rows = all_rows[device]
        moving = all_counts[device]
        low_x = take_run(particle_rows, 0, moving[0])
        high_x = take_run(particle_rows, moving[0], moving[1])
        low_y = take_run(particle_rows, moving[0] + moving[1], moving[2])
        high_y = take_run(particle_rows, moving[0] + moving[1] + moving[2], moving[3])
        return low_x + high_x + low_y + high_y
    low_x, low_x_live, high_x, high_x_live, low_y_run, low_y_run_live, high_y_run, high_y_run_live = lax.map(runs, device_ids)

    def arrived_x(device):
        from_left, from_right, below, above = neighbours(device)
        arrivals = jnp.concatenate([high_x[from_left].at[3].add(-CXL), low_x[from_right].at[3].add(CXL)], 1)
        arrive_live = jnp.concatenate([high_x_live[from_left], low_x_live[from_right]])
        return (arrivals, arrive_live)

    def y_buffers(device):
        arrivals, arrive_live = arrived_x(device)
        moving = all_counts[device]
        downward = arrive_live & (arrivals[4] < 0.0)
        upward = arrive_live & (arrivals[4] >= CYL)
        low_buffer = forward(low_y_run[device], moving[2], arrivals, downward)
        high_buffer = forward(high_y_run[device], moving[3], arrivals, upward)
        return low_buffer + high_buffer
    low_y, low_y_live, high_y, high_y_live = lax.map(y_buffers, device_ids)

    def particle_set(device):
        from_left, from_right, below, above = neighbours(device)
        arrivals, arrive_live = arrived_x(device)
        staying = arrive_live & (arrivals[4] >= 0.0) & (arrivals[4] < CYL)
        from_below = high_y[below].at[4].add(-CYL)
        from_above = low_y[above].at[4].add(CYL)
        moving = all_counts[device]
        own_live = jnp.arange(P_SIZE, dtype=jnp.int32) >= moving[0] + moving[1] + moving[2] + moving[3]
        settled = jnp.concatenate([all_rows[device], arrivals, from_below, from_above], 1)
        living = jnp.concatenate([own_live, staying, high_y_live[below], low_y_live[above]])
        return (settled, living)

    def partials(device):
        settled, living = particle_set(device)
        flat_ids = cell_ids(settled, living, grid_shift)
        weights = jnp.stack([jnp.ones_like(settled[0]), settled[0], settled[1], settled[2]], 1)
        sums = jax.ops.segment_sum(weights, flat_ids, num_segments=extent + 1)[:extent]
        return sums.T.reshape(4, CXL + 1, CYL + 1, CZ)
    grids = lax.map(partials, device_ids).reshape(N_GX, N_GY, 4, CXL + 1, CYL + 1, CZ)
    owned = grids[:, :, :, :CXL, :CYL]
    owned = owned.at[:, :, :, 0, :].add(jnp.roll(grids[:, :, :, CXL, :CYL], 1, axis=0))
    owned = owned.at[:, :, :, :, 0].add(jnp.roll(grids[:, :, :, :CXL, CYL], 1, axis=1))
    owned = owned.at[:, :, :, 0, 0].add(jnp.roll(grids[:, :, :, CXL, CYL], (1, 1), axis=(0, 1)))
    mean_cells = owned[:, :, 1:4] / jnp.maximum(owned[:, :, 0:1], 1.0)
    axes_cells = axis_table()[:, axis_index].reshape(3, N_GX, N_GY, CXL, CYL, CZ).transpose(1, 2, 0, 3, 4, 5)
    cell_flow = mean_cells.transpose(2, 0, 1, 3, 4, 5).reshape(3, N_GX, N_GY, CELLS)
    fields = jnp.concatenate([mean_cells, axes_cells], 2)
    column = jnp.roll(fields[:, :, :, 0], -1, axis=0)
    top_row = jnp.roll(fields[:, :, :, :, 0], -1, axis=1)
    corner = jnp.roll(fields[:, :, :, 0, 0], (-1, -1), axis=(0, 1))
    wide = jnp.concatenate([fields, column[:, :, :, None]], 3)
    top_full = jnp.concatenate([top_row, corner[:, :, :, None]], 3)
    ext_fields = jnp.concatenate([wide, top_full[:, :, :, :, None]], 4).reshape(devices, 6, extent)

    def collide(device):
        settled, living = particle_set(device)
        flat_ids = jnp.minimum(cell_ids(settled, living, grid_shift), extent - 1)
        looked = ext_fields[device][:, flat_ids]
        return rotate(settled[0:3], looked[0:3], looked[3:6], living)
    new_velocity = lax.map(collide, device_ids).reshape(N_GX, N_GY, 3, PCAP).transpose(2, 0, 1, 3)
    return (new_velocity, cell_flow)
```

```python
import math

import jax
import jax.numpy as jnp
from jax import lax
from jax.experimental import pallas as pl
from jax.experimental.pallas import tpu as pltpu
from jax.sharding import PartitionSpec as P

CXL = 8
CYL = 8
CZ = 128
NAX = 16
MIG = 1024
ROWS = 64
SLOTS = 96
GRID = 10
HALF = GRID // 2
CELL_ROWS = GRID * HALF
PAD_ROWS = 56
SIDE_ROWS = 136
CORNER_ROWS = 24
PLANES = 10

COS_TURN = -0.6427876096865393
SIN_TURN = 0.766044443118978
GOLDEN_TURN = 2.399963229728653

F32 = jnp.float32
BF16 = jnp.bfloat16
MESH = pl.DeviceIdType.MESH


def axis_table():
    table = []
    for number in range(NAX):
        height = 1.0 - (2.0 * number + 1.0) / NAX
        radius = math.sqrt(1.0 - height * height)
        phase = number * GOLDEN_TURN
        table.append((radius * math.cos(phase), radius * math.sin(phase), height))
    return table


def split(value):
    high = value.astype(BF16)
    return high, (value - high.astype(F32)).astype(BF16)


def dot_nt(a, b):
    return lax.dot_general(a, b, (((1,), (1,)), ((), ())), preferred_element_type=F32)


def iota(shape, dim):
    return lax.broadcasted_iota(jnp.int32, shape, dim)


def prep_kernel(
    leaving, shift, vel, pos, axis, side, corner, grid, ids, row_s, col_s, a_s, b_s, sums, run_s, prep_s
):
    shifts = [shift[k].astype(F32) * 0.25 for k in range(3)]
    low_x = (shift[0] == 1).astype(jnp.int32)
    low_y = (shift[1] == 1).astype(jnp.int32)
    cell_x = jnp.floor(pos[0] + shifts[0]) + low_x.astype(F32)
    cell_y = jnp.floor(pos[1] + shifts[1]) + low_y.astype(F32)
    cell_z = jnp.floor(pos[2] + shifts[2])
    cell_z = jnp.where(cell_z >= float(CZ), cell_z - float(CZ), cell_z)
    half = jnp.floor(cell_y * 0.5)
    row = cell_x * float(HALF) + half
    col = (cell_y - 2.0 * half) * float(CZ) + cell_z
    row_s[...] = row
    col_s[...] = col
    ids[...] = row * 256.0 + col

    row_of = iota((64, 128), 0).astype(F32).astype(BF16)
    col_of = iota((256, 128), 0).astype(F32).astype(BF16)
    zero = jnp.zeros((64, 128), BF16)
    one = jnp.ones((64, 128), BF16)
    for chunk in range(8):
        for j in range(8):
            r = chunk * 8 + j
            lanes = slice(j * 128, (j + 1) * 128)
            hit = row_of == jnp.broadcast_to(row_s[r : r + 1, :], (64, 128)).astype(BF16)
            a_s[0:64, lanes] = jnp.where(hit, one, zero)
            for c in range(3):
                high, low = split(vel[c, r : r + 1, :])
                high = jnp.broadcast_to(high.astype(F32), (64, 128)).astype(BF16)
                low = jnp.broadcast_to(low.astype(F32), (64, 128)).astype(BF16)
                at = 64 + 128 * c
                a_s[at : at + 64, lanes] = jnp.where(hit, high, zero)
                a_s[at + 64 : at + 128, lanes] = jnp.where(hit, low, zero)
            hit = col_of == jnp.broadcast_to(col_s[r : r + 1, :], (256, 128)).astype(BF16)
            b_s[:, lanes] = jnp.where(hit, jnp.ones((256, 128), BF16), jnp.zeros((256, 128), BF16))
        part = dot_nt(a_s[...], b_s[...])
        if chunk == 0:
            sums[...] = part
        else:
            sums[...] += part
    for par in range(2):
        lanes = slice(par * 128, (par + 1) * 128)
        grid[par] = sums[0:PAD_ROWS, lanes]
        for c in range(3):
            at = 64 + 128 * c
            grid[2 + 2 * c + par] = sums[at : at + PAD_ROWS, lanes] + sums[at + 64 : at + 64 + PAD_ROWS, lanes]
        grid[8 + par] = jnp.zeros((PAD_ROWS, 128), F32)
    for cx in range(CXL):
        base = (cx + low_x) * HALF
        grid[8 + low_y, pl.ds(base, 4), :] = axis[pl.ds(cx * 8, 4, stride=2), :].astype(F32)
        grid[9 - low_y, pl.ds(base + low_y, 4), :] = axis[pl.ds(cx * 8 + 1, 4, stride=2), :].astype(F32)
    for p in range(PLANES):
        at = slice(p * 10, p * 10 + 10)
        side[0, at, :] = grid[p, 0:10, :]
        side[1, at, :] = grid[p, 40:50, :]
        side[2, at, :] = grid[p, pl.ds(0, 10, stride=5), :]
        side[3, at, :] = grid[p, pl.ds(4, 10, stride=5), :]
        for k, start in enumerate((0, 4, 40, 44)):
            corner[k, p * 2 : p * 2 + 2, :] = grid[p, pl.ds(start, 2, stride=5), :]
    for d in range(4):
        side[d, 100:104, :] = jnp.zeros((4, 128), F32)

    slot = iota((8, 128), 0) * 128 + iota((8, 128), 1)
    lane = iota((8, 128), 1)
    counts = [leaving[k] for k in range(4)]
    starts = [jnp.int32(0), counts[0], counts[0] + counts[1], counts[0] + counts[1] + counts[2]]

    def run(load, d):
        if d == 0:
            return load(0)
        q = starts[d] // 128
        r = starts[d] - q * 128
        back = jnp.where(r == 0, 0, 128 - r)
        here = pltpu.roll(load(q), back, 1)
        after = pltpu.roll(load(q + 1), back, 1)
        return jnp.where(lane < 128 - r, here, after)

    moves = (40.0, -40.0, 4.0, -4.0)
    flags = []
    for d in range(4):
        live = slot < counts[d]
        values = [run(lambda q, c=c: vel[c, pl.ds(q, 8), :], d) for c in range(3)]
        run_id = run(lambda q: ids[pl.ds(q, 8), :], d)
        kept = live
        if d < 2:
            y = run(lambda q: pos[1, pl.ds(q, 8), :], d)
            down = live & (y < 0.0)
            up = live & (y >= float(CYL))
            kept = live & (y >= 0.0) & (y < float(CYL))
            flags += [down, up]
            for c in range(3):
                high = values[c].astype(BF16).astype(F32)
                run_s[d, 16 * c : 16 * c + 8, :] = high
                run_s[d, 16 * c + 8 : 16 * c + 16, :] = values[c] - high
            run_row = jnp.floor(run_id * (1.0 / 256.0))
            run_s[d, 48:56, :] = run_row
            run_s[d, 56:64, :] = run_id - run_row * 256.0
            run_s[d, 64:72, :] = jnp.ones((8, 128), F32)
            run_s[d, 72:128, :] = jnp.zeros((56, 128), F32)
        for c in range(3):
            side[d, 104 + 8 * c : 112 + 8 * c, :] = values[c]
        side[d, 128:136, :] = jnp.where(kept, run_id + moves[d] * 256.0, -1.0)

    flag = jnp.concatenate([f.astype(F32) for f in flags], 0)
    flag16 = flag.astype(BF16)
    before = (iota((128, 128), 0) < iota((128, 128), 1)).astype(F32).astype(BF16)
    inside = jnp.dot(flag16, before, preferred_element_type=F32)
    total = jnp.dot(flag16, jnp.ones((128, 128), BF16), preferred_element_type=F32)
    r0, r1 = iota((32, 32), 0), iota((32, 32), 1)
    earlier = ((r1 < r0) & (r0 // 8 == r1 // 8)).astype(F32).astype(BF16)
    offset = jnp.dot(earlier, total.astype(BF16), preferred_element_type=F32)
    rank = jnp.where(flag > 0.0, inside + offset, -1.0)
    prep_s[...] = rank
    rank_of = iota((128, 128), 0).astype(F32).astype(BF16)
    for d in range(2):
        rows = jnp.concatenate(
            [run_s[d, pl.ds(r, 16, stride=8), :] for r in range(8)], 1
        ).astype(BF16)
        for s in range(2):
            at = d * 16 + s * 8
            hits = []
            for r in range(8):
                hit = rank_of == jnp.broadcast_to(prep_s[at + r : at + r + 1, :], (128, 128)).astype(BF16)
                hits.append(jnp.where(hit, jnp.ones((128, 128), BF16), jnp.zeros((128, 128), BF16)))
            packed = dot_nt(rows, jnp.concatenate(hits, 1))
            k = d * 2 + s
            for c in range(3):
                corner[k, 20 + c : 21 + c, :] = packed[2 * c : 2 * c + 1] + packed[2 * c + 1 : 2 * c + 2]
            moved = packed[6:7] * 256.0 + packed[7:8] + (moves[d] + moves[2 + s]) * 256.0
            corner[k, 23:24, :] = jnp.where(packed[8:9] > 0.5, moved, -1.0)


def exchange_kernel(side, corner, got_side, got_corner, send_side, recv_side, send_corner, recv_corner):
    x, y = lax.axis_index("gx"), lax.axis_index("gy")
    nx, ny = lax.axis_size("gx"), lax.axis_size("gy")
    left, right = lax.rem(x + nx - 1, nx), lax.rem(x + 1, nx)
    down, up = lax.rem(y + ny - 1, ny), lax.rem(y + 1, ny)
    sides = [(left, y), (right, y), (x, down), (x, up)]
    corners = [(left, down), (left, up), (right, down), (right, up)]
    barrier = pltpu.get_barrier_semaphore()
    for target in sides + corners:
        pl.semaphore_signal(barrier, inc=1, device_id=target, device_id_type=MESH)
    pl.semaphore_wait(barrier, 8)
    copies = []
    for k in range(4):
        copies.append(
            pltpu.make_async_remote_copy(
                src_ref=side.at[k],
                dst_ref=got_side.at[k],
                send_sem=send_side.at[k],
                recv_sem=recv_side.at[k],
                device_id=sides[k],
                device_id_type=MESH,
            )
        )
        copies.append(
            pltpu.make_async_remote_copy(
                src_ref=corner.at[k],
                dst_ref=got_corner.at[k],
                send_sem=send_corner.at[k],
                recv_sem=recv_corner.at[k],
                device_id=corners[k],
                device_id_type=MESH,
            )
        )
    for copy in copies:
        copy.start()
    for copy in copies:
        copy.wait()


def collide_kernel(
    leaving, shift, vel, ids, grid, side, corner, out, flow, total, table, slot_v, slot_id, found
):
    low_x = (shift[0] == 1).astype(jnp.int32)
    low_y = (shift[1] == 1).astype(jnp.int32)
    total[...] = grid[...]
    for p in range(PLANES):
        at = slice(p * 10, p * 10 + 10)
        total[p, 0:10, :] += side[1, at, :]
        total[p, 40:50, :] += side[0, at, :]
        total[p, pl.ds(0, 10, stride=5), :] += side[3, at, :]
        total[p, pl.ds(4, 10, stride=5), :] += side[2, at, :]
        for k, start in ((3, 0), (2, 4), (1, 40), (0, 44)):
            total[p, pl.ds(start, 2, stride=5), :] += corner[k, p * 2 : p * 2 + 2, :]
    table[...] = jnp.zeros((256, 512), BF16)
    for par in range(2):
        most = jnp.maximum(total[par], 1.0)
        lanes = slice(par * 128, par * 128 + 128)
        lanes_low = slice(256 + par * 128, 384 + par * 128)
        pad = jnp.zeros((64 - PAD_ROWS, 128), F32)
        for c in range(3):
            mean = total[2 + 2 * c + par] / most
            total[2 + 2 * c + par] = mean
            high, low = split(jnp.concatenate([mean, pad], 0))
            table[64 * c : 64 * c + 64, lanes] = high
            table[64 * c : 64 * c + 64, lanes_low] = low
        table[192:256, lanes] = jnp.concatenate([total[8 + par], pad], 0).astype(BF16)
    for cx in range(CXL):
        base = (cx + low_x) * HALF
        for c in range(3):
            flow[c, pl.ds(cx * 8, 4, stride=2), :] = total[2 + 2 * c + low_y, pl.ds(base, 4), :]
            flow[c, pl.ds(cx * 8 + 1, 4, stride=2), :] = total[
                3 + 2 * c - low_y, pl.ds(base + low_y, 4), :
            ]

    slot = iota((8, 128), 0) * 128 + iota((8, 128), 1)
    for c in range(3):
        slot_v[c, 0:ROWS, :] = vel[c]
        slot_v[c, 64:72, :] = side[1, 104 + 8 * c : 112 + 8 * c, :]
        slot_v[c, 72:80, :] = side[0, 104 + 8 * c : 112 + 8 * c, :]
    gone = leaving[0] + leaving[1] + leaving[2] + leaving[3]
    place = iota((ROWS, 128), 0) * 128 + iota((ROWS, 128), 1)
    slot_id[0:ROWS, :] = jnp.where(place >= gone, ids[...], -1.0)
    slot_id[64:72, :] = side[1, 128:136, :]
    slot_id[72:80, :] = side[0, 128:136, :]
    for at, d, first, second in ((80, 3, 3, 1), (88, 2, 2, 0)):
        run_id = side[d, 128:136, :]
        n0 = jnp.sum((run_id >= 0.0).astype(jnp.int32))
        n1 = jnp.sum((corner[first, 23:24, :] >= 0.0).astype(jnp.int32))
        in_first = (slot >= n0) & (slot < n0 + n1)
        in_second = slot >= n0 + n1
        turn = lax.rem(n0, 128)
        turn2 = lax.rem(n0 + n1, 128)
        in_second = in_second & (slot < n0 + n1 + 128)
        for c in range(4):
            row = 20 + c
            one = pltpu.roll(jnp.broadcast_to(corner[first, row : row + 1, :], (8, 128)), turn, 1)
            two = pltpu.roll(jnp.broadcast_to(corner[second, row : row + 1, :], (8, 128)), turn2, 1)
            base = side[d, 104 + 8 * c : 112 + 8 * c, :]
            merged = jnp.where(in_first, one, jnp.where(in_second, two, base))
            if c < 3:
                slot_v[c, at : at + 8, :] = merged
            else:
                slot_id[at : at + 8, :] = merged

    col_of = iota((256, 128), 0).astype(F32).astype(BF16)
    row_of = iota((PAD_ROWS, 128), 0).astype(F32)
    out[:, 0:8, :] = jnp.zeros((3, 8, 128), F32)

    def group(b, carry):
        at = pl.multiple_of(8 + b * 8, 8)
        block = slot_id[pl.ds(at, 8), :]
        rows = jnp.floor(block * (1.0 / 256.0))
        cols = block - rows * 256.0
        looked = [[], [], [], []]
        for j in range(0, 8, 2):
            hits = []
            for i in (j, j + 1):
                hit = col_of == jnp.broadcast_to(cols[i : i + 1, :], (256, 128)).astype(BF16)
                hits.append(jnp.where(hit, jnp.ones((256, 128), BF16), jnp.zeros((256, 128), BF16)))
            hits = jnp.concatenate(hits, 1)
            both = jnp.dot(
                table[...], jnp.concatenate([hits, hits], 0), preferred_element_type=F32
            )
            for i in (0, 1):
                hit = row_of == jnp.broadcast_to(rows[j + i : j + i + 1, :], (PAD_ROWS, 128))
                for c in range(4):
                    part = both[64 * c : 64 * c + PAD_ROWS, i * 128 : i * 128 + 128]
                    looked[c].append(jnp.sum(jnp.where(hit, part, 0.0), axis=0, keepdims=True))
        mean = [jnp.concatenate(looked[c], 0) for c in range(3)]
        number = jnp.concatenate(looked[3], 0).astype(jnp.int32)
        bits = [(number & (1 << k)) != 0 for k in range(4)]
        turn_axis = []
        for c in range(3):
            level = [row[c] for row in axis_table()]
            for k in range(4):
                level = [
                    jnp.where(bits[k], level[2 * m + 1], level[2 * m]) for m in range(len(level) // 2)
                ]
            turn_axis.append(level[0])
        live = block >= 0.0
        w = [slot_v[c, pl.ds(at, 8), :] - mean[c] for c in range(3)]
        a = turn_axis
        cross = [
            a[1] * w[2] - a[2] * w[1],
            a[2] * w[0] - a[0] * w[2],
            a[0] * w[1] - a[1] * w[0],
        ]
        along = (a[0] * w[0] + a[1] * w[1] + a[2] * w[2]) * (1.0 - COS_TURN)
        for c in range(3):
            turned = mean[c] + COS_TURN * w[c] + SIN_TURN * cross[c] + along * a[c]
            out[c, pl.ds(at, 8), :] = jnp.where(live, turned, 0.0)
        return carry

    lax.fori_loop(0, 11, group, 0)


def per_device(velocity, position, leaving, grid_shift, axis_index):
    vel = velocity.reshape(3, ROWS, 128)
    pos = position.reshape(3, ROWS, 128)
    axis = axis_index.reshape(64, 128)
    leaving = leaving.reshape(4)
    vmem = pl.BlockSpec(memory_space=pltpu.VMEM)
    smem = pl.BlockSpec(memory_space=pltpu.SMEM)
    anywhere = pl.BlockSpec(memory_space=pl.ANY)
    side_shape = jax.ShapeDtypeStruct((4, SIDE_ROWS, 128), F32)
    corner_shape = jax.ShapeDtypeStruct((4, CORNER_ROWS, 128), F32)
    side, corner, grid, ids = pl.pallas_call(
        prep_kernel,
        name="prep",
        out_shape=(
            side_shape,
            corner_shape,
            jax.ShapeDtypeStruct((PLANES, PAD_ROWS, 128), F32),
            jax.ShapeDtypeStruct((ROWS, 128), F32),
        ),
        in_specs=[smem, smem, vmem, vmem, vmem],
        out_specs=(vmem, vmem, vmem, vmem),
        scratch_shapes=[
            pltpu.VMEM((ROWS, 128), F32),
            pltpu.VMEM((ROWS, 128), F32),
            pltpu.VMEM((448, 1024), BF16),
            pltpu.VMEM((256, 1024), BF16),
            pltpu.VMEM((448, 256), F32),
            pltpu.VMEM((2, 128, 128), F32),
            pltpu.VMEM((32, 128), F32),
        ],
        compiler_params=pltpu.CompilerParams(vmem_limit_bytes=32 << 20),
    )(leaving, grid_shift, vel, pos, axis)
    got_side, got_corner = pl.pallas_call(
        exchange_kernel,
        name="exchange",
        out_shape=(side_shape, corner_shape),
        in_specs=[anywhere, anywhere],
        out_specs=(anywhere, anywhere),
        scratch_shapes=[pltpu.SemaphoreType.DMA((4,)) for _ in range(4)],
        compiler_params=pltpu.CompilerParams(collective_id=0, has_side_effects=True),
    )(side, corner)
    out, flow = pl.pallas_call(
        collide_kernel,
        name="collide",
        out_shape=(
            jax.ShapeDtypeStruct((3, SLOTS, 128), F32),
            jax.ShapeDtypeStruct((3, 64, 128), F32),
        ),
        in_specs=[smem, smem, vmem, vmem, vmem, vmem, vmem],
        out_specs=(vmem, vmem),
        scratch_shapes=[
            pltpu.VMEM((PLANES, PAD_ROWS, 128), F32),
            pltpu.VMEM((256, 512), BF16),
            pltpu.VMEM((3, SLOTS, 128), F32),
            pltpu.VMEM((SLOTS, 128), F32),
            pltpu.VMEM((4, SLOTS, 128), F32),
        ],
        compiler_params=pltpu.CompilerParams(vmem_limit_bytes=32 << 20),
    )(leaving, grid_shift, vel, ids, grid, got_side, got_corner)
    return out.reshape(3, 1, 1, SLOTS * 128), flow.reshape(3, 1, 1, 64 * 128)


def solution(mesh):
    return jax.shard_map(
        per_device,
        mesh=mesh,
        in_specs=(
            P(None, "gx", "gy", None),
            P(None, "gx", "gy", None),
            P("gx", "gy", None),
            P(),
            P("gx", "gy", None),
        ),
        out_specs=(P(None, "gx", "gy", None), P(None, "gx", "gy", None)),
        check_vma=False,
    )
```

```python
import math

import jax
import jax.numpy as jnp
from jax import lax
from jax.experimental import pallas as pl
from jax.experimental.pallas import tpu as pltpu
from jax.sharding import PartitionSpec as P

CXL = 8
CYL = 8
CZ = 128
NAX = 16
MIG = 1024
ROWS = 64
SLOTS = 96
GRID = 10
HALF = GRID // 2
CELL_ROWS = GRID * HALF
PAD_ROWS = 56
PLANES = 10

COS_TURN = -0.6427876096865393
SIN_TURN = 0.766044443118978
GOLDEN_TURN = 2.399963229728653

F32 = jnp.float32
BF16 = jnp.bfloat16
MESH = pl.DeviceIdType.MESH


def axis_table():
    table = []
    for number in range(NAX):
        height = 1.0 - (2.0 * number + 1.0) / NAX
        radius = math.sqrt(1.0 - height * height)
        phase = number * GOLDEN_TURN
        table.append((radius * math.cos(phase), radius * math.sin(phase), height))
    return table


def split(value):
    high = value.astype(BF16)
    return high, (value - high.astype(F32)).astype(BF16)


def dot_nt(a, b):
    return lax.dot_general(a, b, (((1,), (1,)), ((), ())), preferred_element_type=F32)


def iota(shape, dim):
    return lax.broadcasted_iota(jnp.int32, shape, dim)


def neighbours():
    x, y = lax.axis_index("gx"), lax.axis_index("gy")
    nx, ny = lax.axis_size("gx"), lax.axis_size("gy")
    left, right = lax.rem(x + nx - 1, nx), lax.rem(x + 1, nx)
    down, up = lax.rem(y + ny - 1, ny), lax.rem(y + 1, ny)
    sides = [(left, y), (right, y), (x, down), (x, up)]
    corners = [(left, down), (left, up), (right, down), (right, up)]
    return sides + corners


def strips(load, side, corner, planes):
    for p in range(planes):
        at = slice(p * 10, p * 10 + 10)
        side[0, at, :] = load(p, 0, 10, 1)
        side[1, at, :] = load(p, 40, 10, 1)
        side[2, at, :] = load(p, 0, 10, 5)
        side[3, at, :] = load(p, 4, 10, 5)
        for k, start in enumerate((0, 4, 40, 44)):
            corner[k, p * 2 : p * 2 + 2, :] = load(p, start, 2, 5)


def prep_kernel(
    leaving_in, shift_in, vel_in, pos_in, axis_in,
    grid, own_axis, ids, got_axis, got_axis_c, got_sum, got_sum_c, got_run, got_run_c,
    leaving, shift, vel, pos, axis, row_s, col_s, sums, run_s, prep_s, axis_s,
    axis_o, axis_oc, sum_o, sum_oc, run_o, run_oc, load_sem, send_sem, recv_sem,
):
    loads = [
        pltpu.make_async_copy(source, target, load_sem.at[k])
        for k, (source, target) in enumerate(
            ((pos_in, pos), (shift_in, shift), (axis_in, axis), (vel_in, vel), (leaving_in, leaving))
        )
    ]
    for load in loads:
        load.start()
    targets = neighbours()
    barrier = pltpu.get_barrier_semaphore()
    for target in targets:
        pl.semaphore_signal(barrier, inc=1, device_id=target, device_id_type=MESH)

    sent = []

    def send(kind, side, corner, got, got_c):
        for k in range(8):
            source, target = (side.at[k], got.at[k]) if k < 4 else (corner.at[k - 4], got_c.at[k - 4])
            copy = pltpu.make_async_remote_copy(
                src_ref=source,
                dst_ref=target,
                send_sem=send_sem.at[kind, k],
                recv_sem=recv_sem.at[kind, k],
                device_id=targets[k],
                device_id_type=MESH,
            )
            copy.start()
            sent.append(copy)

    axis_s[...] = jnp.zeros(axis_s.shape, F32)
    axis_o[:, 16:24, :] = jnp.zeros((4, 8, 128), F32)
    axis_oc[...] = jnp.zeros((4, 8, 128), F32)
    loads[2].wait()
    for cx in range(CXL):
        base = 5 + cx * HALF
        even = axis[pl.ds(cx * 8, 4, stride=2), :].astype(F32)
        odd = axis[pl.ds(cx * 8 + 1, 4, stride=2), :].astype(F32)
        axis_s[0, base : base + 4, :] = even
        axis_s[1, base + 1 : base + 5, :] = odd
        axis_s[2, base : base + 4, :] = odd
        axis_s[3, base : base + 4, :] = even
    loads[1].wait()
    low_x = (shift[0] == 1).astype(jnp.int32)
    low_y = (shift[1] == 1).astype(jnp.int32)
    for par in range(2):
        own_axis[par] = axis_s[2 * par + low_y, pl.ds(5 - 5 * low_x, PAD_ROWS), :]
    strips(lambda p, at, n, step: own_axis[p, pl.ds(at, n, stride=step), :], axis_o, axis_oc, 2)
    pl.semaphore_wait(barrier, 8)
    send(0, axis_o, axis_oc, got_axis, got_axis_c)

    loads[0].wait()
    shifts = [shift[k].astype(F32) * 0.25 for k in range(3)]
    cell_x = jnp.floor(pos[0] + shifts[0]) + low_x.astype(F32)
    cell_y = jnp.floor(pos[1] + shifts[1]) + low_y.astype(F32)
    cell_z = jnp.floor(pos[2] + shifts[2])
    cell_z = jnp.where(cell_z >= float(CZ), cell_z - float(CZ), cell_z)
    half = jnp.floor(cell_y * 0.5)
    row = cell_x * float(HALF) + half
    col = (cell_y - 2.0 * half) * float(CZ) + cell_z
    row_s[...] = row
    col_s[...] = col
    ids[...] = row * 256.0 + col

    loads[3].wait()
    row_of = iota((64, 128), 0).astype(F32).astype(BF16)
    col_of = iota((256, 128), 0).astype(F32).astype(BF16)
    zero = jnp.zeros((64, 128), BF16)
    one = jnp.ones((64, 128), BF16)
    for chunk in range(8):
        left_parts = [[] for _ in range(7)]
        right_parts = []
        for j in range(8):
            r = chunk * 8 + j
            hit = row_of == jnp.broadcast_to(row_s[r : r + 1, :], (64, 128)).astype(BF16)
            left_parts[0].append(jnp.where(hit, one, zero))
            for c in range(3):
                high, low = split(vel[c, r : r + 1, :])
                high = jnp.broadcast_to(high.astype(F32), (64, 128)).astype(BF16)
                low = jnp.broadcast_to(low.astype(F32), (64, 128)).astype(BF16)
                left_parts[1 + 2 * c].append(jnp.where(hit, high, zero))
                left_parts[2 + 2 * c].append(jnp.where(hit, low, zero))
            hit = col_of == jnp.broadcast_to(col_s[r : r + 1, :], (256, 128)).astype(BF16)
            right_parts.append(
                jnp.where(hit, jnp.ones((256, 128), BF16), jnp.zeros((256, 128), BF16))
            )
        part = dot_nt(
            jnp.concatenate([jnp.concatenate(p, 1) for p in left_parts], 0),
            jnp.concatenate(right_parts, 1),
        )
        if chunk == 0:
            sums[...] = part
        else:
            sums[...] += part
    for par in range(2):
        lanes = slice(par * 128, (par + 1) * 128)
        grid[par] = sums[0:PAD_ROWS, lanes]
        for c in range(3):
            at = 64 + 128 * c
            grid[2 + 2 * c + par] = sums[at : at + PAD_ROWS, lanes] + sums[at + 64 : at + 64 + PAD_ROWS, lanes]
    strips(lambda p, at, n, step: grid[p, pl.ds(at, n, stride=step), :], sum_o, sum_oc, 8)
    send(1, sum_o, sum_oc, got_sum, got_sum_c)

    loads[4].wait()
    slot = iota((8, 128), 0) * 128 + iota((8, 128), 1)
    lane = iota((8, 128), 1)
    counts = [leaving[k] for k in range(4)]
    starts = [jnp.int32(0), counts[0], counts[0] + counts[1], counts[0] + counts[1] + counts[2]]

    def run(load, d):
        if d == 0:
            return load(0)
        q = starts[d] // 128
        r = starts[d] - q * 128
        back = jnp.where(r == 0, 0, 128 - r)
        here = pltpu.roll(load(q), back, 1)
        after = pltpu.roll(load(q + 1), back, 1)
        return jnp.where(lane < 128 - r, here, after)

    moves = (40.0, -40.0, 4.0, -4.0)
    flags = []
    for d in range(4):
        live = slot < counts[d]
        values = [run(lambda q, c=c: vel[c, pl.ds(q, 8), :], d) for c in range(3)]
        run_id = run(lambda q: ids[pl.ds(q, 8), :], d)
        kept = live
        if d < 2:
            y = run(lambda q: pos[1, pl.ds(q, 8), :], d)
            down = live & (y < 0.0)
            up = live & (y >= float(CYL))
            kept = live & (y >= 0.0) & (y < float(CYL))
            flags += [down, up]
            for c in range(3):
                high = values[c].astype(BF16).astype(F32)
                run_s[d, 16 * c : 16 * c + 8, :] = high
                run_s[d, 16 * c + 8 : 16 * c + 16, :] = values[c] - high
            run_row = jnp.floor(run_id * (1.0 / 256.0))
            run_s[d, 48:56, :] = run_row
            run_s[d, 56:64, :] = run_id - run_row * 256.0
            run_s[d, 64:72, :] = jnp.ones((8, 128), F32)
            run_s[d, 72:128, :] = jnp.zeros((56, 128), F32)
        for c in range(3):
            run_o[d, 8 * c : 8 * c + 8, :] = values[c]
        run_o[d, 24:32, :] = jnp.where(kept, run_id + moves[d] * 256.0, -1.0)

    flag = jnp.concatenate([f.astype(F32) for f in flags], 0)
    flag16 = flag.astype(BF16)
    before = (iota((128, 128), 0) < iota((128, 128), 1)).astype(F32).astype(BF16)
    inside = jnp.dot(flag16, before, preferred_element_type=F32)
    total = jnp.dot(flag16, jnp.ones((128, 128), BF16), preferred_element_type=F32)
    r0, r1 = iota((32, 32), 0), iota((32, 32), 1)
    earlier = ((r1 < r0) & (r0 // 8 == r1 // 8)).astype(F32).astype(BF16)
    offset = jnp.dot(earlier, total.astype(BF16), preferred_element_type=F32)
    rank = jnp.where(flag > 0.0, inside + offset, -1.0)
    prep_s[...] = rank
    rank_of = iota((128, 128), 0).astype(F32).astype(BF16)
    for d in range(2):
        rows = jnp.concatenate(
            [run_s[d, pl.ds(r, 16, stride=8), :] for r in range(8)], 1
        ).astype(BF16)
        for s in range(2):
            at = d * 16 + s * 8
            hits = []
            for r in range(8):
                hit = rank_of == jnp.broadcast_to(prep_s[at + r : at + r + 1, :], (128, 128)).astype(BF16)
                hits.append(jnp.where(hit, jnp.ones((128, 128), BF16), jnp.zeros((128, 128), BF16)))
            packed = dot_nt(rows, jnp.concatenate(hits, 1))
            k = d * 2 + s
            for c in range(3):
                run_oc[k, c : c + 1, :] = packed[2 * c : 2 * c + 1] + packed[2 * c + 1 : 2 * c + 2]
            moved = packed[6:7] * 256.0 + packed[7:8] + (moves[d] + moves[2 + s]) * 256.0
            run_oc[k, 3:4, :] = jnp.where(packed[8:9] > 0.5, moved, -1.0)
            run_oc[k, 4:8, :] = jnp.zeros((4, 128), F32)
    send(2, run_o, run_oc, got_run, got_run_c)
    for copy in sent:
        copy.wait()


def collide_kernel(
    leaving_in, shift_in, vel_in, ids, grid, own_axis, got_axis, got_axis_c, got_sum, got_sum_c, got_run, got_run_c,
    out_hbm, flow_hbm,
    leaving, shift, slot_v, out, flow, total, slot_id, load_sem, store_sem,
):
    loads = [
        pltpu.make_async_copy(source, target, load_sem.at[k])
        for k, (source, target) in enumerate(
            ((shift_in, shift), (leaving_in, leaving), (vel_in, slot_v.at[:, 0:ROWS, :]))
        )
    ]
    for load in loads:
        load.start()
    for p in range(PLANES):
        if p < 8:
            own, side, corner, q = grid, got_sum, got_sum_c, p
        else:
            own, side, corner, q = own_axis, got_axis, got_axis_c, p - 8
        total[p] = own[q]
        at = slice(q * 10, q * 10 + 10)
        total[p, 0:10, :] += side[1, at, :]
        total[p, 40:50, :] += side[0, at, :]
        total[p, pl.ds(0, 10, stride=5), :] += side[3, at, :]
        total[p, pl.ds(4, 10, stride=5), :] += side[2, at, :]
        for k, start in ((3, 0), (2, 4), (1, 40), (0, 44)):
            total[p, pl.ds(start, 2, stride=5), :] += corner[k, q * 2 : q * 2 + 2, :]
    high_rows = [[], [], [], []]
    low_rows = [[], [], []]
    most = [jnp.maximum(total[par], 1.0) for par in range(2)]
    for c in range(3):
        means = [total[2 + 2 * c + par] / most[par] for par in range(2)]
        for par in range(2):
            total[2 + 2 * c + par] = means[par]
        mean = jnp.concatenate(means, 1)
        high = mean.astype(BF16).astype(F32)
        high_rows[c] = high
        low_rows[c] = mean - high
    high_rows[3] = jnp.concatenate([total[8], total[9]], 1)
    table = jnp.concatenate(high_rows + low_rows + [jnp.zeros((8, 256), F32)], 0).astype(BF16)

    loads[0].wait()
    low_x = (shift[0] == 1).astype(jnp.int32)
    low_y = (shift[1] == 1).astype(jnp.int32)
    for cx in range(CXL):
        base = (cx + low_x) * HALF
        for c in range(3):
            flow[c, pl.ds(cx * 8, 4, stride=2), :] = total[2 + 2 * c + low_y, pl.ds(base, 4), :]
            flow[c, pl.ds(cx * 8 + 1, 4, stride=2), :] = total[
                3 + 2 * c - low_y, pl.ds(base + low_y, 4), :
            ]
    stores = [pltpu.make_async_copy(flow, flow_hbm, store_sem.at[0])]
    stores[0].start()

    loads[1].wait()
    loads[2].wait()
    slot = iota((8, 128), 0) * 128 + iota((8, 128), 1)
    for c in range(3):
        slot_v[c, 64:72, :] = got_run[1, 8 * c : 8 * c + 8, :]
        slot_v[c, 72:80, :] = got_run[0, 8 * c : 8 * c + 8, :]
    gone = leaving[0] + leaving[1] + leaving[2] + leaving[3]
    place = iota((ROWS, 128), 0) * 128 + iota((ROWS, 128), 1)
    slot_id[0:ROWS, :] = jnp.where(place >= gone, ids[...], -1.0)
    slot_id[64:72, :] = got_run[1, 24:32, :]
    slot_id[72:80, :] = got_run[0, 24:32, :]
    for at, d, first, second in ((80, 3, 3, 1), (88, 2, 2, 0)):
        run_id = got_run[d, 24:32, :]
        n0 = jnp.sum((run_id >= 0.0).astype(jnp.int32))
        n1 = jnp.sum((got_run_c[first, 3:4, :] >= 0.0).astype(jnp.int32))
        in_first = (slot >= n0) & (slot < n0 + n1)
        in_second = (slot >= n0 + n1) & (slot < n0 + n1 + 128)
        turn = lax.rem(n0, 128)
        turn2 = lax.rem(n0 + n1, 128)
        for c in range(4):
            one = pltpu.roll(jnp.broadcast_to(got_run_c[first, c : c + 1, :], (8, 128)), turn, 1)
            two = pltpu.roll(jnp.broadcast_to(got_run_c[second, c : c + 1, :], (8, 128)), turn2, 1)
            base = got_run[d, 8 * c : 8 * c + 8, :]
            merged = jnp.where(in_first, one, jnp.where(in_second, two, base))
            if c < 3:
                slot_v[c, at : at + 8, :] = merged
            else:
                slot_id[at : at + 8, :] = merged

    col_of = iota((256, 128), 0).astype(F32).astype(BF16)
    row_of = iota((PAD_ROWS, 128), 0).astype(F32)
    out[:, 0:8, :] = jnp.zeros((3, 8, 128), F32)
    choices = axis_table()
    for b in range(11):
        at = slice(8 + b * 8, 16 + b * 8)
        block = slot_id[at, :]
        rows = jnp.floor(block * (1.0 / 256.0))
        cols = block - rows * 256.0
        looked = [[], [], [], []]
        for j in range(0, 8, 2):
            hits = []
            for i in (j, j + 1):
                hit = col_of == jnp.broadcast_to(cols[i : i + 1, :], (256, 128)).astype(BF16)
                hits.append(jnp.where(hit, jnp.ones((256, 128), BF16), jnp.zeros((256, 128), BF16)))
            both = jnp.dot(table, jnp.concatenate(hits, 1), preferred_element_type=F32)
            for i in (0, 1):
                lanes = slice(i * 128, i * 128 + 128)
                hit = row_of == jnp.broadcast_to(rows[j + i : j + i + 1, :], (PAD_ROWS, 128))
                for c in range(4):
                    part = both[PAD_ROWS * c : PAD_ROWS * (c + 1), lanes]
                    if c < 3:
                        part = part + both[PAD_ROWS * (4 + c) : PAD_ROWS * (5 + c), lanes]
                    looked[c].append(jnp.sum(jnp.where(hit, part, 0.0), axis=0, keepdims=True))
        mean = [jnp.concatenate(looked[c], 0) for c in range(3)]
        number = jnp.concatenate(looked[3], 0).astype(jnp.int32)
        bits = [(number & (1 << k)) != 0 for k in range(4)]
        a = []
        for c in range(3):
            level = [entry[c] for entry in choices]
            for k in range(4):
                level = [
                    jnp.where(bits[k], level[2 * m + 1], level[2 * m]) for m in range(len(level) // 2)
                ]
            a.append(level[0])
        live = block >= 0.0
        w = [slot_v[c, at, :] - mean[c] for c in range(3)]
        cross = [
            a[1] * w[2] - a[2] * w[1],
            a[2] * w[0] - a[0] * w[2],
            a[0] * w[1] - a[1] * w[0],
        ]
        along = (a[0] * w[0] + a[1] * w[1] + a[2] * w[2]) * (1.0 - COS_TURN)
        for c in range(3):
            turned = mean[c] + COS_TURN * w[c] + SIN_TURN * cross[c] + along * a[c]
            out[c, at, :] = jnp.where(live, turned, 0.0)
    stores.append(pltpu.make_async_copy(out, out_hbm, store_sem.at[1]))
    stores[1].start()
    for store in stores:
        store.wait()


def shape(*dims):
    return jax.ShapeDtypeStruct(dims, F32)


def per_device(velocity, position, leaving, grid_shift, axis_index):
    vel = velocity.reshape(3, ROWS, 128)
    pos = position.reshape(3, ROWS, 128)
    axis = axis_index.reshape(64, 128)
    leaving = leaving.reshape(4)
    vmem = pl.BlockSpec(memory_space=pltpu.VMEM)
    anywhere = pl.BlockSpec(memory_space=pl.ANY)
    parts = pl.pallas_call(
        prep_kernel,
        name="prep",
        out_shape=(
            shape(8, PAD_ROWS, 128),
            shape(2, PAD_ROWS, 128),
            shape(ROWS, 128),
            shape(4, 24, 128),
            shape(4, 8, 128),
            shape(4, 80, 128),
            shape(4, 16, 128),
            shape(4, 32, 128),
            shape(4, 8, 128),
        ),
        in_specs=[anywhere] * 5,
        out_specs=(vmem,) * 9,
        scratch_shapes=[
            pltpu.SMEM((4,), jnp.int32),
            pltpu.SMEM((3,), jnp.int32),
            pltpu.VMEM((3, ROWS, 128), F32),
            pltpu.VMEM((3, ROWS, 128), F32),
            pltpu.VMEM((64, 128), jnp.int32),
            pltpu.VMEM((ROWS, 128), F32),
            pltpu.VMEM((ROWS, 128), F32),
            pltpu.VMEM((448, 256), F32),
            pltpu.VMEM((2, 128, 128), F32),
            pltpu.VMEM((32, 128), F32),
            pltpu.VMEM((4, 64, 128), F32),
            pltpu.VMEM((4, 24, 128), F32),
            pltpu.VMEM((4, 8, 128), F32),
            pltpu.VMEM((4, 80, 128), F32),
            pltpu.VMEM((4, 16, 128), F32),
            pltpu.VMEM((4, 32, 128), F32),
            pltpu.VMEM((4, 8, 128), F32),
            pltpu.SemaphoreType.DMA((5,)),
            pltpu.SemaphoreType.DMA((3, 8)),
            pltpu.SemaphoreType.DMA((3, 8)),
        ],
        compiler_params=pltpu.CompilerParams(
            collective_id=0, has_side_effects=True, vmem_limit_bytes=32 << 20
        ),
    )(leaving, grid_shift, vel, pos, axis)
    grid, own_axis, ids = parts[:3]
    out, flow = pl.pallas_call(
        collide_kernel,
        name="collide",
        out_shape=(shape(3, SLOTS, 128), shape(3, 64, 128)),
        in_specs=[anywhere] * 3 + [vmem] * 9,
        out_specs=(anywhere, anywhere),
        scratch_shapes=[
            pltpu.SMEM((4,), jnp.int32),
            pltpu.SMEM((3,), jnp.int32),
            pltpu.VMEM((3, SLOTS, 128), F32),
            pltpu.VMEM((3, SLOTS, 128), F32),
            pltpu.VMEM((3, 64, 128), F32),
            pltpu.VMEM((PLANES, PAD_ROWS, 128), F32),
            pltpu.VMEM((SLOTS, 128), F32),
            pltpu.SemaphoreType.DMA((3,)),
            pltpu.SemaphoreType.DMA((2,)),
        ],
        compiler_params=pltpu.CompilerParams(vmem_limit_bytes=32 << 20),
    )(leaving, grid_shift, vel, ids, grid, own_axis, *parts[3:])
    return out.reshape(3, 1, 1, SLOTS * 128), flow.reshape(3, 1, 1, 64 * 128)


def solution(mesh):
    return jax.shard_map(
        per_device,
        mesh=mesh,
        in_specs=(
            P(None, "gx", "gy", None),
            P(None, "gx", "gy", None),
            P("gx", "gy", None),
            P(),
            P("gx", "gy", None),
        ),
        out_specs=(P(None, "gx", "gy", None), P(None, "gx", "gy", None)),
        check_vma=False,
    )
```

```python
import math

import jax
import jax.numpy as jnp
from jax import lax
from jax.experimental import pallas as pl
from jax.experimental.pallas import tpu as pltpu
from jax.sharding import PartitionSpec as P

CXL = 8
CYL = 8
CZ = 128
NAX = 16
MIG = 1024
ROWS = 64
SLOTS = 96
GRID = 10
HALF = GRID // 2
CELL_ROWS = GRID * HALF
PAD_ROWS = 56
PLANES = 10

COS_TURN = -0.6427876096865393
SIN_TURN = 0.766044443118978
GOLDEN_TURN = 2.399963229728653

F32 = jnp.float32
BF16 = jnp.bfloat16
MESH = pl.DeviceIdType.MESH


def axis_table():
    table = []
    for number in range(NAX):
        height = 1.0 - (2.0 * number + 1.0) / NAX
        radius = math.sqrt(1.0 - height * height)
        phase = number * GOLDEN_TURN
        table.append((radius * math.cos(phase), radius * math.sin(phase), height))
    return table


def split(value):
    high = value.astype(BF16)
    return high, (value - high.astype(F32)).astype(BF16)


def dot_nt(a, b):
    return lax.dot_general(a, b, (((1,), (1,)), ((), ())), preferred_element_type=F32)


def iota(shape, dim):
    return lax.broadcasted_iota(jnp.int32, shape, dim)


def neighbours():
    x, y = lax.axis_index("gx"), lax.axis_index("gy")
    nx, ny = lax.axis_size("gx"), lax.axis_size("gy")
    left, right = lax.rem(x + nx - 1, nx), lax.rem(x + 1, nx)
    down, up = lax.rem(y + ny - 1, ny), lax.rem(y + 1, ny)
    sides = [(left, y), (right, y), (x, down), (x, up)]
    corners = [(left, down), (left, up), (right, down), (right, up)]
    return sides + corners


def strips(load, side, corner, planes):
    for p in range(planes):
        at = slice(p * 10, p * 10 + 10)
        side[0, at, :] = load(p, 0, 10, 1)
        side[1, at, :] = load(p, 40, 10, 1)
        side[2, at, :] = load(p, 0, 10, 5)
        side[3, at, :] = load(p, 4, 10, 5)
        for k, start in enumerate((0, 4, 40, 44)):
            corner[k, p * 2 : p * 2 + 2, :] = load(p, start, 2, 5)


def prep_kernel(
    leaving_in, shift_in, vel_in, pos_in, axis_in,
    grid, own_axis, ids, got_axis, got_axis_c, got_sum, got_sum_c, got_run, got_run_c,
    leaving, shift, vel, pos, axis, row_s, col_s, sums, run_s, prep_s, axis_s,
    axis_o, axis_oc, sum_o, sum_oc, run_o, run_oc, load_sem, send_sem, recv_sem,
):
    loads = [
        pltpu.make_async_copy(source, target, load_sem.at[k])
        for k, (source, target) in enumerate(
            ((pos_in, pos), (shift_in, shift), (axis_in, axis), (vel_in, vel), (leaving_in, leaving))
        )
    ]
    for load in loads:
        load.start()
    targets = neighbours()
    barrier = pltpu.get_barrier_semaphore()
    for target in targets:
        pl.semaphore_signal(barrier, inc=1, device_id=target, device_id_type=MESH)

    sent = []

    def send(kind, side, corner, got, got_c):
        for k in range(8):
            source, target = (side.at[k], got.at[k]) if k < 4 else (corner.at[k - 4], got_c.at[k - 4])
            copy = pltpu.make_async_remote_copy(
                src_ref=source,
                dst_ref=target,
                send_sem=send_sem.at[kind, k],
                recv_sem=recv_sem.at[kind, k],
                device_id=targets[k],
                device_id_type=MESH,
            )
            copy.start()
            sent.append(copy)

    axis_s[...] = jnp.zeros(axis_s.shape, F32)
    axis_o[:, 16:24, :] = jnp.zeros((4, 8, 128), F32)
    axis_oc[...] = jnp.zeros((4, 8, 128), F32)
    loads[2].wait()
    for cx in range(CXL):
        base = 5 + cx * HALF
        even = axis[pl.ds(cx * 8, 4, stride=2), :].astype(F32)
        odd = axis[pl.ds(cx * 8 + 1, 4, stride=2), :].astype(F32)
        axis_s[0, base : base + 4, :] = even
        axis_s[1, base + 1 : base + 5, :] = odd
        axis_s[2, base : base + 4, :] = odd
        axis_s[3, base : base + 4, :] = even
    loads[1].wait()
    low_x = (shift[0] == 1).astype(jnp.int32)
    low_y = (shift[1] == 1).astype(jnp.int32)
    for par in range(2):
        own_axis[par] = axis_s[2 * par + low_y, pl.ds(5 - 5 * low_x, PAD_ROWS), :]
    strips(lambda p, at, n, step: own_axis[p, pl.ds(at, n, stride=step), :], axis_o, axis_oc, 2)

    loads[0].wait()
    shifts = [shift[k].astype(F32) * 0.25 for k in range(3)]
    cell_x = jnp.floor(pos[0] + shifts[0]) + low_x.astype(F32)
    cell_y = jnp.floor(pos[1] + shifts[1]) + low_y.astype(F32)
    cell_z = jnp.floor(pos[2] + shifts[2])
    cell_z = jnp.where(cell_z >= float(CZ), cell_z - float(CZ), cell_z)
    half = jnp.floor(cell_y * 0.5)
    row = cell_x * float(HALF) + half
    col = (cell_y - 2.0 * half) * float(CZ) + cell_z
    row_s[...] = row
    col_s[...] = col
    ids[...] = row * 256.0 + col

    loads[3].wait()
    row_of = iota((64, 128), 0).astype(F32).astype(BF16)
    col_of = iota((256, 128), 0).astype(F32).astype(BF16)
    zero = jnp.zeros((64, 128), BF16)
    one = jnp.ones((64, 128), BF16)
    for chunk in range(8):
        left_parts = [[] for _ in range(7)]
        right_parts = []
        for j in range(8):
            r = chunk * 8 + j
            hit = row_of == jnp.broadcast_to(row_s[r : r + 1, :], (64, 128)).astype(BF16)
            left_parts[0].append(jnp.where(hit, one, zero))
            for c in range(3):
                high, low = split(vel[c, r : r + 1, :])
                high = jnp.broadcast_to(high.astype(F32), (64, 128)).astype(BF16)
                low = jnp.broadcast_to(low.astype(F32), (64, 128)).astype(BF16)
                left_parts[1 + 2 * c].append(jnp.where(hit, high, zero))
                left_parts[2 + 2 * c].append(jnp.where(hit, low, zero))
            hit = col_of == jnp.broadcast_to(col_s[r : r + 1, :], (256, 128)).astype(BF16)
            right_parts.append(
                jnp.where(hit, jnp.ones((256, 128), BF16), jnp.zeros((256, 128), BF16))
            )
        part = dot_nt(
            jnp.concatenate([jnp.concatenate(p, 1) for p in left_parts], 0),
            jnp.concatenate(right_parts, 1),
        )
        if chunk == 0:
            sums[...] = part
        else:
            sums[...] += part
    for par in range(2):
        lanes = slice(par * 128, (par + 1) * 128)
        grid[par] = sums[0:PAD_ROWS, lanes]
        for c in range(3):
            at = 64 + 128 * c
            grid[2 + 2 * c + par] = sums[at : at + PAD_ROWS, lanes] + sums[at + 64 : at + 64 + PAD_ROWS, lanes]
    strips(lambda p, at, n, step: grid[p, pl.ds(at, n, stride=step), :], sum_o, sum_oc, 8)
    pl.semaphore_wait(barrier, 8)
    send(1, sum_o, sum_oc, got_sum, got_sum_c)
    send(0, axis_o, axis_oc, got_axis, got_axis_c)

    loads[4].wait()
    slot = iota((8, 128), 0) * 128 + iota((8, 128), 1)
    lane = iota((8, 128), 1)
    counts = [leaving[k] for k in range(4)]
    starts = [jnp.int32(0), counts[0], counts[0] + counts[1], counts[0] + counts[1] + counts[2]]

    def run(load, d):
        if d == 0:
            return load(0)
        q = starts[d] // 128
        r = starts[d] - q * 128
        back = jnp.where(r == 0, 0, 128 - r)
        here = pltpu.roll(load(q), back, 1)
        after = pltpu.roll(load(q + 1), back, 1)
        return jnp.where(lane < 128 - r, here, after)

    moves = (40.0, -40.0, 4.0, -4.0)
    flags = []
    for d in range(4):
        live = slot < counts[d]
        values = [run(lambda q, c=c: vel[c, pl.ds(q, 8), :], d) for c in range(3)]
        run_id = run(lambda q: ids[pl.ds(q, 8), :], d)
        kept = live
        if d < 2:
            y = run(lambda q: pos[1, pl.ds(q, 8), :], d)
            down = live & (y < 0.0)
            up = live & (y >= float(CYL))
            kept = live & (y >= 0.0) & (y < float(CYL))
            flags += [down, up]
            for c in range(3):
                high = values[c].astype(BF16).astype(F32)
                run_s[d, 16 * c : 16 * c + 8, :] = high
                run_s[d, 16 * c + 8 : 16 * c + 16, :] = values[c] - high
            run_row = jnp.floor(run_id * (1.0 / 256.0))
            run_s[d, 48:56, :] = run_row
            run_s[d, 56:64, :] = run_id - run_row * 256.0
            run_s[d, 64:72, :] = jnp.ones((8, 128), F32)
            run_s[d, 72:128, :] = jnp.zeros((56, 128), F32)
        for c in range(3):
            run_o[d, 8 * c : 8 * c + 8, :] = values[c]
        run_o[d, 24:32, :] = jnp.where(kept, run_id + moves[d] * 256.0, -1.0)

    flag = jnp.concatenate([f.astype(F32) for f in flags], 0)
    flag16 = flag.astype(BF16)
    before = (iota((128, 128), 0) < iota((128, 128), 1)).astype(F32).astype(BF16)
    inside = jnp.dot(flag16, before, preferred_element_type=F32)
    total = jnp.dot(flag16, jnp.ones((128, 128), BF16), preferred_element_type=F32)
    r0, r1 = iota((32, 32), 0), iota((32, 32), 1)
    earlier = ((r1 < r0) & (r0 // 8 == r1 // 8)).astype(F32).astype(BF16)
    offset = jnp.dot(earlier, total.astype(BF16), preferred_element_type=F32)
    rank = jnp.where(flag > 0.0, inside + offset, -1.0)
    prep_s[...] = rank
    rank_of = iota((128, 128), 0).astype(F32).astype(BF16)
    for d in range(2):
        rows = jnp.concatenate(
            [run_s[d, pl.ds(r, 16, stride=8), :] for r in range(8)], 1
        ).astype(BF16)
        for s in range(2):
            at = d * 16 + s * 8
            hits = []
            for r in range(8):
                hit = rank_of == jnp.broadcast_to(prep_s[at + r : at + r + 1, :], (128, 128)).astype(BF16)
                hits.append(jnp.where(hit, jnp.ones((128, 128), BF16), jnp.zeros((128, 128), BF16)))
            packed = dot_nt(rows, jnp.concatenate(hits, 1))
            k = d * 2 + s
            for c in range(3):
                run_oc[k, c : c + 1, :] = packed[2 * c : 2 * c + 1] + packed[2 * c + 1 : 2 * c + 2]
            moved = packed[6:7] * 256.0 + packed[7:8] + (moves[d] + moves[2 + s]) * 256.0
            run_oc[k, 3:4, :] = jnp.where(packed[8:9] > 0.5, moved, -1.0)
            run_oc[k, 4:8, :] = jnp.zeros((4, 128), F32)
    send(2, run_o, run_oc, got_run, got_run_c)
    for copy in sent:
        copy.wait()


def collide_kernel(
    leaving_in, shift_in, vel_in, ids, grid, own_axis, got_axis, got_axis_c, got_sum, got_sum_c, got_run, got_run_c,
    out_hbm, flow_hbm,
    leaving, shift, slot_v, out, flow, total, slot_id, load_sem, store_sem,
):
    loads = [
        pltpu.make_async_copy(source, target, load_sem.at[k])
        for k, (source, target) in enumerate(
            ((shift_in, shift), (leaving_in, leaving), (vel_in, slot_v.at[:, 0:ROWS, :]))
        )
    ]
    for load in loads:
        load.start()
    for p in range(PLANES):
        if p < 8:
            own, side, corner, q = grid, got_sum, got_sum_c, p
        else:
            own, side, corner, q = own_axis, got_axis, got_axis_c, p - 8
        total[p] = own[q]
        at = slice(q * 10, q * 10 + 10)
        total[p, 0:10, :] += side[1, at, :]
        total[p, 40:50, :] += side[0, at, :]
        total[p, pl.ds(0, 10, stride=5), :] += side[3, at, :]
        total[p, pl.ds(4, 10, stride=5), :] += side[2, at, :]
        for k, start in ((3, 0), (2, 4), (1, 40), (0, 44)):
            total[p, pl.ds(start, 2, stride=5), :] += corner[k, q * 2 : q * 2 + 2, :]
    high_rows = [[], [], [], []]
    low_rows = [[], [], []]
    most = [jnp.maximum(total[par], 1.0) for par in range(2)]
    for c in range(3):
        means = [total[2 + 2 * c + par] / most[par] for par in range(2)]
        for par in range(2):
            total[2 + 2 * c + par] = means[par]
        mean = jnp.concatenate(means, 1)
        high = mean.astype(BF16).astype(F32)
        high_rows[c] = high
        low_rows[c] = mean - high
    high_rows[3] = jnp.concatenate([total[8], total[9]], 1)
    table = jnp.concatenate(high_rows + low_rows + [jnp.zeros((8, 256), F32)], 0).astype(BF16)

    loads[0].wait()
    low_x = (shift[0] == 1).astype(jnp.int32)
    low_y = (shift[1] == 1).astype(jnp.int32)
    for cx in range(CXL):
        base = (cx + low_x) * HALF
        for c in range(3):
            flow[c, pl.ds(cx * 8, 4, stride=2), :] = total[2 + 2 * c + low_y, pl.ds(base, 4), :]
            flow[c, pl.ds(cx * 8 + 1, 4, stride=2), :] = total[
                3 + 2 * c - low_y, pl.ds(base + low_y, 4), :
            ]
    stores = [pltpu.make_async_copy(flow, flow_hbm, store_sem.at[0])]
    stores[0].start()

    loads[1].wait()
    loads[2].wait()
    slot = iota((8, 128), 0) * 128 + iota((8, 128), 1)
    for c in range(3):
        slot_v[c, 64:72, :] = got_run[1, 8 * c : 8 * c + 8, :]
        slot_v[c, 72:80, :] = got_run[0, 8 * c : 8 * c + 8, :]
    gone = leaving[0] + leaving[1] + leaving[2] + leaving[3]
    place = iota((ROWS, 128), 0) * 128 + iota((ROWS, 128), 1)
    slot_id[0:ROWS, :] = jnp.where(place >= gone, ids[...], -1.0)
    slot_id[64:72, :] = got_run[1, 24:32, :]
    slot_id[72:80, :] = got_run[0, 24:32, :]
    for at, d, first, second in ((80, 3, 3, 1), (88, 2, 2, 0)):
        run_id = got_run[d, 24:32, :]
        n0 = jnp.sum((run_id >= 0.0).astype(jnp.int32))
        n1 = jnp.sum((got_run_c[first, 3:4, :] >= 0.0).astype(jnp.int32))
        in_first = (slot >= n0) & (slot < n0 + n1)
        in_second = (slot >= n0 + n1) & (slot < n0 + n1 + 128)
        turn = lax.rem(n0, 128)
        turn2 = lax.rem(n0 + n1, 128)
        for c in range(4):
            one = pltpu.roll(jnp.broadcast_to(got_run_c[first, c : c + 1, :], (8, 128)), turn, 1)
            two = pltpu.roll(jnp.broadcast_to(got_run_c[second, c : c + 1, :], (8, 128)), turn2, 1)
            base = got_run[d, 8 * c : 8 * c + 8, :]
            merged = jnp.where(in_first, one, jnp.where(in_second, two, base))
            if c < 3:
                slot_v[c, at : at + 8, :] = merged
            else:
                slot_id[at : at + 8, :] = merged

    col_of = iota((256, 128), 0).astype(F32).astype(BF16)
    row_of = iota((PAD_ROWS, 128), 0).astype(F32)
    out[:, 0:8, :] = jnp.zeros((3, 8, 128), F32)
    choices = axis_table()
    for b in range(11):
        at = slice(8 + b * 8, 16 + b * 8)
        block = slot_id[at, :]
        rows = jnp.floor(block * (1.0 / 256.0))
        cols = block - rows * 256.0
        looked = [[], [], [], []]
        for j in range(0, 8, 2):
            hits = []
            for i in (j, j + 1):
                hit = col_of == jnp.broadcast_to(cols[i : i + 1, :], (256, 128)).astype(BF16)
                hits.append(jnp.where(hit, jnp.ones((256, 128), BF16), jnp.zeros((256, 128), BF16)))
            both = jnp.dot(table, jnp.concatenate(hits, 1), preferred_element_type=F32)
            for i in (0, 1):
                lanes = slice(i * 128, i * 128 + 128)
                hit = row_of == jnp.broadcast_to(rows[j + i : j + i + 1, :], (PAD_ROWS, 128))
                for c in range(4):
                    part = both[PAD_ROWS * c : PAD_ROWS * (c + 1), lanes]
                    if c < 3:
                        part = part + both[PAD_ROWS * (4 + c) : PAD_ROWS * (5 + c), lanes]
                    looked[c].append(jnp.sum(jnp.where(hit, part, 0.0), axis=0, keepdims=True))
        mean = [jnp.concatenate(looked[c], 0) for c in range(3)]
        number = jnp.concatenate(looked[3], 0).astype(jnp.int32)
        bits = [(number & (1 << k)) != 0 for k in range(4)]
        a = []
        for c in range(3):
            level = [entry[c] for entry in choices]
            for k in range(4):
                level = [
                    jnp.where(bits[k], level[2 * m + 1], level[2 * m]) for m in range(len(level) // 2)
                ]
            a.append(level[0])
        live = block >= 0.0
        w = [slot_v[c, at, :] - mean[c] for c in range(3)]
        cross = [
            a[1] * w[2] - a[2] * w[1],
            a[2] * w[0] - a[0] * w[2],
            a[0] * w[1] - a[1] * w[0],
        ]
        along = (a[0] * w[0] + a[1] * w[1] + a[2] * w[2]) * (1.0 - COS_TURN)
        for c in range(3):
            turned = mean[c] + COS_TURN * w[c] + SIN_TURN * cross[c] + along * a[c]
            out[c, at, :] = jnp.where(live, turned, 0.0)
    stores.append(pltpu.make_async_copy(out, out_hbm, store_sem.at[1]))
    stores[1].start()
    for store in stores:
        store.wait()


def shape(*dims):
    return jax.ShapeDtypeStruct(dims, F32)


def per_device(velocity, position, leaving, grid_shift, axis_index):
    vel = velocity.reshape(3, ROWS, 128)
    pos = position.reshape(3, ROWS, 128)
    axis = axis_index.reshape(64, 128)
    leaving = leaving.reshape(4)
    vel, pos, axis, leaving, grid_shift = [
        pltpu.with_memory_space_constraint(v, pltpu.HBM) for v in (vel, pos, axis, leaving, grid_shift)
    ]
    vmem = pl.BlockSpec(memory_space=pltpu.VMEM)
    anywhere = pl.BlockSpec(memory_space=pltpu.HBM)
    parts = pl.pallas_call(
        prep_kernel,
        name="prep",
        out_shape=(
            shape(8, PAD_ROWS, 128),
            shape(2, PAD_ROWS, 128),
            shape(ROWS, 128),
            shape(4, 24, 128),
            shape(4, 8, 128),
            shape(4, 80, 128),
            shape(4, 16, 128),
            shape(4, 32, 128),
            shape(4, 8, 128),
        ),
        in_specs=[anywhere] * 5,
        out_specs=(vmem,) * 9,
        scratch_shapes=[
            pltpu.SMEM((4,), jnp.int32),
            pltpu.SMEM((3,), jnp.int32),
            pltpu.VMEM((3, ROWS, 128), F32),
            pltpu.VMEM((3, ROWS, 128), F32),
            pltpu.VMEM((64, 128), jnp.int32),
            pltpu.VMEM((ROWS, 128), F32),
            pltpu.VMEM((ROWS, 128), F32),
            pltpu.VMEM((448, 256), F32),
            pltpu.VMEM((2, 128, 128), F32),
            pltpu.VMEM((32, 128), F32),
            pltpu.VMEM((4, 64, 128), F32),
            pltpu.VMEM((4, 24, 128), F32),
            pltpu.VMEM((4, 8, 128), F32),
            pltpu.VMEM((4, 80, 128), F32),
            pltpu.VMEM((4, 16, 128), F32),
            pltpu.VMEM((4, 32, 128), F32),
            pltpu.VMEM((4, 8, 128), F32),
            pltpu.SemaphoreType.DMA((5,)),
            pltpu.SemaphoreType.DMA((3, 8)),
            pltpu.SemaphoreType.DMA((3, 8)),
        ],
        compiler_params=pltpu.CompilerParams(
            collective_id=0, has_side_effects=True, vmem_limit_bytes=32 << 20
        ),
    )(leaving, grid_shift, vel, pos, axis)
    grid, own_axis, ids = parts[:3]
    out, flow = pl.pallas_call(
        collide_kernel,
        name="collide",
        out_shape=(shape(3, SLOTS, 128), shape(3, 64, 128)),
        in_specs=[anywhere] * 3 + [vmem] * 9,
        out_specs=(anywhere, anywhere),
        scratch_shapes=[
            pltpu.SMEM((4,), jnp.int32),
            pltpu.SMEM((3,), jnp.int32),
            pltpu.VMEM((3, SLOTS, 128), F32),
            pltpu.VMEM((3, SLOTS, 128), F32),
            pltpu.VMEM((3, 64, 128), F32),
            pltpu.VMEM((PLANES, PAD_ROWS, 128), F32),
            pltpu.VMEM((SLOTS, 128), F32),
            pltpu.SemaphoreType.DMA((3,)),
            pltpu.SemaphoreType.DMA((2,)),
        ],
        compiler_params=pltpu.CompilerParams(vmem_limit_bytes=32 << 20),
    )(leaving, grid_shift, vel, ids, grid, own_axis, *parts[3:])
    return out.reshape(3, 1, 1, SLOTS * 128), flow.reshape(3, 1, 1, 64 * 128)


def solution(mesh):
    return jax.shard_map(
        per_device,
        mesh=mesh,
        in_specs=(
            P(None, "gx", "gy", None),
            P(None, "gx", "gy", None),
            P("gx", "gy", None),
            P(),
            P("gx", "gy", None),
        ),
        out_specs=(P(None, "gx", "gy", None), P(None, "gx", "gy", None)),
        check_vma=False,
    )
```

```python
import math

import jax
import jax.numpy as jnp
from jax import lax
from jax.experimental import pallas as pl
from jax.experimental.pallas import tpu as pltpu
from jax.sharding import PartitionSpec as P

CXL = 8
CYL = 8
CZ = 128
NAX = 16
ROWS = 64
SLOTS = 96
BORDER = 32
INNER = 18
MAIN = 48

COS_TURN = -0.6427876096865393
SIN_TURN = 0.766044443118978
GOLDEN_TURN = 2.399963229728653

F32 = jnp.float32
BF16 = jnp.bfloat16
MESH = pl.DeviceIdType.MESH


def axis_table():
    table = []
    for number in range(NAX):
        height = 1.0 - (2.0 * number + 1.0) / NAX
        radius = math.sqrt(1.0 - height * height)
        phase = number * GOLDEN_TURN
        table.append((radius * math.cos(phase), radius * math.sin(phase), height))
    return table


def dot_nt(a, b):
    return lax.dot_general(a, b, (((1,), (1,)), ((), ())), preferred_element_type=F32)


def iota(shape, dim):
    return lax.broadcasted_iota(jnp.int32, shape, dim)


def iota16(shape, dim):
    return iota(shape, dim).astype(F32).astype(BF16)


def spread(row, height):
    return jnp.broadcast_to(row, (height, 128)).astype(BF16)


def one_hot(hit):
    return jnp.where(hit, jnp.ones(hit.shape, BF16), jnp.zeros(hit.shape, BF16))


def high_part(value):
    return value.astype(BF16).astype(F32)


PIECES = (
    [(0, 2, 0, 1, 0, 0), (8, 2, 0, 1, 4, 0), (16, 2, 8, 1, 4, 0), (24, 2, 8, 1, 0, 0)]
    + [(10, 6, 2, 1, 4, 0), (26, 6, 2, 1, 0, 0)]
    + [(2 + 3 * u, 3, u, 0, 1, 1) for u in range(2)]
    + [(18 + 3 * u, 3, 8 + u, 0, 1, 1) for u in range(2)]
    + [(32 + 3 * w, 3, 2 + w, 0, 1, 1) for w in range(6)]
)


def look_up(table, heights, groups, cols, local, j):
    col_of = iota16((256, 128), 0)
    row_of = iota((heights, 128), 0).astype(F32)
    hits = [one_hot(col_of == spread(cols[i : i + 1, :], 256)) for i in (j, j + 1)]
    both = jnp.dot(table, jnp.concatenate(hits, 1), preferred_element_type=F32)
    found = []
    for i in (0, 1):
        lanes = slice(i * 128, i * 128 + 128)
        hit = row_of == jnp.broadcast_to(local[j + i : j + i + 1, :], (heights, 128))
        row = []
        for c in range(4):
            part = both[heights * c : heights * (c + 1), lanes]
            if c < 3:
                part = part + both[heights * (4 + c) : heights * (5 + c), lanes]
            row.append(jnp.sum(jnp.where(hit, part, 0.0), axis=0, keepdims=True))
        found.append(row)
    return found


def look_up_block(table, heights, cols, local):
    found = []
    for j in range(0, 8, 2):
        found += look_up(table, heights, 7, cols, local, j)
    return [jnp.concatenate([row[c] for row in found], 0) for c in range(4)]


def neighbours():
    x, y = lax.axis_index("gx"), lax.axis_index("gy")
    nx, ny = lax.axis_size("gx"), lax.axis_size("gy")
    left, right = lax.rem(x + nx - 1, nx), lax.rem(x + 1, nx)
    down, up = lax.rem(y + ny - 1, ny), lax.rem(y + 1, ny)
    sides = [(left, y), (right, y), (x, down), (x, up)]
    corners = [(left, down), (left, up), (right, down), (right, up)]
    return sides + corners


def prep_kernel(
    leaving_in, shift_in, vel_in, pos_in, axis_in,
    border, own_axis, ids, inner_mean, found, vel, got_sum, got_sum_c, got_run, got_run_c,
    leaving, shift, pos, axis, row_s, col_s, sums, run_s, prep_s, axis_s, run_o, run_oc,
    load_sem, send_sem, recv_sem,
):
    loads = [
        pltpu.make_async_copy(source, target, load_sem.at[k])
        for k, (source, target) in enumerate(
            ((pos_in, pos), (shift_in, shift), (axis_in, axis), (vel_in, vel), (leaving_in, leaving))
        )
    ]
    for load in loads:
        load.start()
    targets = neighbours()
    barrier = pltpu.get_barrier_semaphore()
    for target in targets:
        pl.semaphore_signal(barrier, inc=1, device_id=target, device_id_type=MESH)
    axis_s[...] = jnp.zeros(axis_s.shape, F32)
    run_o[...] = jnp.zeros(run_o.shape, F32)
    for load in loads:
        load.wait()

    low_x = (shift[0] == 1).astype(jnp.int32)
    low_y = (shift[1] == 1).astype(jnp.int32)
    shifts = [shift[k].astype(F32) * 0.25 for k in range(3)]
    cell_x = jnp.floor(pos[0] + shifts[0]) + low_x.astype(F32)
    cell_y = jnp.floor(pos[1] + shifts[1]) + low_y.astype(F32)
    cell_z = jnp.floor(pos[2] + shifts[2])
    cell_z = jnp.where(cell_z >= float(CZ), cell_z - float(CZ), cell_z)
    half = jnp.floor(cell_y * 0.5)
    is_left = cell_x < 2.0
    is_right = cell_x > 7.0
    bottom = cell_x + jnp.where(is_left, 0.0, jnp.where(is_right, 16.0, 24.0))
    middle = 3.0 * cell_x + half + jnp.where(is_left, 1.0, jnp.where(is_right, -7.0, 25.0))
    row = jnp.where(half < 1.0, bottom, jnp.where(half > 3.0, cell_x + 8.0, middle))
    col = (cell_y - 2.0 * half) * float(CZ) + cell_z
    row_s[...] = row
    col_s[...] = col
    ids[...] = row * 256.0 + col

    row_of = iota16((MAIN, 128), 0)
    col_of = iota16((256, 128), 0)
    rest = iota((16, 128), 0)
    rest_row = (MAIN + rest % 2).astype(F32).astype(BF16)
    rest_is = [rest // 2 == g for g in range(7)]
    for chunk in range(8):
        left_parts = [[] for _ in range(8)]
        right_parts = []
        for j in range(8):
            r = chunk * 8 + j
            values = [jnp.ones((1, 128), F32)]
            for c in range(3):
                high = high_part(vel[c, r : r + 1, :])
                values += [high, vel[c, r : r + 1, :] - high]
            hit = row_of == spread(row_s[r : r + 1, :], MAIN)
            tail = jnp.broadcast_to(values[0], (16, 128))
            for g in range(7):
                wide = spread(values[g], MAIN)
                left_parts[g].append(jnp.where(hit, wide, jnp.zeros((MAIN, 128), BF16)))
                if g:
                    tail = jnp.where(rest_is[g], jnp.broadcast_to(values[g], (16, 128)), tail)
            hit = rest_row == spread(row_s[r : r + 1, :], 16)
            left_parts[7].append(jnp.where(hit, tail.astype(BF16), jnp.zeros((16, 128), BF16)))
            right_parts.append(one_hot(col_of == spread(col_s[r : r + 1, :], 256)))
        part = dot_nt(
            jnp.concatenate([jnp.concatenate(p, 1) for p in left_parts], 0),
            jnp.concatenate(right_parts, 1),
        )
        if chunk == 0:
            sums[...] = part
        else:
            sums[...] += part
    for c in range(4):
        if c == 0:
            group = sums[0:BORDER, :]
        else:
            at = (2 * c - 1) * MAIN
            group = sums[at : at + BORDER, :] + sums[at + MAIN : at + MAIN + BORDER, :]
        for par in range(2):
            lanes = slice(par * 128, par * 128 + 128)
            border[pl.ds(2 * c + par, BORDER, stride=8), :] = group[:, lanes]
    border[8 * BORDER : 8 * BORDER + 16, :] = border[0:16, :]

    for cx in range(CXL):
        at = (cx + 1) * 11 + 1
        axis_s[at : at + 8, :] = axis[cx * 8 : cx * 8 + 8, :].astype(F32)
    for par in range(2):
        for first, n, cx, cx_step, half_y, half_step in PIECES:
            start = (cx + 1 - low_x) * 11 + 2 * half_y + par + 1 - low_y
            step = 11 * cx_step + 2 * half_step
            own_axis[par, first : first + n, :] = axis_s[pl.ds(start, n, stride=step), :]
        own_axis[par, 50:56, :] = jnp.zeros((6, 128), F32)
        base = 32 + 16 * par
        for k, order in enumerate(
            (((8, 2), (2, 6), (0, 2)), ((24, 2), (18, 6), (16, 2)), ((0, 2), (26, 6), (24, 2)), ((16, 2), (10, 6), (8, 2)))
        ):
            at = base
            for first, n in order:
                run_o[k, at : at + n, :] = own_axis[par, first : first + n, :]
                at += n
        for k, first in enumerate((0, 8, 24, 16)):
            run_oc[k, 4 + 2 * par : 6 + 2 * par, :] = own_axis[par, first : first + 2, :]

    slot = iota((8, 128), 0) * 128 + iota((8, 128), 1)
    lane = iota((8, 128), 1)
    counts = [leaving[k] for k in range(4)]
    starts = [jnp.int32(0), counts[0], counts[0] + counts[1], counts[0] + counts[1] + counts[2]]

    def run(load, d):
        if d == 0:
            return load(0)
        q = starts[d] // 128
        r = starts[d] - q * 128
        back = jnp.where(r == 0, 0, 128 - r)
        here = pltpu.roll(load(q), back, 1)
        after = pltpu.roll(load(q + 1), back, 1)
        return jnp.where(lane < 128 - r, here, after)

    def moved(d, run_row):
        if d == 0:
            return run_row + jnp.where(run_row < 2.0, 24.0, jnp.where(run_row < 8.0, 16.0, 8.0))
        if d == 1:
            return run_row - jnp.where(run_row < 18.0, 8.0, jnp.where(run_row < 24.0, 16.0, 24.0))
        if d == 2:
            return run_row + jnp.where(run_row < 2.0, 8.0, jnp.where(run_row < 26.0, -8.0, -16.0))
        return run_row + jnp.where(run_row < 10.0, -8.0, jnp.where(run_row < 16.0, 16.0, 8.0))

    flags = []
    for d in range(4):
        live = slot < counts[d]
        values = [run(lambda q, c=c: vel[c, pl.ds(q, 8), :], d) for c in range(3)]
        run_row = run(lambda q: row_s[pl.ds(q, 8), :], d)
        run_col = run(lambda q: col_s[pl.ds(q, 8), :], d)
        kept = live
        if d < 2:
            y = run(lambda q: pos[1, pl.ds(q, 8), :], d)
            down = live & (y < 0.0)
            up = live & (y >= float(CYL))
            kept = live & (y >= 0.0) & (y < float(CYL))
            flags += [down, up]
            for c in range(3):
                high = high_part(values[c])
                run_s[d, 16 * c : 16 * c + 8, :] = high
                run_s[d, 16 * c + 8 : 16 * c + 16, :] = values[c] - high
            run_s[d, 48:56, :] = run_row
            run_s[d, 56:64, :] = run_col
            run_s[d, 64:72, :] = jnp.ones((8, 128), F32)
            run_s[d, 72:128, :] = jnp.zeros((56, 128), F32)
        for c in range(3):
            run_o[d, 8 * c : 8 * c + 8, :] = values[c]
        run_o[d, 24:32, :] = jnp.where(kept, moved(d, run_row) * 256.0 + run_col, -1.0)

    flag = jnp.concatenate([f.astype(F32) for f in flags], 0)
    flag16 = flag.astype(BF16)
    before = (iota((128, 128), 0) < iota((128, 128), 1)).astype(F32).astype(BF16)
    inside = jnp.dot(flag16, before, preferred_element_type=F32)
    total = jnp.dot(flag16, jnp.ones((128, 128), BF16), preferred_element_type=F32)
    r0, r1 = iota((32, 32), 0), iota((32, 32), 1)
    earlier = ((r1 < r0) & (r0 // 8 == r1 // 8)).astype(F32).astype(BF16)
    offset = jnp.dot(earlier, total.astype(BF16), preferred_element_type=F32)
    prep_s[...] = jnp.where(flag > 0.0, inside + offset, -1.0)
    rank_of = iota16((128, 128), 0)
    for d in range(2):
        rows = jnp.concatenate([run_s[d, pl.ds(r, 16, stride=8), :] for r in range(8)], 1).astype(BF16)
        for s in range(2):
            at = d * 16 + s * 8
            hits = [one_hot(rank_of == spread(prep_s[at + r : at + r + 1, :], 128)) for r in range(8)]
            packed = dot_nt(rows, jnp.concatenate(hits, 1))
            k = d * 2 + s
            for c in range(3):
                run_oc[k, c : c + 1, :] = packed[2 * c : 2 * c + 1] + packed[2 * c + 1 : 2 * c + 2]
            there = (packed[6:7] + (16.0 - 32.0 * d)) * 256.0 + packed[7:8]
            run_oc[k, 3:4, :] = jnp.where(packed[8:9] > 0.5, there, -1.0)

    pl.semaphore_wait(barrier, 8)
    copies = []
    for k in (4, 5, 6, 7, 0, 1, 2, 3):
        if k < 4:
            source = border.at[pl.ds(8 * (0, 16, 24, 8)[k], 80), :]
            target = got_sum.at[k]
        else:
            source = border.at[pl.ds(8 * (0, 8, 24, 16)[k - 4], 16), :]
            target = got_sum_c.at[k - 4]
        copies.append((0, k, source, target))
    for k in (4, 5, 6, 7, 0, 1, 2, 3):
        if k < 4:
            copies.append((1, k, run_o.at[k], got_run.at[k]))
        else:
            copies.append((1, k, run_oc.at[k - 4], got_run_c.at[k - 4]))
    sent = []
    for kind, k, source, target in copies:
        copy = pltpu.make_async_remote_copy(
            src_ref=source,
            dst_ref=target,
            send_sem=send_sem.at[kind, k],
            recv_sem=recv_sem.at[kind, k],
            device_id=targets[k],
            device_id_type=MESH,
        )
        copy.start()
        sent.append(copy)

    def inner(group):
        at = group * MAIN + BORDER
        end = 7 * MAIN + 2 * group
        return jnp.concatenate([sums[at : at + 16, :], sums[end : end + 2, :], jnp.zeros((6, 256), F32)], 0)

    most = jnp.maximum(inner(0), 1.0)
    high_rows, low_rows = [], []
    for c in range(3):
        mean = (inner(1 + 2 * c) + inner(2 + 2 * c)) / most
        inner_mean[c] = mean
        high = high_part(mean)
        high_rows.append(high)
        low_rows.append(mean - high)
    high_rows.append(jnp.concatenate([own_axis[0, BORDER:56, :], own_axis[1, BORDER:56, :]], 1))
    table = jnp.concatenate(high_rows + low_rows, 0).astype(BF16)
    for b in range(1, 8):
        at = slice(8 * b, 8 * b + 8)
        looked = look_up_block(table, 24, col_s[at, :], row_s[at, :] - float(BORDER))
        for c in range(4):
            found[c, at, :] = looked[c]
    gone = starts[3] + counts[3]
    place = iota((ROWS, 128), 0) * 128 + iota((ROWS, 128), 1)
    ids[...] = jnp.where(place >= gone, ids[...], -1.0)
    for copy in sent:
        copy.wait()


def collide_kernel(
    shift_in, border, own_axis, ids, inner_mean, found, vel, got_sum, got_sum_c, got_run, got_run_c,
    out_hbm, flow_hbm,
    shift, out, flow, total, means, load_sem, store_sem,
):
    load = pltpu.make_async_copy(shift_in, shift, load_sem)
    load.start()
    total[...] = border[0 : 8 * BORDER, :]
    for k, places in enumerate(
        (
            ((24, 0, 2), (18, 2, 6), (16, 8, 2)),
            ((8, 0, 2), (2, 2, 6), (0, 8, 2)),
            ((16, 0, 2), (10, 2, 6), (8, 8, 2)),
            ((0, 0, 2), (26, 2, 6), (24, 8, 2)),
        )
    ):
        for mine, theirs, n in places:
            total[8 * mine : 8 * (mine + n), :] += got_sum[k, 8 * theirs : 8 * (theirs + n), :]
    for k, mine in enumerate((16, 24, 8, 0)):
        total[8 * mine : 8 * mine + 16, :] += got_sum_c[k]
    numbers = []
    for par in range(2):
        number = own_axis[par, 0:BORDER, :]
        at = 32 + 16 * par
        zero = jnp.zeros((16, 128), F32)
        for k, (before, after) in enumerate(((16, 0), (0, 16), (8, 8))):
            strip = got_run[k, at : at + 16, :]
            parts = [jnp.zeros((before, 128), F32)] * (before > 0) + [strip]
            parts += [jnp.zeros((after, 128), F32)] * (after > 0)
            number = number + jnp.concatenate(parts, 0)
        strip = got_run[3, at : at + 16, :]
        number = number + jnp.concatenate([strip[8:16], zero, strip[0:8]], 0)
        pair = [got_run_c[k, 4 + 2 * par : 6 + 2 * par, :] for k in range(4)]
        gap = jnp.zeros((6, 128), F32)
        number = number + jnp.concatenate([pair[3], gap, pair[2], gap, pair[0], gap, pair[1], gap], 0)
        numbers.append(number)
    groups = [None] * 7
    most = [jnp.maximum(total[pl.ds(par, BORDER, stride=8), :], 1.0) for par in range(2)]
    border_mean = []
    for c in range(3):
        halves = [total[pl.ds(2 + 2 * c + par, BORDER, stride=8), :] / most[par] for par in range(2)]
        mean = jnp.concatenate(halves, 1)
        border_mean.append(mean)
        groups[c] = high_part(mean)
        groups[4 + c] = mean - groups[c]
    groups[3] = jnp.concatenate(numbers, 1)
    table = jnp.concatenate(groups, 0).astype(BF16)
    choices = axis_table()

    def turn(at, live, v, looked):
        mean = looked[:3]
        number = looked[3].astype(jnp.int32)
        bits = [(number & (1 << k)) != 0 for k in range(4)]
        a = []
        for c in range(3):
            level = [entry[c] for entry in choices]
            for k in range(4):
                level = [jnp.where(bits[k], level[2 * m + 1], level[2 * m]) for m in range(len(level) // 2)]
            a.append(level[0])
        w = [v[c] - mean[c] for c in range(3)]
        cross = [
            a[1] * w[2] - a[2] * w[1],
            a[2] * w[0] - a[0] * w[2],
            a[0] * w[1] - a[1] * w[0],
        ]
        along = (a[0] * w[0] + a[1] * w[1] + a[2] * w[2]) * (1.0 - COS_TURN)
        for c in range(3):
            turned = mean[c] + COS_TURN * w[c] + SIN_TURN * cross[c] + along * a[c]
            out[c, at, :] = jnp.where(live, turned, 0.0)

    out[:, 0:8, :] = jnp.zeros((3, 8, 128), F32)
    for b in range(1, 8):
        at = slice(8 * b, 8 * b + 8)
        block = ids[at, :]
        rows = jnp.floor(block * (1.0 / 256.0))
        looked = look_up_block(table, BORDER, block - rows * 256.0, rows)
        turn(at, block >= 0.0, [vel[c, at, :] for c in range(3)], [looked[c] + found[c, at, :] for c in range(4)])

    slot = iota((8, 128), 0) * 128 + iota((8, 128), 1)
    for at, k, window in ((64, 1, 0), (72, 0, 16), (80, 3, 24), (88, 2, 8)):
        v = [got_run[k, 8 * c : 8 * c + 8, :] for c in range(4)]
        if k > 1:
            first, second = ((2, 0), (3, 1))[k - 2]
            n0 = jnp.sum((v[3] >= 0.0).astype(jnp.int32))
            n1 = jnp.sum((got_run_c[first, 3:4, :] >= 0.0).astype(jnp.int32))
            in_first = (slot >= n0) & (slot < n0 + n1)
            in_second = (slot >= n0 + n1) & (slot < n0 + n1 + 128)
            by1, by2 = lax.rem(n0, 128), lax.rem(n0 + n1, 128)
            for c in range(4):
                one = pltpu.roll(jnp.broadcast_to(got_run_c[first, c : c + 1, :], (8, 128)), by1, 1)
                two = pltpu.roll(jnp.broadcast_to(got_run_c[second, c : c + 1, :], (8, 128)), by2, 1)
                v[c] = jnp.where(in_first, one, jnp.where(in_second, two, v[c]))
        rows = jnp.floor(v[3] * (1.0 / 256.0))
        cols = v[3] - rows * 256.0
        if window == 24:
            part = [jnp.concatenate([g[24:32], g[0:8]], 0) for g in groups]
            local = jnp.where(rows < 2.0, rows + 8.0, rows - 24.0)
        else:
            part = [g[window : window + 16] for g in groups]
            local = rows - float(window)
        looked = look_up_block(jnp.concatenate(part, 0).astype(BF16), 16, cols, local)
        turn(slice(at, at + 8), v[3] >= 0.0, v, looked)
    stores = [pltpu.make_async_copy(out, out_hbm, store_sem.at[0])]
    stores[0].start()

    for c in range(3):
        for par in range(2):
            lanes = slice(par * 128, par * 128 + 128)
            for first, n, cx, cx_step, half_y, half_step in PIECES:
                if first < BORDER:
                    piece = border_mean[c][first : first + n, lanes]
                else:
                    piece = inner_mean[c, first - BORDER : first - BORDER + n, lanes]
                start = cx * 10 + 2 * half_y + par
                means[c, pl.ds(start, n, stride=10 * cx_step + 2 * half_step), :] = piece
    load.wait()
    low_x = (shift[0] == 1).astype(jnp.int32)
    low_y = (shift[1] == 1).astype(jnp.int32)
    for c in range(3):
        for cx in range(CXL):
            flow[c, cx * 8 : cx * 8 + 8, :] = means[c, pl.ds((cx + low_x) * 10 + low_y, 8), :]
    stores.append(pltpu.make_async_copy(flow, flow_hbm, store_sem.at[1]))
    stores[1].start()
    for store in stores:
        store.wait()


def shape(*dims):
    return jax.ShapeDtypeStruct(dims, F32)


def per_device(velocity, position, leaving, grid_shift, axis_index):
    vel = velocity.reshape(3, ROWS, 128)
    pos = position.reshape(3, ROWS, 128)
    axis = axis_index.reshape(64, 128)
    leaving = leaving.reshape(4)
    vel, pos, axis, leaving, grid_shift = [
        pltpu.with_memory_space_constraint(v, pltpu.HBM) for v in (vel, pos, axis, leaving, grid_shift)
    ]
    vmem = pl.BlockSpec(memory_space=pltpu.VMEM)
    hbm = pl.BlockSpec(memory_space=pltpu.HBM)
    parts = pl.pallas_call(
        prep_kernel,
        name="prep",
        out_shape=(
            shape(8 * (BORDER + 2), 128),
            shape(2, 56, 128),
            shape(ROWS, 128),
            shape(3, 24, 256),
            shape(4, ROWS, 128),
            shape(3, ROWS, 128),
            shape(4, 80, 128),
            shape(4, 16, 128),
            shape(4, 64, 128),
            shape(4, 8, 128),
        ),
        in_specs=[hbm] * 5,
        out_specs=(vmem,) * 10,
        scratch_shapes=[
            pltpu.SMEM((4,), jnp.int32),
            pltpu.SMEM((3,), jnp.int32),
            pltpu.VMEM((3, ROWS, 128), F32),
            pltpu.VMEM((64, 128), jnp.int32),
            pltpu.VMEM((ROWS, 128), F32),
            pltpu.VMEM((ROWS, 128), F32),
            pltpu.VMEM((7 * MAIN + 16, 256), F32),
            pltpu.VMEM((2, 128, 128), F32),
            pltpu.VMEM((32, 128), F32),
            pltpu.VMEM((128, 128), F32),
            pltpu.VMEM((4, 64, 128), F32),
            pltpu.VMEM((4, 8, 128), F32),
            pltpu.SemaphoreType.DMA((5,)),
            pltpu.SemaphoreType.DMA((2, 8)),
            pltpu.SemaphoreType.DMA((2, 8)),
        ],
        compiler_params=pltpu.CompilerParams(
            collective_id=0, has_side_effects=True, vmem_limit_bytes=32 << 20
        ),
    )(leaving, grid_shift, vel, pos, axis)
    out, flow = pl.pallas_call(
        collide_kernel,
        name="collide",
        out_shape=(shape(3, SLOTS, 128), shape(3, 64, 128)),
        in_specs=[hbm] + [vmem] * 10,
        out_specs=(hbm, hbm),
        scratch_shapes=[
            pltpu.SMEM((3,), jnp.int32),
            pltpu.VMEM((3, SLOTS, 128), F32),
            pltpu.VMEM((3, 64, 128), F32),
            pltpu.VMEM((8 * BORDER, 128), F32),
            pltpu.VMEM((3, 104, 128), F32),
            pltpu.SemaphoreType.DMA,
            pltpu.SemaphoreType.DMA((2,)),
        ],
        compiler_params=pltpu.CompilerParams(vmem_limit_bytes=32 << 20),
    )(grid_shift, *parts)
    return out.reshape(3, 1, 1, SLOTS * 128), flow.reshape(3, 1, 1, 64 * 128)


def solution(mesh):
    return jax.shard_map(
        per_device,
        mesh=mesh,
        in_specs=(
            P(None, "gx", "gy", None),
            P(None, "gx", "gy", None),
            P("gx", "gy", None),
            P(),
            P("gx", "gy", None),
        ),
        out_specs=(P(None, "gx", "gy", None), P(None, "gx", "gy", None)),
        check_vma=False,
    )
```

```python
import math

import jax
import jax.numpy as jnp
from jax import lax
from jax.experimental import pallas as pl
from jax.experimental.pallas import tpu as pltpu
from jax.sharding import PartitionSpec as P

CXL = 8
CYL = 8
CZ = 128
NAX = 16
ROWS = 64
SLOTS = 96
BORDER = 32
INNER = 18
MAIN = 48

COS_TURN = -0.6427876096865393
SIN_TURN = 0.766044443118978
GOLDEN_TURN = 2.399963229728653

F32 = jnp.float32
BF16 = jnp.bfloat16
MESH = pl.DeviceIdType.MESH


def axis_table():
    table = []
    for number in range(NAX):
        height = 1.0 - (2.0 * number + 1.0) / NAX
        radius = math.sqrt(1.0 - height * height)
        phase = number * GOLDEN_TURN
        table.append((radius * math.cos(phase), radius * math.sin(phase), height))
    return table


def dot_nt(a, b):
    return lax.dot_general(a, b, (((1,), (1,)), ((), ())), preferred_element_type=F32)


def iota(shape, dim):
    return lax.broadcasted_iota(jnp.int32, shape, dim)


def iota16(shape, dim):
    return iota(shape, dim).astype(F32).astype(BF16)


def spread(row, height):
    return jnp.broadcast_to(row, (height, 128)).astype(BF16)


def one_hot(hit):
    return jnp.where(hit, jnp.ones(hit.shape, BF16), jnp.zeros(hit.shape, BF16))


def high_part(value):
    return value.astype(BF16).astype(F32)


PIECES = (
    [(0, 2, 0, 1, 0, 0), (8, 2, 0, 1, 4, 0), (16, 2, 8, 1, 4, 0), (24, 2, 8, 1, 0, 0)]
    + [(10, 6, 2, 1, 4, 0), (26, 6, 2, 1, 0, 0)]
    + [(2 + 3 * u, 3, u, 0, 1, 1) for u in range(2)]
    + [(18 + 3 * u, 3, 8 + u, 0, 1, 1) for u in range(2)]
    + [(32 + 3 * w, 3, 2 + w, 0, 1, 1) for w in range(6)]
)


def look_up(table, heights, groups, cols, local, j):
    col_of = iota16((256, 128), 0)
    row_of = iota((heights, 128), 0).astype(F32)
    hits = [one_hot(col_of == spread(cols[i : i + 1, :], 256)) for i in (j, j + 1)]
    both = jnp.dot(table, jnp.concatenate(hits, 1), preferred_element_type=F32)
    found = []
    for i in (0, 1):
        lanes = slice(i * 128, i * 128 + 128)
        hit = row_of == jnp.broadcast_to(local[j + i : j + i + 1, :], (heights, 128))
        row = []
        for c in range(4):
            part = both[heights * c : heights * (c + 1), lanes]
            if c < 3:
                part = part + both[heights * (4 + c) : heights * (5 + c), lanes]
            row.append(jnp.sum(jnp.where(hit, part, 0.0), axis=0, keepdims=True))
        found.append(row)
    return found


def look_up_block(table, heights, cols, local):
    found = []
    for j in range(0, 8, 2):
        found += look_up(table, heights, 7, cols, local, j)
    return [jnp.concatenate([row[c] for row in found], 0) for c in range(4)]


def neighbours():
    x, y = lax.axis_index("gx"), lax.axis_index("gy")
    nx, ny = lax.axis_size("gx"), lax.axis_size("gy")
    left, right = lax.rem(x + nx - 1, nx), lax.rem(x + 1, nx)
    down, up = lax.rem(y + ny - 1, ny), lax.rem(y + 1, ny)
    sides = [(left, y), (right, y), (x, down), (x, up)]
    corners = [(left, down), (left, up), (right, down), (right, up)]
    return sides + corners


def prep_kernel(
    leaving_in, shift_in, vel_in, pos_in, axis_in,
    border, own_axis, ids, inner_mean, found, vel, got_side, got_corner,
    leaving, shift, pos, axis, row_s, col_s, sums, run_s, prep_s, axis_s, side, corner,
    load_sem, send_sem, recv_sem,
):
    loads = [
        pltpu.make_async_copy(source, target, load_sem.at[k])
        for k, (source, target) in enumerate(
            ((pos_in, pos), (shift_in, shift), (axis_in, axis), (vel_in, vel), (leaving_in, leaving))
        )
    ]
    for load in loads:
        load.start()
    targets = neighbours()
    barrier = pltpu.get_barrier_semaphore()
    for target in targets:
        pl.semaphore_signal(barrier, inc=1, device_id=target, device_id_type=MESH)
    axis_s[...] = jnp.zeros(axis_s.shape, F32)
    side[:, 112:144, :] = jnp.zeros((4, 32, 128), F32)
    for load in loads:
        load.wait()

    low_x = (shift[0] == 1).astype(jnp.int32)
    low_y = (shift[1] == 1).astype(jnp.int32)
    shifts = [shift[k].astype(F32) * 0.25 for k in range(3)]
    cell_x = jnp.floor(pos[0] + shifts[0]) + low_x.astype(F32)
    cell_y = jnp.floor(pos[1] + shifts[1]) + low_y.astype(F32)
    cell_z = jnp.floor(pos[2] + shifts[2])
    cell_z = jnp.where(cell_z >= float(CZ), cell_z - float(CZ), cell_z)
    half = jnp.floor(cell_y * 0.5)
    is_left = cell_x < 2.0
    is_right = cell_x > 7.0
    bottom = cell_x + jnp.where(is_left, 0.0, jnp.where(is_right, 16.0, 24.0))
    middle = 3.0 * cell_x + half + jnp.where(is_left, 1.0, jnp.where(is_right, -7.0, 25.0))
    row = jnp.where(half < 1.0, bottom, jnp.where(half > 3.0, cell_x + 8.0, middle))
    col = (cell_y - 2.0 * half) * float(CZ) + cell_z
    row_s[...] = row
    col_s[...] = col
    ids[...] = row * 256.0 + col

    row_of = iota16((MAIN, 128), 0)
    col_of = iota16((256, 128), 0)
    rest = iota((16, 128), 0)
    rest_row = (MAIN + rest % 2).astype(F32).astype(BF16)
    rest_is = [rest // 2 == g for g in range(7)]
    for chunk in range(8):
        left_parts = [[] for _ in range(8)]
        right_parts = []
        for j in range(8):
            r = chunk * 8 + j
            values = [jnp.ones((1, 128), F32)]
            for c in range(3):
                high = high_part(vel[c, r : r + 1, :])
                values += [high, vel[c, r : r + 1, :] - high]
            hit = row_of == spread(row_s[r : r + 1, :], MAIN)
            tail = jnp.broadcast_to(values[0], (16, 128))
            for g in range(7):
                wide = spread(values[g], MAIN)
                left_parts[g].append(jnp.where(hit, wide, jnp.zeros((MAIN, 128), BF16)))
                if g:
                    tail = jnp.where(rest_is[g], jnp.broadcast_to(values[g], (16, 128)), tail)
            hit = rest_row == spread(row_s[r : r + 1, :], 16)
            left_parts[7].append(jnp.where(hit, tail.astype(BF16), jnp.zeros((16, 128), BF16)))
            right_parts.append(one_hot(col_of == spread(col_s[r : r + 1, :], 256)))
        part = dot_nt(
            jnp.concatenate([jnp.concatenate(p, 1) for p in left_parts], 0),
            jnp.concatenate(right_parts, 1),
        )
        if chunk == 0:
            sums[...] = part
        else:
            sums[...] += part
    for c in range(4):
        if c == 0:
            group = sums[0:BORDER, :]
        else:
            at = (2 * c - 1) * MAIN
            group = sums[at : at + BORDER, :] + sums[at + MAIN : at + MAIN + BORDER, :]
        for par in range(2):
            lanes = slice(par * 128, par * 128 + 128)
            border[pl.ds(2 * c + par, BORDER, stride=8), :] = group[:, lanes]
    for k, start in enumerate((0, 16, 24, 8)):
        if start == 24:
            side[k, 0:64, :] = border[192:256, :]
            side[k, 64:80, :] = border[0:16, :]
        else:
            side[k, 0:80, :] = border[8 * start : 8 * start + 80, :]
    for k, start in enumerate((0, 8, 24, 16)):
        corner[k, 0:16, :] = border[8 * start : 8 * start + 16, :]

    for cx in range(CXL):
        at = (cx + 1) * 11 + 1
        axis_s[at : at + 8, :] = axis[cx * 8 : cx * 8 + 8, :].astype(F32)
    for par in range(2):
        for first, n, cx, cx_step, half_y, half_step in PIECES:
            start = (cx + 1 - low_x) * 11 + 2 * half_y + par + 1 - low_y
            step = 11 * cx_step + 2 * half_step
            own_axis[par, first : first + n, :] = axis_s[pl.ds(start, n, stride=step), :]
        own_axis[par, 50:56, :] = jnp.zeros((6, 128), F32)
        base = 112 + 16 * par
        for k, order in enumerate(
            (((8, 2), (2, 6), (0, 2)), ((24, 2), (18, 6), (16, 2)), ((0, 2), (26, 6), (24, 2)), ((16, 2), (10, 6), (8, 2)))
        ):
            at = base
            for first, n in order:
                side[k, at : at + n, :] = own_axis[par, first : first + n, :]
                at += n
        for k, first in enumerate((0, 8, 24, 16)):
            corner[k, 20 + 2 * par : 22 + 2 * par, :] = own_axis[par, first : first + 2, :]

    slot = iota((8, 128), 0) * 128 + iota((8, 128), 1)
    lane = iota((8, 128), 1)
    counts = [leaving[k] for k in range(4)]
    starts = [jnp.int32(0), counts[0], counts[0] + counts[1], counts[0] + counts[1] + counts[2]]

    def run(load, d):
        if d == 0:
            return load(0)
        q = starts[d] // 128
        r = starts[d] - q * 128
        back = jnp.where(r == 0, 0, 128 - r)
        here = pltpu.roll(load(q), back, 1)
        after = pltpu.roll(load(q + 1), back, 1)
        return jnp.where(lane < 128 - r, here, after)

    def moved(d, run_row):
        if d == 0:
            return run_row + jnp.where(run_row < 2.0, 24.0, jnp.where(run_row < 8.0, 16.0, 8.0))
        if d == 1:
            return run_row - jnp.where(run_row < 18.0, 8.0, jnp.where(run_row < 24.0, 16.0, 24.0))
        if d == 2:
            return run_row + jnp.where(run_row < 2.0, 8.0, jnp.where(run_row < 26.0, -8.0, -16.0))
        return run_row + jnp.where(run_row < 10.0, -8.0, jnp.where(run_row < 16.0, 16.0, 8.0))

    flags = []
    for d in range(4):
        live = slot < counts[d]
        values = [run(lambda q, c=c: vel[c, pl.ds(q, 8), :], d) for c in range(3)]
        run_row = run(lambda q: row_s[pl.ds(q, 8), :], d)
        run_col = run(lambda q: col_s[pl.ds(q, 8), :], d)
        kept = live
        if d < 2:
            y = run(lambda q: pos[1, pl.ds(q, 8), :], d)
            down = live & (y < 0.0)
            up = live & (y >= float(CYL))
            kept = live & (y >= 0.0) & (y < float(CYL))
            flags += [down, up]
            for c in range(3):
                high = high_part(values[c])
                run_s[d, 16 * c : 16 * c + 8, :] = high
                run_s[d, 16 * c + 8 : 16 * c + 16, :] = values[c] - high
            run_s[d, 48:56, :] = run_row
            run_s[d, 56:64, :] = run_col
            run_s[d, 64:72, :] = jnp.ones((8, 128), F32)
            run_s[d, 72:128, :] = jnp.zeros((56, 128), F32)
        for c in range(3):
            side[d, 80 + 8 * c : 88 + 8 * c, :] = values[c]
        side[d, 104:112, :] = jnp.where(kept, moved(d, run_row) * 256.0 + run_col, -1.0)

    flag = jnp.concatenate([f.astype(F32) for f in flags], 0)
    flag16 = flag.astype(BF16)
    before = (iota((128, 128), 0) < iota((128, 128), 1)).astype(F32).astype(BF16)
    inside = jnp.dot(flag16, before, preferred_element_type=F32)
    total = jnp.dot(flag16, jnp.ones((128, 128), BF16), preferred_element_type=F32)
    r0, r1 = iota((32, 32), 0), iota((32, 32), 1)
    earlier = ((r1 < r0) & (r0 // 8 == r1 // 8)).astype(F32).astype(BF16)
    offset = jnp.dot(earlier, total.astype(BF16), preferred_element_type=F32)
    prep_s[...] = jnp.where(flag > 0.0, inside + offset, -1.0)
    rank_of = iota16((128, 128), 0)
    for d in range(2):
        rows = jnp.concatenate([run_s[d, pl.ds(r, 16, stride=8), :] for r in range(8)], 1).astype(BF16)
        for s in range(2):
            at = d * 16 + s * 8
            hits = [one_hot(rank_of == spread(prep_s[at + r : at + r + 1, :], 128)) for r in range(8)]
            packed = dot_nt(rows, jnp.concatenate(hits, 1))
            k = d * 2 + s
            for c in range(3):
                corner[k, 16 + c : 17 + c, :] = packed[2 * c : 2 * c + 1] + packed[2 * c + 1 : 2 * c + 2]
            there = (packed[6:7] + (16.0 - 32.0 * d)) * 256.0 + packed[7:8]
            corner[k, 19:20, :] = jnp.where(packed[8:9] > 0.5, there, -1.0)

    pl.semaphore_wait(barrier, 8)
    copies = []
    for k in (4, 5, 6, 7, 0, 1, 2, 3):
        source, target = (side.at[k], got_side.at[k]) if k < 4 else (corner.at[k - 4], got_corner.at[k - 4])
        copy = pltpu.make_async_remote_copy(
            src_ref=source,
            dst_ref=target,
            send_sem=send_sem.at[k],
            recv_sem=recv_sem.at[k],
            device_id=targets[k],
            device_id_type=MESH,
        )
        copy.start()
        copies.append(copy)

    def inner(group):
        at = group * MAIN + BORDER
        end = 7 * MAIN + 2 * group
        return jnp.concatenate([sums[at : at + 16, :], sums[end : end + 2, :], jnp.zeros((6, 256), F32)], 0)

    most = jnp.maximum(inner(0), 1.0)
    high_rows, low_rows = [], []
    for c in range(3):
        mean = (inner(1 + 2 * c) + inner(2 + 2 * c)) / most
        inner_mean[c] = mean
        high = high_part(mean)
        high_rows.append(high)
        low_rows.append(mean - high)
    high_rows.append(jnp.concatenate([own_axis[0, BORDER:56, :], own_axis[1, BORDER:56, :]], 1))
    table = jnp.concatenate(high_rows + low_rows, 0).astype(BF16)
    for b in range(1, 8):
        at = slice(8 * b, 8 * b + 8)
        looked = look_up_block(table, 24, col_s[at, :], row_s[at, :] - float(BORDER))
        for c in range(4):
            found[c, at, :] = looked[c]
    gone = starts[3] + counts[3]
    place = iota((ROWS, 128), 0) * 128 + iota((ROWS, 128), 1)
    ids[...] = jnp.where(place >= gone, ids[...], -1.0)
    for copy in copies:
        copy.wait()


def collide_kernel(
    shift_in, border, own_axis, ids, inner_mean, found, vel, got_side, got_corner,
    out_hbm, flow_hbm,
    shift, out, flow, total, means, load_sem, store_sem,
):
    load = pltpu.make_async_copy(shift_in, shift, load_sem)
    load.start()
    total[...] = border[...]
    for k, places in enumerate(
        (
            ((24, 0, 2), (18, 2, 6), (16, 8, 2)),
            ((8, 0, 2), (2, 2, 6), (0, 8, 2)),
            ((16, 0, 2), (10, 2, 6), (8, 8, 2)),
            ((0, 0, 2), (26, 2, 6), (24, 8, 2)),
        )
    ):
        for mine, theirs, n in places:
            total[8 * mine : 8 * (mine + n), :] += got_side[k, 8 * theirs : 8 * (theirs + n), :]
    for k, mine in enumerate((16, 24, 8, 0)):
        total[8 * mine : 8 * mine + 16, :] += got_corner[k, 0:16, :]
    numbers = []
    for par in range(2):
        number = own_axis[par, 0:BORDER, :]
        at = 112 + 16 * par
        zero = jnp.zeros((16, 128), F32)
        for k, (before, after) in enumerate(((16, 0), (0, 16), (8, 8))):
            strip = got_side[k, at : at + 16, :]
            parts = [jnp.zeros((before, 128), F32)] * (before > 0) + [strip]
            parts += [jnp.zeros((after, 128), F32)] * (after > 0)
            number = number + jnp.concatenate(parts, 0)
        strip = got_side[3, at : at + 16, :]
        number = number + jnp.concatenate([strip[8:16], zero, strip[0:8]], 0)
        pair = [got_corner[k, 20 + 2 * par : 22 + 2 * par, :] for k in range(4)]
        gap = jnp.zeros((6, 128), F32)
        number = number + jnp.concatenate([pair[3], gap, pair[2], gap, pair[0], gap, pair[1], gap], 0)
        numbers.append(number)
    groups = [None] * 7
    most = [jnp.maximum(total[pl.ds(par, BORDER, stride=8), :], 1.0) for par in range(2)]
    border_mean = []
    for c in range(3):
        halves = [total[pl.ds(2 + 2 * c + par, BORDER, stride=8), :] / most[par] for par in range(2)]
        mean = jnp.concatenate(halves, 1)
        border_mean.append(mean)
        groups[c] = high_part(mean)
        groups[4 + c] = mean - groups[c]
    groups[3] = jnp.concatenate(numbers, 1)
    table = jnp.concatenate(groups, 0).astype(BF16)
    choices = axis_table()

    def turn(at, live, v, looked):
        mean = looked[:3]
        number = looked[3].astype(jnp.int32)
        bits = [(number & (1 << k)) != 0 for k in range(4)]
        a = []
        for c in range(3):
            level = [entry[c] for entry in choices]
            for k in range(4):
                level = [jnp.where(bits[k], level[2 * m + 1], level[2 * m]) for m in range(len(level) // 2)]
            a.append(level[0])
        w = [v[c] - mean[c] for c in range(3)]
        cross = [
            a[1] * w[2] - a[2] * w[1],
            a[2] * w[0] - a[0] * w[2],
            a[0] * w[1] - a[1] * w[0],
        ]
        along = (a[0] * w[0] + a[1] * w[1] + a[2] * w[2]) * (1.0 - COS_TURN)
        for c in range(3):
            turned = mean[c] + COS_TURN * w[c] + SIN_TURN * cross[c] + along * a[c]
            out[c, at, :] = jnp.where(live, turned, 0.0)

    slot = iota((8, 128), 0) * 128 + iota((8, 128), 1)
    arrived = []
    for k in (1, 0, 3, 2):
        v = [got_side[k, 80 + 8 * c : 88 + 8 * c, :] for c in range(4)]
        if k > 1:
            first, second = ((2, 0), (3, 1))[k - 2]
            n0 = jnp.sum((v[3] >= 0.0).astype(jnp.int32))
            n1 = jnp.sum((got_corner[first, 19:20, :] >= 0.0).astype(jnp.int32))
            in_first = (slot >= n0) & (slot < n0 + n1)
            in_second = (slot >= n0 + n1) & (slot < n0 + n1 + 128)
            by1, by2 = lax.rem(n0, 128), lax.rem(n0 + n1, 128)
            for c in range(4):
                at = slice(16 + c, 17 + c)
                one = pltpu.roll(jnp.broadcast_to(got_corner[first, at, :], (8, 128)), by1, 1)
                two = pltpu.roll(jnp.broadcast_to(got_corner[second, at, :], (8, 128)), by2, 1)
                v[c] = jnp.where(in_first, one, jnp.where(in_second, two, v[c]))
        arrived.append(v)

    out[:, 0:8, :] = jnp.zeros((3, 8, 128), F32)
    for b in range(1, 8):
        at = slice(8 * b, 8 * b + 8)
        block = ids[at, :]
        rows = jnp.floor(block * (1.0 / 256.0))
        looked = look_up_block(table, BORDER, block - rows * 256.0, rows)
        turn(at, block >= 0.0, [vel[c, at, :] for c in range(3)], [looked[c] + found[c, at, :] for c in range(4)])
    stores = []

    def store(source, target):
        copy = pltpu.make_async_copy(source, target, store_sem.at[len(stores)])
        copy.start()
        stores.append(copy)

    for v, at, window in zip(arrived, (64, 72, 80, 88), (0, 16, 24, 8)):
        rows = jnp.floor(v[3] * (1.0 / 256.0))
        cols = v[3] - rows * 256.0
        if window == 24:
            part = [jnp.concatenate([g[24:32], g[0:8]], 0) for g in groups]
            local = jnp.where(rows < 2.0, rows + 8.0, rows - 24.0)
        else:
            part = [g[window : window + 16] for g in groups]
            local = rows - float(window)
        looked = look_up_block(jnp.concatenate(part, 0).astype(BF16), 16, cols, local)
        turn(slice(at, at + 8), v[3] >= 0.0, v, looked)
    store(out, out_hbm)

    for c in range(3):
        for par in range(2):
            lanes = slice(par * 128, par * 128 + 128)
            for first, n, cx, cx_step, half_y, half_step in PIECES:
                if first < BORDER:
                    piece = border_mean[c][first : first + n, lanes]
                else:
                    piece = inner_mean[c, first - BORDER : first - BORDER + n, lanes]
                start = cx * 10 + 2 * half_y + par
                means[c, pl.ds(start, n, stride=10 * cx_step + 2 * half_step), :] = piece
    load.wait()
    low_x = (shift[0] == 1).astype(jnp.int32)
    low_y = (shift[1] == 1).astype(jnp.int32)
    for c in range(3):
        for cx in range(CXL):
            flow[c, cx * 8 : cx * 8 + 8, :] = means[c, pl.ds((cx + low_x) * 10 + low_y, 8), :]
    store(flow, flow_hbm)
    for copy in stores:
        copy.wait()


def shape(*dims):
    return jax.ShapeDtypeStruct(dims, F32)


def per_device(velocity, position, leaving, grid_shift, axis_index):
    vel = velocity.reshape(3, ROWS, 128)
    pos = position.reshape(3, ROWS, 128)
    axis = axis_index.reshape(64, 128)
    leaving = leaving.reshape(4)
    vel, pos, axis, leaving, grid_shift = [
        pltpu.with_memory_space_constraint(v, pltpu.HBM) for v in (vel, pos, axis, leaving, grid_shift)
    ]
    vmem = pl.BlockSpec(memory_space=pltpu.VMEM)
    hbm = pl.BlockSpec(memory_space=pltpu.HBM)
    parts = pl.pallas_call(
        prep_kernel,
        name="prep",
        out_shape=(
            shape(8 * BORDER, 128),
            shape(2, 56, 128),
            shape(ROWS, 128),
            shape(3, 24, 256),
            shape(4, ROWS, 128),
            shape(3, ROWS, 128),
            shape(4, 144, 128),
            shape(4, 24, 128),
        ),
        in_specs=[hbm] * 5,
        out_specs=(vmem,) * 8,
        scratch_shapes=[
            pltpu.SMEM((4,), jnp.int32),
            pltpu.SMEM((3,), jnp.int32),
            pltpu.VMEM((3, ROWS, 128), F32),
            pltpu.VMEM((64, 128), jnp.int32),
            pltpu.VMEM((ROWS, 128), F32),
            pltpu.VMEM((ROWS, 128), F32),
            pltpu.VMEM((7 * MAIN + 16, 256), F32),
            pltpu.VMEM((2, 128, 128), F32),
            pltpu.VMEM((32, 128), F32),
            pltpu.VMEM((128, 128), F32),
            pltpu.VMEM((4, 144, 128), F32),
            pltpu.VMEM((4, 24, 128), F32),
            pltpu.SemaphoreType.DMA((5,)),
            pltpu.SemaphoreType.DMA((8,)),
            pltpu.SemaphoreType.DMA((8,)),
        ],
        compiler_params=pltpu.CompilerParams(
            collective_id=0, has_side_effects=True, vmem_limit_bytes=32 << 20
        ),
    )(leaving, grid_shift, vel, pos, axis)
    out, flow = pl.pallas_call(
        collide_kernel,
        name="collide",
        out_shape=(shape(3, SLOTS, 128), shape(3, 64, 128)),
        in_specs=[hbm] + [vmem] * 8,
        out_specs=(hbm, hbm),
        scratch_shapes=[
            pltpu.SMEM((3,), jnp.int32),
            pltpu.VMEM((3, SLOTS, 128), F32),
            pltpu.VMEM((3, 64, 128), F32),
            pltpu.VMEM((8 * BORDER, 128), F32),
            pltpu.VMEM((3, 104, 128), F32),
            pltpu.SemaphoreType.DMA,
            pltpu.SemaphoreType.DMA((3,)),
        ],
        compiler_params=pltpu.CompilerParams(vmem_limit_bytes=32 << 20),
    )(grid_shift, *parts)
    return out.reshape(3, 1, 1, SLOTS * 128), flow.reshape(3, 1, 1, 64 * 128)


def solution(mesh):
    return jax.shard_map(
        per_device,
        mesh=mesh,
        in_specs=(
            P(None, "gx", "gy", None),
            P(None, "gx", "gy", None),
            P("gx", "gy", None),
            P(),
            P("gx", "gy", None),
        ),
        out_specs=(P(None, "gx", "gy", None), P(None, "gx", "gy", None)),
        check_vma=False,
    )
```

```python
import math

import jax
import jax.numpy as jnp
from jax import lax
from jax.experimental import pallas as pl
from jax.experimental.pallas import tpu as pltpu
from jax.sharding import PartitionSpec as P

CXL = 8
CYL = 8
CZ = 128
NAX = 16
ROWS = 64
SLOTS = 96
BORDER = 32
INNER = 18
MAIN = 48

COS_TURN = -0.6427876096865393
SIN_TURN = 0.766044443118978
GOLDEN_TURN = 2.399963229728653

F32 = jnp.float32
BF16 = jnp.bfloat16
MESH = pl.DeviceIdType.MESH


def axis_table():
    table = []
    for number in range(NAX):
        height = 1.0 - (2.0 * number + 1.0) / NAX
        radius = math.sqrt(1.0 - height * height)
        phase = number * GOLDEN_TURN
        table.append((radius * math.cos(phase), radius * math.sin(phase), height))
    return table


def dot_nt(a, b):
    return lax.dot_general(a, b, (((1,), (1,)), ((), ())), preferred_element_type=F32)


def iota(shape, dim):
    return lax.broadcasted_iota(jnp.int32, shape, dim)


def iota16(shape, dim):
    return iota(shape, dim).astype(F32).astype(BF16)


def spread(row, height):
    return jnp.broadcast_to(row, (height, 128)).astype(BF16)


def one_hot(hit):
    return jnp.where(hit, jnp.ones(hit.shape, BF16), jnp.zeros(hit.shape, BF16))


def high_part(value):
    return value.astype(BF16).astype(F32)


PIECES = (
    [(0, 2, 0, 1, 0, 0), (8, 2, 0, 1, 4, 0), (16, 2, 8, 1, 4, 0), (24, 2, 8, 1, 0, 0)]
    + [(10, 6, 2, 1, 4, 0), (26, 6, 2, 1, 0, 0)]
    + [(2 + 3 * u, 3, u, 0, 1, 1) for u in range(2)]
    + [(18 + 3 * u, 3, 8 + u, 0, 1, 1) for u in range(2)]
    + [(32 + 3 * w, 3, 2 + w, 0, 1, 1) for w in range(6)]
)


def look_up(table, heights, groups, cols, local, j):
    col_of = iota16((256, 128), 0)
    row_of = iota((heights, 128), 0).astype(F32)
    hits = [one_hot(col_of == spread(cols[i : i + 1, :], 256)) for i in (j, j + 1)]
    both = jnp.dot(table, jnp.concatenate(hits, 1), preferred_element_type=F32)
    found = []
    for i in (0, 1):
        lanes = slice(i * 128, i * 128 + 128)
        hit = row_of == jnp.broadcast_to(local[j + i : j + i + 1, :], (heights, 128))
        row = []
        for c in range(4):
            part = both[heights * c : heights * (c + 1), lanes]
            if c < 3:
                part = part + both[heights * (4 + c) : heights * (5 + c), lanes]
            row.append(jnp.sum(jnp.where(hit, part, 0.0), axis=0, keepdims=True))
        found.append(row)
    return found


def look_up_block(table, heights, cols, local):
    found = []
    for j in range(0, 8, 2):
        found += look_up(table, heights, 7, cols, local, j)
    return [jnp.concatenate([row[c] for row in found], 0) for c in range(4)]


def neighbours():
    x, y = lax.axis_index("gx"), lax.axis_index("gy")
    nx, ny = lax.axis_size("gx"), lax.axis_size("gy")
    left, right = lax.rem(x + nx - 1, nx), lax.rem(x + 1, nx)
    down, up = lax.rem(y + ny - 1, ny), lax.rem(y + 1, ny)
    sides = [(left, y), (right, y), (x, down), (x, up)]
    corners = [(left, down), (left, up), (right, down), (right, up)]
    return sides + corners


def prep_kernel(
    leaving_in, shift_in, vel_in, pos_in, axis_in,
    border, own_axis, ids, inner_mean, found, vel, got_side, got_corner,
    leaving, shift, pos, axis, row_s, col_s, sums, run_s, prep_s, axis_s, side, corner,
    load_sem, send_sem, recv_sem,
):
    targets = neighbours()
    barrier = pltpu.get_barrier_semaphore()
    for target in targets:
        pl.semaphore_signal(barrier, inc=1, device_id=target, device_id_type=MESH)
    loads = [
        pltpu.make_async_copy(source, target, load_sem.at[k])
        for k, (source, target) in enumerate(
            ((pos_in, pos), (shift_in, shift), (axis_in, axis), (vel_in, vel), (leaving_in, leaving))
        )
    ]
    for load in loads:
        load.start()
    axis_s[...] = jnp.zeros(axis_s.shape, F32)
    for k in (0, 2):
        side[k, 112:144, :] = jnp.zeros((32, 128), F32)
    corner[:, 20:24, :] = jnp.zeros((4, 4, 128), F32)
    for load in loads:
        load.wait()

    low_x = (shift[0] == 1).astype(jnp.int32)
    low_y = (shift[1] == 1).astype(jnp.int32)
    shifts = [shift[k].astype(F32) * 0.25 for k in range(3)]
    cell_x = jnp.floor(pos[0] + shifts[0]) + low_x.astype(F32)
    cell_y = jnp.floor(pos[1] + shifts[1]) + low_y.astype(F32)
    cell_z = jnp.floor(pos[2] + shifts[2])
    cell_z = jnp.where(cell_z >= float(CZ), cell_z - float(CZ), cell_z)
    half = jnp.floor(cell_y * 0.5)
    is_left = cell_x < 2.0
    is_right = cell_x > 7.0
    bottom = cell_x + jnp.where(is_left, 0.0, jnp.where(is_right, 16.0, 24.0))
    middle = 3.0 * cell_x + half + jnp.where(is_left, 1.0, jnp.where(is_right, -7.0, 25.0))
    row = jnp.where(half < 1.0, bottom, jnp.where(half > 3.0, cell_x + 8.0, middle))
    col = (cell_y - 2.0 * half) * float(CZ) + cell_z
    row_s[...] = row
    col_s[...] = col
    ids[...] = row * 256.0 + col

    row_of = iota16((MAIN, 128), 0)
    col_of = iota16((256, 128), 0)
    rest = iota((16, 128), 0)
    rest_row = (MAIN + rest % 2).astype(F32).astype(BF16)
    rest_is = [rest // 2 == g for g in range(7)]
    for chunk in range(8):
        left_parts = [[] for _ in range(8)]
        right_parts = []
        for j in range(8):
            r = chunk * 8 + j
            values = [jnp.ones((1, 128), F32)]
            for c in range(3):
                high = high_part(vel[c, r : r + 1, :])
                values += [high, vel[c, r : r + 1, :] - high]
            hit = row_of == spread(row_s[r : r + 1, :], MAIN)
            tail = jnp.broadcast_to(values[0], (16, 128))
            for g in range(7):
                wide = spread(values[g], MAIN)
                left_parts[g].append(jnp.where(hit, wide, jnp.zeros((MAIN, 128), BF16)))
                if g:
                    tail = jnp.where(rest_is[g], jnp.broadcast_to(values[g], (16, 128)), tail)
            hit = rest_row == spread(row_s[r : r + 1, :], 16)
            left_parts[7].append(jnp.where(hit, tail.astype(BF16), jnp.zeros((16, 128), BF16)))
            right_parts.append(one_hot(col_of == spread(col_s[r : r + 1, :], 256)))
        part = dot_nt(
            jnp.concatenate([jnp.concatenate(p, 1) for p in left_parts], 0),
            jnp.concatenate(right_parts, 1),
        )
        if chunk == 0:
            sums[...] = part
        else:
            sums[...] += part
    for c in range(4):
        if c == 0:
            group = sums[0:BORDER, :]
        else:
            at = (2 * c - 1) * MAIN
            group = sums[at : at + BORDER, :] + sums[at + MAIN : at + MAIN + BORDER, :]
        for par in range(2):
            lanes = slice(par * 128, par * 128 + 128)
            border[pl.ds(2 * c + par, BORDER, stride=8), :] = group[:, lanes]
    for k, start in enumerate((0, 16, 24, 8)):
        if start == 24:
            side[k, 0:64, :] = border[192:256, :]
            side[k, 64:80, :] = border[0:16, :]
        else:
            side[k, 0:80, :] = border[8 * start : 8 * start + 80, :]
    for k, start in enumerate((0, 8, 24, 16)):
        corner[k, 0:16, :] = border[8 * start : 8 * start + 16, :]

    for cx in range(CXL):
        at = (cx + 1) * 11 + 1
        axis_s[at : at + 8, :] = axis[cx * 8 : cx * 8 + 8, :].astype(F32)
    for par in range(2):
        for first, n, cx, cx_step, half_y, half_step in PIECES:
            start = (cx + 1 - low_x) * 11 + 2 * half_y + par + 1 - low_y
            step = 11 * cx_step + 2 * half_step
            own_axis[par, first : first + n, :] = axis_s[pl.ds(start, n, stride=step), :]
        own_axis[par, 50:56, :] = jnp.zeros((6, 128), F32)
        base = 112 + 16 * par
        for k, order in ((0, ((8, 2), (2, 6), (0, 2))), (2, ((0, 2), (26, 6), (24, 2)))):
            at = base
            for first, n in order:
                side[k, at : at + n, :] = own_axis[par, first : first + n, :]
                at += n
        corner[0, 20 + 2 * par : 22 + 2 * par, :] = own_axis[par, 0:2, :]

    slot = iota((8, 128), 0) * 128 + iota((8, 128), 1)
    lane = iota((8, 128), 1)
    counts = [leaving[k] for k in range(4)]
    starts = [jnp.int32(0), counts[0], counts[0] + counts[1], counts[0] + counts[1] + counts[2]]

    def run(load, d):
        if d == 0:
            return load(0)
        q = starts[d] // 128
        r = starts[d] - q * 128
        back = jnp.where(r == 0, 0, 128 - r)
        here = pltpu.roll(load(q), back, 1)
        after = pltpu.roll(load(q + 1), back, 1)
        return jnp.where(lane < 128 - r, here, after)

    def moved(d, run_row):
        if d == 0:
            return run_row + jnp.where(run_row < 2.0, 24.0, jnp.where(run_row < 8.0, 16.0, 8.0))
        if d == 1:
            return run_row - jnp.where(run_row < 18.0, 8.0, jnp.where(run_row < 24.0, 16.0, 24.0))
        if d == 2:
            return run_row + jnp.where(run_row < 2.0, 8.0, jnp.where(run_row < 26.0, -8.0, -16.0))
        return run_row + jnp.where(run_row < 10.0, -8.0, jnp.where(run_row < 16.0, 16.0, 8.0))

    flags = []
    for d in range(4):
        live = slot < counts[d]
        values = [run(lambda q, c=c: vel[c, pl.ds(q, 8), :], d) for c in range(3)]
        run_row = run(lambda q: row_s[pl.ds(q, 8), :], d)
        run_col = run(lambda q: col_s[pl.ds(q, 8), :], d)
        kept = live
        if d < 2:
            y = run(lambda q: pos[1, pl.ds(q, 8), :], d)
            down = live & (y < 0.0)
            up = live & (y >= float(CYL))
            kept = live & (y >= 0.0) & (y < float(CYL))
            flags += [down, up]
            for c in range(3):
                high = high_part(values[c])
                run_s[d, 16 * c : 16 * c + 8, :] = high
                run_s[d, 16 * c + 8 : 16 * c + 16, :] = values[c] - high
            run_s[d, 48:56, :] = run_row
            run_s[d, 56:64, :] = run_col
            run_s[d, 64:72, :] = jnp.ones((8, 128), F32)
            run_s[d, 72:128, :] = jnp.zeros((56, 128), F32)
        for c in range(3):
            side[d, 80 + 8 * c : 88 + 8 * c, :] = values[c]
        side[d, 104:112, :] = jnp.where(kept, moved(d, run_row) * 256.0 + run_col, -1.0)

    flag = jnp.concatenate([f.astype(F32) for f in flags], 0)
    flag16 = flag.astype(BF16)
    before = (iota((128, 128), 0) < iota((128, 128), 1)).astype(F32).astype(BF16)
    inside = jnp.dot(flag16, before, preferred_element_type=F32)
    total = jnp.dot(flag16, jnp.ones((128, 128), BF16), preferred_element_type=F32)
    r0, r1 = iota((32, 32), 0), iota((32, 32), 1)
    earlier = ((r1 < r0) & (r0 // 8 == r1 // 8)).astype(F32).astype(BF16)
    offset = jnp.dot(earlier, total.astype(BF16), preferred_element_type=F32)
    prep_s[...] = jnp.where(flag > 0.0, inside + offset, -1.0)
    rank_of = iota16((128, 128), 0)
    for d in range(2):
        rows = jnp.concatenate([run_s[d, pl.ds(r, 16, stride=8), :] for r in range(8)], 1).astype(BF16)
        for s in range(2):
            at = d * 16 + s * 8
            hits = [one_hot(rank_of == spread(prep_s[at + r : at + r + 1, :], 128)) for r in range(8)]
            packed = dot_nt(rows, jnp.concatenate(hits, 1))
            k = d * 2 + s
            for c in range(3):
                corner[k, 16 + c : 17 + c, :] = packed[2 * c : 2 * c + 1] + packed[2 * c + 1 : 2 * c + 2]
            there = (packed[6:7] + (16.0 - 32.0 * d)) * 256.0 + packed[7:8]
            corner[k, 19:20, :] = jnp.where(packed[8:9] > 0.5, there, -1.0)

    pl.semaphore_wait(barrier, 8)
    copies = []
    for k in range(8):
        if k < 4:
            size = 144 if k in (0, 2) else 112
            source, target = side.at[k, pl.ds(0, size), :], got_side.at[k, pl.ds(0, size), :]
        else:
            source, target = corner.at[k - 4], got_corner.at[k - 4]
        copies.append(
            pltpu.make_async_remote_copy(
                src_ref=source,
                dst_ref=target,
                send_sem=send_sem.at[k],
                recv_sem=recv_sem.at[k],
                device_id=targets[k],
                device_id_type=MESH,
            )
        )
    right_first = lax.rem(lax.axis_index("gx"), 4) == 3

    @pl.when(right_first)
    def _():
        for k in (6, 7, 1, 4, 5, 0, 2, 3):
            copies[k].start()

    @pl.when(jnp.logical_not(right_first))
    def _():
        for k in (4, 5, 0, 6, 7, 1, 2, 3):
            copies[k].start()

    def inner(group):
        at = group * MAIN + BORDER
        end = 7 * MAIN + 2 * group
        return jnp.concatenate([sums[at : at + 16, :], sums[end : end + 2, :], jnp.zeros((6, 256), F32)], 0)

    most = jnp.maximum(inner(0), 1.0)
    high_rows, low_rows = [], []
    for c in range(3):
        mean = (inner(1 + 2 * c) + inner(2 + 2 * c)) / most
        inner_mean[c] = mean
        high = high_part(mean)
        high_rows.append(high)
        low_rows.append(mean - high)
    high_rows.append(jnp.concatenate([own_axis[0, BORDER:56, :], own_axis[1, BORDER:56, :]], 1))
    table = jnp.concatenate(high_rows + low_rows, 0).astype(BF16)
    for b in range(1, 8):
        at = slice(8 * b, 8 * b + 8)
        looked = look_up_block(table, 24, col_s[at, :], row_s[at, :] - float(BORDER))
        for c in range(4):
            found[c, at, :] = looked[c]
    gone = starts[3] + counts[3]
    place = iota((ROWS, 128), 0) * 128 + iota((ROWS, 128), 1)
    ids[...] = jnp.where(place >= gone, ids[...], -1.0)
    for copy in copies:
        copy.wait()


def collide_kernel(
    shift_in, border, own_axis, ids, inner_mean, found, vel, got_side, got_corner,
    out_hbm, flow_hbm,
    shift, out, flow, total, means, load_sem, store_sem,
):
    load = pltpu.make_async_copy(shift_in, shift, load_sem)
    load.start()
    total[...] = border[...]
    for k, places in enumerate(
        (
            ((24, 0, 2), (18, 2, 6), (16, 8, 2)),
            ((8, 0, 2), (2, 2, 6), (0, 8, 2)),
            ((16, 0, 2), (10, 2, 6), (8, 8, 2)),
            ((0, 0, 2), (26, 2, 6), (24, 8, 2)),
        )
    ):
        for mine, theirs, n in places:
            total[8 * mine : 8 * (mine + n), :] += got_side[k, 8 * theirs : 8 * (theirs + n), :]
    for k, mine in enumerate((16, 24, 8, 0)):
        total[8 * mine : 8 * mine + 16, :] += got_corner[k, 0:16, :]
    numbers = []
    for par in range(2):
        number = own_axis[par, 0:BORDER, :]
        at = 112 + 16 * par
        gap = jnp.zeros((16, 128), F32)
        number = number + jnp.concatenate([gap, got_side[0, at : at + 16, :]], 0)
        number = number + jnp.concatenate([gap[0:8], got_side[2, at : at + 16, :], gap[0:8]], 0)
        pair = got_corner[0, 20 + 2 * par : 22 + 2 * par, :]
        number = number + jnp.concatenate([gap, pair, gap[0:14]], 0)
        numbers.append(number)
    groups = [None] * 7
    most = [jnp.maximum(total[pl.ds(par, BORDER, stride=8), :], 1.0) for par in range(2)]
    border_mean = []
    for c in range(3):
        halves = [total[pl.ds(2 + 2 * c + par, BORDER, stride=8), :] / most[par] for par in range(2)]
        mean = jnp.concatenate(halves, 1)
        border_mean.append(mean)
        groups[c] = high_part(mean)
        groups[4 + c] = mean - groups[c]
    groups[3] = jnp.concatenate(numbers, 1)
    table = jnp.concatenate(groups, 0).astype(BF16)
    choices = axis_table()

    def turn(at, live, v, looked):
        mean = looked[:3]
        number = looked[3].astype(jnp.int32)
        bits = [(number & (1 << k)) != 0 for k in range(4)]
        a = []
        for c in range(3):
            level = [entry[c] for entry in choices]
            for k in range(4):
                level = [jnp.where(bits[k], level[2 * m + 1], level[2 * m]) for m in range(len(level) // 2)]
            a.append(level[0])
        w = [v[c] - mean[c] for c in range(3)]
        cross = [
            a[1] * w[2] - a[2] * w[1],
            a[2] * w[0] - a[0] * w[2],
            a[0] * w[1] - a[1] * w[0],
        ]
        along = (a[0] * w[0] + a[1] * w[1] + a[2] * w[2]) * (1.0 - COS_TURN)
        for c in range(3):
            turned = mean[c] + COS_TURN * w[c] + SIN_TURN * cross[c] + along * a[c]
            out[c, at, :] = jnp.where(live, turned, 0.0)

    slot = iota((8, 128), 0) * 128 + iota((8, 128), 1)
    arrived = []
    for k in (1, 0, 3, 2):
        v = [got_side[k, 80 + 8 * c : 88 + 8 * c, :] for c in range(4)]
        if k > 1:
            first, second = ((2, 0), (3, 1))[k - 2]
            n0 = jnp.sum((v[3] >= 0.0).astype(jnp.int32))
            n1 = jnp.sum((got_corner[first, 19:20, :] >= 0.0).astype(jnp.int32))
            in_first = (slot >= n0) & (slot < n0 + n1)
            in_second = (slot >= n0 + n1) & (slot < n0 + n1 + 128)
            by1, by2 = lax.rem(n0, 128), lax.rem(n0 + n1, 128)
            for c in range(4):
                at = slice(16 + c, 17 + c)
                one = pltpu.roll(jnp.broadcast_to(got_corner[first, at, :], (8, 128)), by1, 1)
                two = pltpu.roll(jnp.broadcast_to(got_corner[second, at, :], (8, 128)), by2, 1)
                v[c] = jnp.where(in_first, one, jnp.where(in_second, two, v[c]))
        arrived.append(v)

    stores = []

    def store(source, target):
        copy = pltpu.make_async_copy(source, target, store_sem.at[len(stores)])
        copy.start()
        stores.append(copy)

    for v, at, window in zip(arrived, (64, 72, 80, 88), (0, 16, 24, 8)):
        rows = jnp.floor(v[3] * (1.0 / 256.0))
        cols = v[3] - rows * 256.0
        if window == 24:
            part = [jnp.concatenate([g[24:32], g[0:8]], 0) for g in groups]
            local = jnp.where(rows < 2.0, rows + 8.0, rows - 24.0)
        else:
            part = [g[window : window + 16] for g in groups]
            local = rows - float(window)
        looked = look_up_block(jnp.concatenate(part, 0).astype(BF16), 16, cols, local)
        turn(slice(at, at + 8), v[3] >= 0.0, v, looked)

    out[:, 0:8, :] = jnp.zeros((3, 8, 128), F32)
    for b in range(1, 8):
        at = slice(8 * b, 8 * b + 8)
        block = ids[at, :]
        rows = jnp.floor(block * (1.0 / 256.0))
        looked = look_up_block(table, BORDER, block - rows * 256.0, rows)
        turn(at, block >= 0.0, [vel[c, at, :] for c in range(3)], [looked[c] + found[c, at, :] for c in range(4)])
    store(out, out_hbm)

    for c in range(3):
        for par in range(2):
            lanes = slice(par * 128, par * 128 + 128)
            for first, n, cx, cx_step, half_y, half_step in PIECES:
                if first < BORDER:
                    piece = border_mean[c][first : first + n, lanes]
                else:
                    piece = inner_mean[c, first - BORDER : first - BORDER + n, lanes]
                start = cx * 10 + 2 * half_y + par
                means[c, pl.ds(start, n, stride=10 * cx_step + 2 * half_step), :] = piece
    load.wait()
    low_x = (shift[0] == 1).astype(jnp.int32)
    low_y = (shift[1] == 1).astype(jnp.int32)
    for c in range(3):
        for cx in range(CXL):
            flow[c, cx * 8 : cx * 8 + 8, :] = means[c, pl.ds((cx + low_x) * 10 + low_y, 8), :]
    store(flow, flow_hbm)
    for copy in stores:
        copy.wait()


def shape(*dims):
    return jax.ShapeDtypeStruct(dims, F32)


def per_device(velocity, position, leaving, grid_shift, axis_index):
    vel = velocity.reshape(3, ROWS, 128)
    pos = position.reshape(3, ROWS, 128)
    axis = axis_index.reshape(64, 128)
    leaving = leaving.reshape(4)
    vel, pos, axis, leaving, grid_shift = [
        pltpu.with_memory_space_constraint(v, pltpu.HBM) for v in (vel, pos, axis, leaving, grid_shift)
    ]
    vmem = pl.BlockSpec(memory_space=pltpu.VMEM)
    hbm = pl.BlockSpec(memory_space=pltpu.HBM)
    parts = pl.pallas_call(
        prep_kernel,
        name="prep",
        out_shape=(
            shape(8 * BORDER, 128),
            shape(2, 56, 128),
            shape(ROWS, 128),
            shape(3, 24, 256),
            shape(4, ROWS, 128),
            shape(3, ROWS, 128),
            shape(4, 144, 128),
            shape(4, 24, 128),
        ),
        in_specs=[hbm] * 5,
        out_specs=(vmem,) * 8,
        scratch_shapes=[
            pltpu.SMEM((4,), jnp.int32),
            pltpu.SMEM((3,), jnp.int32),
            pltpu.VMEM((3, ROWS, 128), F32),
            pltpu.VMEM((64, 128), jnp.int32),
            pltpu.VMEM((ROWS, 128), F32),
            pltpu.VMEM((ROWS, 128), F32),
            pltpu.VMEM((7 * MAIN + 16, 256), F32),
            pltpu.VMEM((2, 128, 128), F32),
            pltpu.VMEM((32, 128), F32),
            pltpu.VMEM((128, 128), F32),
            pltpu.VMEM((4, 144, 128), F32),
            pltpu.VMEM((4, 24, 128), F32),
            pltpu.SemaphoreType.DMA((5,)),
            pltpu.SemaphoreType.DMA((8,)),
            pltpu.SemaphoreType.DMA((8,)),
        ],
        compiler_params=pltpu.CompilerParams(
            collective_id=0, has_side_effects=True, vmem_limit_bytes=32 << 20
        ),
    )(leaving, grid_shift, vel, pos, axis)
    out, flow = pl.pallas_call(
        collide_kernel,
        name="collide",
        out_shape=(shape(3, SLOTS, 128), shape(3, 64, 128)),
        in_specs=[hbm] + [vmem] * 8,
        out_specs=(hbm, hbm),
        scratch_shapes=[
            pltpu.SMEM((3,), jnp.int32),
            pltpu.VMEM((3, SLOTS, 128), F32),
            pltpu.VMEM((3, 64, 128), F32),
            pltpu.VMEM((8 * BORDER, 128), F32),
            pltpu.VMEM((3, 104, 128), F32),
            pltpu.SemaphoreType.DMA,
            pltpu.SemaphoreType.DMA((3,)),
        ],
        compiler_params=pltpu.CompilerParams(vmem_limit_bytes=32 << 20),
    )(grid_shift, *parts)
    return out.reshape(3, 1, 1, SLOTS * 128), flow.reshape(3, 1, 1, 64 * 128)


def solution(mesh):
    return jax.shard_map(
        per_device,
        mesh=mesh,
        in_specs=(
            P(None, "gx", "gy", None),
            P(None, "gx", "gy", None),
            P("gx", "gy", None),
            P(),
            P("gx", "gy", None),
        ),
        out_specs=(P(None, "gx", "gy", None), P(None, "gx", "gy", None)),
        check_vma=False,
    )
```

```python
import math

import jax
import jax.numpy as jnp
from jax import lax
from jax.experimental import pallas as pl
from jax.experimental.pallas import tpu as pltpu
from jax.sharding import PartitionSpec as P

CXL = 8
CYL = 8
CZ = 128
NAX = 16
ROWS = 64
SLOTS = 96
BORDER = 32
INNER = 18
MAIN = 48

COS_TURN = -0.6427876096865393
SIN_TURN = 0.766044443118978
GOLDEN_TURN = 2.399963229728653

F32 = jnp.float32
BF16 = jnp.bfloat16
MESH = pl.DeviceIdType.MESH


def axis_table():
    table = []
    for number in range(NAX):
        height = 1.0 - (2.0 * number + 1.0) / NAX
        radius = math.sqrt(1.0 - height * height)
        phase = number * GOLDEN_TURN
        table.append((radius * math.cos(phase), radius * math.sin(phase), height))
    return table


def dot_nt(a, b):
    return lax.dot_general(a, b, (((1,), (1,)), ((), ())), preferred_element_type=F32)


def iota(shape, dim):
    return lax.broadcasted_iota(jnp.int32, shape, dim)


def iota16(shape, dim):
    return iota(shape, dim).astype(F32).astype(BF16)


def spread(row, height):
    return jnp.broadcast_to(row, (height, 128)).astype(BF16)


def one_hot(hit):
    return jnp.where(hit, jnp.ones(hit.shape, BF16), jnp.zeros(hit.shape, BF16))


def high_part(value):
    return value.astype(BF16).astype(F32)


PIECES = (
    [(0, 2, 0, 1, 0, 0), (8, 2, 0, 1, 4, 0), (16, 2, 8, 1, 4, 0), (24, 2, 8, 1, 0, 0)]
    + [(10, 6, 2, 1, 4, 0), (26, 6, 2, 1, 0, 0)]
    + [(2 + 3 * u, 3, u, 0, 1, 1) for u in range(2)]
    + [(18 + 3 * u, 3, 8 + u, 0, 1, 1) for u in range(2)]
    + [(32 + 3 * w, 3, 2 + w, 0, 1, 1) for w in range(6)]
)


def look_up(table, heights, groups, cols, local, j):
    col_of = iota16((256, 128), 0)
    row_of = iota((heights, 128), 0).astype(F32)
    hits = [one_hot(col_of == spread(cols[i : i + 1, :], 256)) for i in (j, j + 1)]
    both = jnp.dot(table, jnp.concatenate(hits, 1), preferred_element_type=F32)
    found = []
    for i in (0, 1):
        lanes = slice(i * 128, i * 128 + 128)
        hit = row_of == jnp.broadcast_to(local[j + i : j + i + 1, :], (heights, 128))
        row = []
        for c in range(4):
            part = both[heights * c : heights * (c + 1), lanes]
            if c < 3:
                part = part + both[heights * (4 + c) : heights * (5 + c), lanes]
            row.append(jnp.sum(jnp.where(hit, part, 0.0), axis=0, keepdims=True))
        found.append(row)
    return found


def look_up_block(table, heights, cols, local):
    found = []
    for j in range(0, 8, 2):
        found += look_up(table, heights, 7, cols, local, j)
    return [jnp.concatenate([row[c] for row in found], 0) for c in range(4)]


def neighbours():
    x, y = lax.axis_index("gx"), lax.axis_index("gy")
    nx, ny = lax.axis_size("gx"), lax.axis_size("gy")
    left, right = lax.rem(x + nx - 1, nx), lax.rem(x + 1, nx)
    down, up = lax.rem(y + ny - 1, ny), lax.rem(y + 1, ny)
    sides = [(left, y), (right, y), (x, down), (x, up)]
    corners = [(left, down), (left, up), (right, down), (right, up)]
    return sides + corners


def prep_kernel(
    leaving_in, shift_in, vel_in, pos_in, axis_in,
    border, own_axis, ids, inner_mean, found, vel, got_side, got_corner,
    leaving, shift, pos, axis, row_s, col_s, sums, run_s, prep_s, axis_s, side, corner,
    load_sem, send_sem, recv_sem,
):
    targets = neighbours()
    barrier = pltpu.get_barrier_semaphore()
    is_first = lax.rem(lax.axis_index("gy"), 16) == 0
    is_last = lax.rem(lax.axis_index("gy"), 16) == 15

    def greet(places):
        for k in places:
            pl.semaphore_signal(barrier, inc=1, device_id=targets[k], device_id_type=MESH)

    greet((4, 6, 0, 1, 2))
    pl.when(jnp.logical_not(is_last))(lambda: greet((5, 7, 3)))
    loads = [
        pltpu.make_async_copy(source, target, load_sem.at[k])
        for k, (source, target) in enumerate(
            ((pos_in, pos), (shift_in, shift), (axis_in, axis), (vel_in, vel), (leaving_in, leaving))
        )
    ]
    for load in loads:
        load.start()
    axis_s[...] = jnp.zeros(axis_s.shape, F32)
    for k in (0, 2):
        side[k, 112:144, :] = jnp.zeros((32, 128), F32)
    corner[:, 20:24, :] = jnp.zeros((4, 4, 128), F32)
    for load in loads:
        load.wait()

    low_x = (shift[0] == 1).astype(jnp.int32)
    low_y = (shift[1] == 1).astype(jnp.int32)
    shifts = [shift[k].astype(F32) * 0.25 for k in range(3)]
    cell_x = jnp.floor(pos[0] + shifts[0]) + low_x.astype(F32)
    cell_y = jnp.floor(pos[1] + shifts[1]) + low_y.astype(F32)
    cell_z = jnp.floor(pos[2] + shifts[2])
    cell_z = jnp.where(cell_z >= float(CZ), cell_z - float(CZ), cell_z)
    half = jnp.floor(cell_y * 0.5)
    is_left = cell_x < 2.0
    is_right = cell_x > 7.0
    bottom = cell_x + jnp.where(is_left, 0.0, jnp.where(is_right, 16.0, 24.0))
    middle = 3.0 * cell_x + half + jnp.where(is_left, 1.0, jnp.where(is_right, -7.0, 25.0))
    row = jnp.where(half < 1.0, bottom, jnp.where(half > 3.0, cell_x + 8.0, middle))
    col = (cell_y - 2.0 * half) * float(CZ) + cell_z
    row_s[...] = row
    col_s[...] = col
    ids[...] = row * 256.0 + col

    row_of = iota16((MAIN, 128), 0)
    col_of = iota16((256, 128), 0)
    rest = iota((16, 128), 0)
    rest_row = (MAIN + rest % 2).astype(F32).astype(BF16)
    rest_is = [rest // 2 == g for g in range(7)]
    for chunk in range(8):
        left_parts = [[] for _ in range(8)]
        right_parts = []
        for j in range(8):
            r = chunk * 8 + j
            values = [jnp.ones((1, 128), F32)]
            for c in range(3):
                high = high_part(vel[c, r : r + 1, :])
                values += [high, vel[c, r : r + 1, :] - high]
            hit = row_of == spread(row_s[r : r + 1, :], MAIN)
            tail = jnp.broadcast_to(values[0], (16, 128))
            for g in range(7):
                wide = spread(values[g], MAIN)
                left_parts[g].append(jnp.where(hit, wide, jnp.zeros((MAIN, 128), BF16)))
                if g:
                    tail = jnp.where(rest_is[g], jnp.broadcast_to(values[g], (16, 128)), tail)
            hit = rest_row == spread(row_s[r : r + 1, :], 16)
            left_parts[7].append(jnp.where(hit, tail.astype(BF16), jnp.zeros((16, 128), BF16)))
            right_parts.append(one_hot(col_of == spread(col_s[r : r + 1, :], 256)))
        part = dot_nt(
            jnp.concatenate([jnp.concatenate(p, 1) for p in left_parts], 0),
            jnp.concatenate(right_parts, 1),
        )
        if chunk == 0:
            sums[...] = part
        else:
            sums[...] += part
    for c in range(4):
        if c == 0:
            group = sums[0:BORDER, :]
        else:
            at = (2 * c - 1) * MAIN
            group = sums[at : at + BORDER, :] + sums[at + MAIN : at + MAIN + BORDER, :]
        for par in range(2):
            lanes = slice(par * 128, par * 128 + 128)
            border[pl.ds(2 * c + par, BORDER, stride=8), :] = group[:, lanes]
    for k, start in enumerate((0, 16, 24, 8)):
        if start == 24:
            side[k, 0:64, :] = border[192:256, :]
            side[k, 64:80, :] = border[0:16, :]
        else:
            side[k, 0:80, :] = border[8 * start : 8 * start + 80, :]
    for k, start in enumerate((0, 8, 24, 16)):
        corner[k, 0:16, :] = border[8 * start : 8 * start + 16, :]

    for cx in range(CXL):
        at = (cx + 1) * 11 + 1
        axis_s[at : at + 8, :] = axis[cx * 8 : cx * 8 + 8, :].astype(F32)
    for par in range(2):
        for first, n, cx, cx_step, half_y, half_step in PIECES:
            start = (cx + 1 - low_x) * 11 + 2 * half_y + par + 1 - low_y
            step = 11 * cx_step + 2 * half_step
            own_axis[par, first : first + n, :] = axis_s[pl.ds(start, n, stride=step), :]
        own_axis[par, 50:56, :] = jnp.zeros((6, 128), F32)
        base = 112 + 16 * par
        for k, order in ((0, ((8, 2), (2, 6), (0, 2))), (2, ((0, 2), (26, 6), (24, 2)))):
            at = base
            for first, n in order:
                side[k, at : at + n, :] = own_axis[par, first : first + n, :]
                at += n
        corner[0, 20 + 2 * par : 22 + 2 * par, :] = own_axis[par, 0:2, :]

    slot = iota((8, 128), 0) * 128 + iota((8, 128), 1)
    lane = iota((8, 128), 1)
    counts = [leaving[k] for k in range(4)]
    starts = [jnp.int32(0), counts[0], counts[0] + counts[1], counts[0] + counts[1] + counts[2]]

    def run(load, d):
        if d == 0:
            return load(0)
        q = starts[d] // 128
        r = starts[d] - q * 128
        back = jnp.where(r == 0, 0, 128 - r)
        here = pltpu.roll(load(q), back, 1)
        after = pltpu.roll(load(q + 1), back, 1)
        return jnp.where(lane < 128 - r, here, after)

    def moved(d, run_row):
        if d == 0:
            return run_row + jnp.where(run_row < 2.0, 24.0, jnp.where(run_row < 8.0, 16.0, 8.0))
        if d == 1:
            return run_row - jnp.where(run_row < 18.0, 8.0, jnp.where(run_row < 24.0, 16.0, 24.0))
        if d == 2:
            return run_row + jnp.where(run_row < 2.0, 8.0, jnp.where(run_row < 26.0, -8.0, -16.0))
        return run_row + jnp.where(run_row < 10.0, -8.0, jnp.where(run_row < 16.0, 16.0, 8.0))

    flags = []
    for d in range(4):
        live = slot < counts[d]
        values = [run(lambda q, c=c: vel[c, pl.ds(q, 8), :], d) for c in range(3)]
        run_row = run(lambda q: row_s[pl.ds(q, 8), :], d)
        run_col = run(lambda q: col_s[pl.ds(q, 8), :], d)
        kept = live
        if d < 2:
            y = run(lambda q: pos[1, pl.ds(q, 8), :], d)
            down = live & (y < 0.0)
            up = live & (y >= float(CYL))
            kept = live & (y >= 0.0) & (y < float(CYL))
            flags += [down, up]
            for c in range(3):
                high = high_part(values[c])
                run_s[d, 16 * c : 16 * c + 8, :] = high
                run_s[d, 16 * c + 8 : 16 * c + 16, :] = values[c] - high
            run_s[d, 48:56, :] = run_row
            run_s[d, 56:64, :] = run_col
            run_s[d, 64:72, :] = jnp.ones((8, 128), F32)
            run_s[d, 72:128, :] = jnp.zeros((56, 128), F32)
        for c in range(3):
            side[d, 80 + 8 * c : 88 + 8 * c, :] = values[c]
        side[d, 104:112, :] = jnp.where(kept, moved(d, run_row) * 256.0 + run_col, -1.0)

    flag = jnp.concatenate([f.astype(F32) for f in flags], 0)
    flag16 = flag.astype(BF16)
    before = (iota((128, 128), 0) < iota((128, 128), 1)).astype(F32).astype(BF16)
    inside = jnp.dot(flag16, before, preferred_element_type=F32)
    total = jnp.dot(flag16, jnp.ones((128, 128), BF16), preferred_element_type=F32)
    r0, r1 = iota((32, 32), 0), iota((32, 32), 1)
    earlier = ((r1 < r0) & (r0 // 8 == r1 // 8)).astype(F32).astype(BF16)
    offset = jnp.dot(earlier, total.astype(BF16), preferred_element_type=F32)
    prep_s[...] = jnp.where(flag > 0.0, inside + offset, -1.0)
    rank_of = iota16((128, 128), 0)
    for d in range(2):
        rows = jnp.concatenate([run_s[d, pl.ds(r, 16, stride=8), :] for r in range(8)], 1).astype(BF16)
        for s in range(2):
            at = d * 16 + s * 8
            hits = [one_hot(rank_of == spread(prep_s[at + r : at + r + 1, :], 128)) for r in range(8)]
            packed = dot_nt(rows, jnp.concatenate(hits, 1))
            k = d * 2 + s
            for c in range(3):
                corner[k, 16 + c : 17 + c, :] = packed[2 * c : 2 * c + 1] + packed[2 * c + 1 : 2 * c + 2]
            there = (packed[6:7] + (16.0 - 32.0 * d)) * 256.0 + packed[7:8]
            corner[k, 19:20, :] = jnp.where(packed[8:9] > 0.5, there, -1.0)

    pl.semaphore_wait(barrier, jnp.where(is_first, 5, 8))
    copies = []
    for k in range(8):
        if k < 4:
            size = 144 if k in (0, 2) else 112
            source, target = side.at[k, pl.ds(0, size), :], got_side.at[k, pl.ds(0, size), :]
        else:
            source, target = corner.at[k - 4], got_corner.at[k - 4]
        copies.append(
            pltpu.make_async_remote_copy(
                src_ref=source,
                dst_ref=target,
                send_sem=send_sem.at[k],
                recv_sem=recv_sem.at[k],
                device_id=targets[k],
                device_id_type=MESH,
            )
        )
    for k in (5, 7, 0, 1, 3):
        copies[k].start()

    @pl.when(jnp.logical_not(is_first))
    def _():
        for k in (4, 6, 2):
            copies[k].start()

    def inner(group):
        at = group * MAIN + BORDER
        end = 7 * MAIN + 2 * group
        return jnp.concatenate([sums[at : at + 16, :], sums[end : end + 2, :], jnp.zeros((6, 256), F32)], 0)

    most = jnp.maximum(inner(0), 1.0)
    high_rows, low_rows = [], []
    for c in range(3):
        mean = (inner(1 + 2 * c) + inner(2 + 2 * c)) / most
        inner_mean[c] = mean
        high = high_part(mean)
        high_rows.append(high)
        low_rows.append(mean - high)
    high_rows.append(jnp.concatenate([own_axis[0, BORDER:56, :], own_axis[1, BORDER:56, :]], 1))
    table = jnp.concatenate(high_rows + low_rows, 0).astype(BF16)
    for b in range(1, 8):
        at = slice(8 * b, 8 * b + 8)
        looked = look_up_block(table, 24, col_s[at, :], row_s[at, :] - float(BORDER))
        for c in range(4):
            found[c, at, :] = looked[c]
    gone = starts[3] + counts[3]
    place = iota((ROWS, 128), 0) * 128 + iota((ROWS, 128), 1)
    ids[...] = jnp.where(place >= gone, ids[...], -1.0)

    for there, back in ((7, 4), (5, 6), (3, 2)):
        copies[there].wait_recv()
        pl.when(is_first)(copies[back].start)
    for k in (0, 1, 2, 4, 6):
        copies[k].wait_recv()
    for copy in copies:
        copy.wait_send()


def collide_kernel(
    shift_in, border, own_axis, ids, inner_mean, found, vel, got_side, got_corner,
    out_hbm, flow_hbm,
    shift, out, flow, total, means, load_sem, store_sem,
):
    load = pltpu.make_async_copy(shift_in, shift, load_sem)
    load.start()
    total[...] = border[...]
    for k, places in enumerate(
        (
            ((24, 0, 2), (18, 2, 6), (16, 8, 2)),
            ((8, 0, 2), (2, 2, 6), (0, 8, 2)),
            ((16, 0, 2), (10, 2, 6), (8, 8, 2)),
            ((0, 0, 2), (26, 2, 6), (24, 8, 2)),
        )
    ):
        for mine, theirs, n in places:
            total[8 * mine : 8 * (mine + n), :] += got_side[k, 8 * theirs : 8 * (theirs + n), :]
    for k, mine in enumerate((16, 24, 8, 0)):
        total[8 * mine : 8 * mine + 16, :] += got_corner[k, 0:16, :]
    numbers = []
    for par in range(2):
        number = own_axis[par, 0:BORDER, :]
        at = 112 + 16 * par
        gap = jnp.zeros((16, 128), F32)
        number = number + jnp.concatenate([gap, got_side[0, at : at + 16, :]], 0)
        number = number + jnp.concatenate([gap[0:8], got_side[2, at : at + 16, :], gap[0:8]], 0)
        pair = got_corner[0, 20 + 2 * par : 22 + 2 * par, :]
        number = number + jnp.concatenate([gap, pair, gap[0:14]], 0)
        numbers.append(number)
    groups = [None] * 7
    most = [jnp.maximum(total[pl.ds(par, BORDER, stride=8), :], 1.0) for par in range(2)]
    border_mean = []
    for c in range(3):
        halves = [total[pl.ds(2 + 2 * c + par, BORDER, stride=8), :] / most[par] for par in range(2)]
        mean = jnp.concatenate(halves, 1)
        border_mean.append(mean)
        groups[c] = high_part(mean)
        groups[4 + c] = mean - groups[c]
    groups[3] = jnp.concatenate(numbers, 1)
    table = jnp.concatenate(groups, 0).astype(BF16)
    choices = axis_table()

    def turn(at, live, v, looked):
        mean = looked[:3]
        number = looked[3].astype(jnp.int32)
        bits = [(number & (1 << k)) != 0 for k in range(4)]
        a = []
        for c in range(3):
            level = [entry[c] for entry in choices]
            for k in range(4):
                level = [jnp.where(bits[k], level[2 * m + 1], level[2 * m]) for m in range(len(level) // 2)]
            a.append(level[0])
        w = [v[c] - mean[c] for c in range(3)]
        cross = [
            a[1] * w[2] - a[2] * w[1],
            a[2] * w[0] - a[0] * w[2],
            a[0] * w[1] - a[1] * w[0],
        ]
        along = (a[0] * w[0] + a[1] * w[1] + a[2] * w[2]) * (1.0 - COS_TURN)
        for c in range(3):
            turned = mean[c] + COS_TURN * w[c] + SIN_TURN * cross[c] + along * a[c]
            out[c, at, :] = jnp.where(live, turned, 0.0)

    slot = iota((8, 128), 0) * 128 + iota((8, 128), 1)
    arrived = []
    for k in (1, 0, 3, 2):
        v = [got_side[k, 80 + 8 * c : 88 + 8 * c, :] for c in range(4)]
        if k > 1:
            first, second = ((2, 0), (3, 1))[k - 2]
            n0 = jnp.sum((v[3] >= 0.0).astype(jnp.int32))
            n1 = jnp.sum((got_corner[first, 19:20, :] >= 0.0).astype(jnp.int32))
            in_first = (slot >= n0) & (slot < n0 + n1)
            in_second = (slot >= n0 + n1) & (slot < n0 + n1 + 128)
            by1, by2 = lax.rem(n0, 128), lax.rem(n0 + n1, 128)
            for c in range(4):
                at = slice(16 + c, 17 + c)
                one = pltpu.roll(jnp.broadcast_to(got_corner[first, at, :], (8, 128)), by1, 1)
                two = pltpu.roll(jnp.broadcast_to(got_corner[second, at, :], (8, 128)), by2, 1)
                v[c] = jnp.where(in_first, one, jnp.where(in_second, two, v[c]))
        arrived.append(v)

    stores = []

    def store(source, target):
        copy = pltpu.make_async_copy(source, target, store_sem.at[len(stores)])
        copy.start()
        stores.append(copy)

    for v, at, window in zip(arrived, (64, 72, 80, 88), (0, 16, 24, 8)):
        rows = jnp.floor(v[3] * (1.0 / 256.0))
        cols = v[3] - rows * 256.0
        if window == 24:
            part = [jnp.concatenate([g[24:32], g[0:8]], 0) for g in groups]
            local = jnp.where(rows < 2.0, rows + 8.0, rows - 24.0)
        else:
            part = [g[window : window + 16] for g in groups]
            local = rows - float(window)
        looked = look_up_block(jnp.concatenate(part, 0).astype(BF16), 16, cols, local)
        turn(slice(at, at + 8), v[3] >= 0.0, v, looked)

    out[:, 0:8, :] = jnp.zeros((3, 8, 128), F32)
    for b in range(1, 8):
        at = slice(8 * b, 8 * b + 8)
        block = ids[at, :]
        rows = jnp.floor(block * (1.0 / 256.0))
        looked = look_up_block(table, BORDER, block - rows * 256.0, rows)
        turn(at, block >= 0.0, [vel[c, at, :] for c in range(3)], [looked[c] + found[c, at, :] for c in range(4)])
    store(out, out_hbm)

    for c in range(3):
        for par in range(2):
            lanes = slice(par * 128, par * 128 + 128)
            for first, n, cx, cx_step, half_y, half_step in PIECES:
                if first < BORDER:
                    piece = border_mean[c][first : first + n, lanes]
                else:
                    piece = inner_mean[c, first - BORDER : first - BORDER + n, lanes]
                start = cx * 10 + 2 * half_y + par
                means[c, pl.ds(start, n, stride=10 * cx_step + 2 * half_step), :] = piece
    load.wait()
    low_x = (shift[0] == 1).astype(jnp.int32)
    low_y = (shift[1] == 1).astype(jnp.int32)
    for c in range(3):
        for cx in range(CXL):
            flow[c, cx * 8 : cx * 8 + 8, :] = means[c, pl.ds((cx + low_x) * 10 + low_y, 8), :]
    store(flow, flow_hbm)
    for copy in stores:
        copy.wait()


def shape(*dims):
    return jax.ShapeDtypeStruct(dims, F32)


def per_device(velocity, position, leaving, grid_shift, axis_index):
    vel = velocity.reshape(3, ROWS, 128)
    pos = position.reshape(3, ROWS, 128)
    axis = axis_index.reshape(64, 128)
    leaving = leaving.reshape(4)
    vel, pos, axis, leaving, grid_shift = [
        pltpu.with_memory_space_constraint(v, pltpu.HBM) for v in (vel, pos, axis, leaving, grid_shift)
    ]
    vmem = pl.BlockSpec(memory_space=pltpu.VMEM)
    hbm = pl.BlockSpec(memory_space=pltpu.HBM)
    parts = pl.pallas_call(
        prep_kernel,
        name="prep",
        out_shape=(
            shape(8 * BORDER, 128),
            shape(2, 56, 128),
            shape(ROWS, 128),
            shape(3, 24, 256),
            shape(4, ROWS, 128),
            shape(3, ROWS, 128),
            shape(4, 144, 128),
            shape(4, 24, 128),
        ),
        in_specs=[hbm] * 5,
        out_specs=(vmem,) * 8,
        scratch_shapes=[
            pltpu.SMEM((4,), jnp.int32),
            pltpu.SMEM((3,), jnp.int32),
            pltpu.VMEM((3, ROWS, 128), F32),
            pltpu.VMEM((64, 128), jnp.int32),
            pltpu.VMEM((ROWS, 128), F32),
            pltpu.VMEM((ROWS, 128), F32),
            pltpu.VMEM((7 * MAIN + 16, 256), F32),
            pltpu.VMEM((2, 128, 128), F32),
            pltpu.VMEM((32, 128), F32),
            pltpu.VMEM((128, 128), F32),
            pltpu.VMEM((4, 144, 128), F32),
            pltpu.VMEM((4, 24, 128), F32),
            pltpu.SemaphoreType.DMA((5,)),
            pltpu.SemaphoreType.DMA((8,)),
            pltpu.SemaphoreType.DMA((8,)),
        ],
        compiler_params=pltpu.CompilerParams(
            collective_id=0, has_side_effects=True, vmem_limit_bytes=32 << 20
        ),
    )(leaving, grid_shift, vel, pos, axis)
    out, flow = pl.pallas_call(
        collide_kernel,
        name="collide",
        out_shape=(shape(3, SLOTS, 128), shape(3, 64, 128)),
        in_specs=[hbm] + [vmem] * 8,
        out_specs=(hbm, hbm),
        scratch_shapes=[
            pltpu.SMEM((3,), jnp.int32),
            pltpu.VMEM((3, SLOTS, 128), F32),
            pltpu.VMEM((3, 64, 128), F32),
            pltpu.VMEM((8 * BORDER, 128), F32),
            pltpu.VMEM((3, 104, 128), F32),
            pltpu.SemaphoreType.DMA,
            pltpu.SemaphoreType.DMA((3,)),
        ],
        compiler_params=pltpu.CompilerParams(vmem_limit_bytes=32 << 20),
    )(grid_shift, *parts)
    return out.reshape(3, 1, 1, SLOTS * 128), flow.reshape(3, 1, 1, 64 * 128)


def solution(mesh):
    return jax.shard_map(
        per_device,
        mesh=mesh,
        in_specs=(
            P(None, "gx", "gy", None),
            P(None, "gx", "gy", None),
            P("gx", "gy", None),
            P(),
            P("gx", "gy", None),
        ),
        out_specs=(P(None, "gx", "gy", None), P(None, "gx", "gy", None)),
        check_vma=False,
    )
```

```python
import math

import jax
import jax.numpy as jnp
from jax import lax
from jax.experimental import pallas as pl
from jax.experimental.pallas import tpu as pltpu
from jax.sharding import PartitionSpec as P

CXL = 8
CYL = 8
CZ = 128
NAX = 16
ROWS = 64
SLOTS = 96
BORDER = 32
INNER = 18
MAIN = 48

COS_TURN = -0.6427876096865393
SIN_TURN = 0.766044443118978
GOLDEN_TURN = 2.399963229728653

F32 = jnp.float32
BF16 = jnp.bfloat16
MESH = pl.DeviceIdType.MESH


def axis_table():
    table = []
    for number in range(NAX):
        height = 1.0 - (2.0 * number + 1.0) / NAX
        radius = math.sqrt(1.0 - height * height)
        phase = number * GOLDEN_TURN
        table.append((radius * math.cos(phase), radius * math.sin(phase), height))
    return table


def dot_nt(a, b):
    return lax.dot_general(a, b, (((1,), (1,)), ((), ())), preferred_element_type=F32)


def iota(shape, dim):
    return lax.broadcasted_iota(jnp.int32, shape, dim)


def iota16(shape, dim):
    return iota(shape, dim).astype(F32).astype(BF16)


def spread(row, height):
    return jnp.broadcast_to(row, (height, 128)).astype(BF16)


def one_hot(hit):
    return jnp.where(hit, jnp.ones(hit.shape, BF16), jnp.zeros(hit.shape, BF16))


def high_part(value):
    return value.astype(BF16).astype(F32)


PIECES = (
    [(0, 2, 0, 1, 0, 0), (8, 2, 0, 1, 4, 0), (16, 2, 8, 1, 4, 0), (24, 2, 8, 1, 0, 0)]
    + [(10, 6, 2, 1, 4, 0), (26, 6, 2, 1, 0, 0)]
    + [(2 + 3 * u, 3, u, 0, 1, 1) for u in range(2)]
    + [(18 + 3 * u, 3, 8 + u, 0, 1, 1) for u in range(2)]
    + [(32 + 3 * w, 3, 2 + w, 0, 1, 1) for w in range(6)]
)


def look_up(table, heights, groups, cols, local, j):
    col_of = iota16((256, 128), 0)
    row_of = iota((heights, 128), 0).astype(F32)
    hits = [one_hot(col_of == spread(cols[i : i + 1, :], 256)) for i in (j, j + 1)]
    both = jnp.dot(table, jnp.concatenate(hits, 1), preferred_element_type=F32)
    found = []
    for i in (0, 1):
        lanes = slice(i * 128, i * 128 + 128)
        hit = row_of == jnp.broadcast_to(local[j + i : j + i + 1, :], (heights, 128))
        row = []
        for c in range(4):
            part = both[heights * c : heights * (c + 1), lanes]
            if c < 3:
                part = part + both[heights * (4 + c) : heights * (5 + c), lanes]
            row.append(jnp.sum(jnp.where(hit, part, 0.0), axis=0, keepdims=True))
        found.append(row)
    return found


def look_up_block(table, heights, cols, local):
    found = []
    for j in range(0, 8, 2):
        found += look_up(table, heights, 7, cols, local, j)
    return [jnp.concatenate([row[c] for row in found], 0) for c in range(4)]


def neighbours():
    x, y = lax.axis_index("gx"), lax.axis_index("gy")
    nx, ny = lax.axis_size("gx"), lax.axis_size("gy")
    left, right = lax.rem(x + nx - 1, nx), lax.rem(x + 1, nx)
    down, up = lax.rem(y + ny - 1, ny), lax.rem(y + 1, ny)
    sides = [(left, y), (right, y), (x, down), (x, up)]
    corners = [(left, down), (left, up), (right, down), (right, up)]
    return sides + corners


def prep_kernel(
    leaving_in, shift_in, vel_in, pos_in, axis_in,
    border, own_axis, ids, inner_mean, found, vel, got_side, got_corner,
    leaving, shift, pos, axis, row_s, col_s, sums, run_s, prep_s, axis_s, side, corner,
    load_sem, send_sem, recv_sem,
):
    targets = neighbours()
    barrier = pltpu.get_barrier_semaphore()
    for k in (7, 5, 6, 4, 1, 0, 3, 2):
        pl.semaphore_signal(barrier, inc=1, device_id=targets[k], device_id_type=MESH)
    loads = [
        pltpu.make_async_copy(source, target, load_sem.at[k])
        for k, (source, target) in enumerate(
            ((pos_in, pos), (shift_in, shift), (axis_in, axis), (vel_in, vel), (leaving_in, leaving))
        )
    ]
    for load in loads:
        load.start()
    axis_s[...] = jnp.zeros(axis_s.shape, F32)
    for k in (0, 2):
        side[k, 112:144, :] = jnp.zeros((32, 128), F32)
    corner[:, 20:24, :] = jnp.zeros((4, 4, 128), F32)
    for load in loads:
        load.wait()

    low_x = (shift[0] == 1).astype(jnp.int32)
    low_y = (shift[1] == 1).astype(jnp.int32)
    shifts = [shift[k].astype(F32) * 0.25 for k in range(3)]
    cell_x = jnp.floor(pos[0] + shifts[0]) + low_x.astype(F32)
    cell_y = jnp.floor(pos[1] + shifts[1]) + low_y.astype(F32)
    cell_z = jnp.floor(pos[2] + shifts[2])
    cell_z = jnp.where(cell_z >= float(CZ), cell_z - float(CZ), cell_z)
    half = jnp.floor(cell_y * 0.5)
    is_left = cell_x < 2.0
    is_right = cell_x > 7.0
    bottom = cell_x + jnp.where(is_left, 0.0, jnp.where(is_right, 16.0, 24.0))
    middle = 3.0 * cell_x + half + jnp.where(is_left, 1.0, jnp.where(is_right, -7.0, 25.0))
    row = jnp.where(half < 1.0, bottom, jnp.where(half > 3.0, cell_x + 8.0, middle))
    col = (cell_y - 2.0 * half) * float(CZ) + cell_z
    row_s[...] = row
    col_s[...] = col
    ids[...] = row * 256.0 + col

    row_of = iota16((MAIN, 128), 0)
    col_of = iota16((256, 128), 0)
    rest = iota((16, 128), 0)
    rest_row = (MAIN + rest % 2).astype(F32).astype(BF16)
    rest_is = [rest // 2 == g for g in range(7)]
    for chunk in range(8):
        left_parts = [[] for _ in range(8)]
        right_parts = []
        for j in range(8):
            r = chunk * 8 + j
            values = [jnp.ones((1, 128), F32)]
            for c in range(3):
                high = high_part(vel[c, r : r + 1, :])
                values += [high, vel[c, r : r + 1, :] - high]
            hit = row_of == spread(row_s[r : r + 1, :], MAIN)
            tail = jnp.broadcast_to(values[0], (16, 128))
            for g in range(7):
                wide = spread(values[g], MAIN)
                left_parts[g].append(jnp.where(hit, wide, jnp.zeros((MAIN, 128), BF16)))
                if g:
                    tail = jnp.where(rest_is[g], jnp.broadcast_to(values[g], (16, 128)), tail)
            hit = rest_row == spread(row_s[r : r + 1, :], 16)
            left_parts[7].append(jnp.where(hit, tail.astype(BF16), jnp.zeros((16, 128), BF16)))
            right_parts.append(one_hot(col_of == spread(col_s[r : r + 1, :], 256)))
        part = dot_nt(
            jnp.concatenate([jnp.concatenate(p, 1) for p in left_parts], 0),
            jnp.concatenate(right_parts, 1),
        )
        if chunk == 0:
            sums[...] = part
        else:
            sums[...] += part
    for c in range(4):
        if c == 0:
            group = sums[0:BORDER, :]
        else:
            at = (2 * c - 1) * MAIN
            group = sums[at : at + BORDER, :] + sums[at + MAIN : at + MAIN + BORDER, :]
        for par in range(2):
            lanes = slice(par * 128, par * 128 + 128)
            border[pl.ds(2 * c + par, BORDER, stride=8), :] = group[:, lanes]
    for k, start in enumerate((0, 16, 24, 8)):
        if start == 24:
            side[k, 0:64, :] = border[192:256, :]
            side[k, 64:80, :] = border[0:16, :]
        else:
            side[k, 0:80, :] = border[8 * start : 8 * start + 80, :]
    for k, start in enumerate((0, 8, 24, 16)):
        corner[k, 0:16, :] = border[8 * start : 8 * start + 16, :]

    for cx in range(CXL):
        at = (cx + 1) * 11 + 1
        axis_s[at : at + 8, :] = axis[cx * 8 : cx * 8 + 8, :].astype(F32)
    for par in range(2):
        for first, n, cx, cx_step, half_y, half_step in PIECES:
            start = (cx + 1 - low_x) * 11 + 2 * half_y + par + 1 - low_y
            step = 11 * cx_step + 2 * half_step
            own_axis[par, first : first + n, :] = axis_s[pl.ds(start, n, stride=step), :]
        own_axis[par, 50:56, :] = jnp.zeros((6, 128), F32)
        base = 112 + 16 * par
        for k, order in ((0, ((8, 2), (2, 6), (0, 2))), (2, ((0, 2), (26, 6), (24, 2)))):
            at = base
            for first, n in order:
                side[k, at : at + n, :] = own_axis[par, first : first + n, :]
                at += n
        corner[0, 20 + 2 * par : 22 + 2 * par, :] = own_axis[par, 0:2, :]

    slot = iota((8, 128), 0) * 128 + iota((8, 128), 1)
    lane = iota((8, 128), 1)
    counts = [leaving[k] for k in range(4)]
    starts = [jnp.int32(0), counts[0], counts[0] + counts[1], counts[0] + counts[1] + counts[2]]

    def run(load, d):
        if d == 0:
            return load(0)
        q = starts[d] // 128
        r = starts[d] - q * 128
        back = jnp.where(r == 0, 0, 128 - r)
        here = pltpu.roll(load(q), back, 1)
        after = pltpu.roll(load(q + 1), back, 1)
        return jnp.where(lane < 128 - r, here, after)

    def moved(d, run_row):
        if d == 0:
            return run_row + jnp.where(run_row < 2.0, 24.0, jnp.where(run_row < 8.0, 16.0, 8.0))
        if d == 1:
            return run_row - jnp.where(run_row < 18.0, 8.0, jnp.where(run_row < 24.0, 16.0, 24.0))
        if d == 2:
            return run_row + jnp.where(run_row < 2.0, 8.0, jnp.where(run_row < 26.0, -8.0, -16.0))
        return run_row + jnp.where(run_row < 10.0, -8.0, jnp.where(run_row < 16.0, 16.0, 8.0))

    flags = []
    for d in range(4):
        live = slot < counts[d]
        values = [run(lambda q, c=c: vel[c, pl.ds(q, 8), :], d) for c in range(3)]
        run_row = run(lambda q: row_s[pl.ds(q, 8), :], d)
        run_col = run(lambda q: col_s[pl.ds(q, 8), :], d)
        kept = live
        if d < 2:
            y = run(lambda q: pos[1, pl.ds(q, 8), :], d)
            down = live & (y < 0.0)
            up = live & (y >= float(CYL))
            kept = live & (y >= 0.0) & (y < float(CYL))
            flags += [down, up]
            for c in range(3):
                high = high_part(values[c])
                run_s[d, 16 * c : 16 * c + 8, :] = high
                run_s[d, 16 * c + 8 : 16 * c + 16, :] = values[c] - high
            run_s[d, 48:56, :] = run_row
            run_s[d, 56:64, :] = run_col
            run_s[d, 64:72, :] = jnp.ones((8, 128), F32)
            run_s[d, 72:128, :] = jnp.zeros((56, 128), F32)
        for c in range(3):
            side[d, 80 + 8 * c : 88 + 8 * c, :] = values[c]
        side[d, 104:112, :] = jnp.where(kept, moved(d, run_row) * 256.0 + run_col, -1.0)

    flag = jnp.concatenate([f.astype(F32) for f in flags], 0)
    flag16 = flag.astype(BF16)
    before = (iota((128, 128), 0) < iota((128, 128), 1)).astype(F32).astype(BF16)
    inside = jnp.dot(flag16, before, preferred_element_type=F32)
    total = jnp.dot(flag16, jnp.ones((128, 128), BF16), preferred_element_type=F32)
    r0, r1 = iota((32, 32), 0), iota((32, 32), 1)
    earlier = ((r1 < r0) & (r0 // 8 == r1 // 8)).astype(F32).astype(BF16)
    offset = jnp.dot(earlier, total.astype(BF16), preferred_element_type=F32)
    prep_s[...] = jnp.where(flag > 0.0, inside + offset, -1.0)
    rank_of = iota16((128, 128), 0)
    for d in range(2):
        rows = jnp.concatenate([run_s[d, pl.ds(r, 16, stride=8), :] for r in range(8)], 1).astype(BF16)
        for s in range(2):
            at = d * 16 + s * 8
            hits = [one_hot(rank_of == spread(prep_s[at + r : at + r + 1, :], 128)) for r in range(8)]
            packed = dot_nt(rows, jnp.concatenate(hits, 1))
            k = d * 2 + s
            for c in range(3):
                corner[k, 16 + c : 17 + c, :] = packed[2 * c : 2 * c + 1] + packed[2 * c + 1 : 2 * c + 2]
            there = (packed[6:7] + (16.0 - 32.0 * d)) * 256.0 + packed[7:8]
            corner[k, 19:20, :] = jnp.where(packed[8:9] > 0.5, there, -1.0)

    pl.semaphore_wait(barrier, 8)
    copies = []
    for k in range(8):
        if k < 4:
            size = 144 if k in (0, 2) else 112
            source, target = side.at[k, pl.ds(0, size), :], got_side.at[k, pl.ds(0, size), :]
        else:
            source, target = corner.at[k - 4], got_corner.at[k - 4]
        copies.append(
            pltpu.make_async_remote_copy(
                src_ref=source,
                dst_ref=target,
                send_sem=send_sem.at[k],
                recv_sem=recv_sem.at[k],
                device_id=targets[k],
                device_id_type=MESH,
            )
        )
    for k in (7, 5, 6, 4, 1, 0, 3, 2):
        copies[k].start()

    def inner(group):
        at = group * MAIN + BORDER
        end = 7 * MAIN + 2 * group
        return jnp.concatenate([sums[at : at + 16, :], sums[end : end + 2, :], jnp.zeros((6, 256), F32)], 0)

    most = jnp.maximum(inner(0), 1.0)
    high_rows, low_rows = [], []
    for c in range(3):
        mean = (inner(1 + 2 * c) + inner(2 + 2 * c)) / most
        inner_mean[c] = mean
        high = high_part(mean)
        high_rows.append(high)
        low_rows.append(mean - high)
    high_rows.append(jnp.concatenate([own_axis[0, BORDER:56, :], own_axis[1, BORDER:56, :]], 1))
    table = jnp.concatenate(high_rows + low_rows, 0).astype(BF16)
    for b in range(1, 8):
        at = slice(8 * b, 8 * b + 8)
        looked = look_up_block(table, 24, col_s[at, :], row_s[at, :] - float(BORDER))
        for c in range(4):
            found[c, at, :] = looked[c]
    gone = starts[3] + counts[3]
    place = iota((ROWS, 128), 0) * 128 + iota((ROWS, 128), 1)
    ids[...] = jnp.where(place >= gone, ids[...], -1.0)
    for copy in copies:
        copy.wait()


def collide_kernel(
    shift_in, border, own_axis, ids, inner_mean, found, vel, got_side, got_corner,
    out_hbm, flow_hbm,
    shift, out, flow, total, means, load_sem, store_sem,
):
    load = pltpu.make_async_copy(shift_in, shift, load_sem)
    load.start()
    total[...] = border[...]
    for k, places in enumerate(
        (
            ((24, 0, 2), (18, 2, 6), (16, 8, 2)),
            ((8, 0, 2), (2, 2, 6), (0, 8, 2)),
            ((16, 0, 2), (10, 2, 6), (8, 8, 2)),
            ((0, 0, 2), (26, 2, 6), (24, 8, 2)),
        )
    ):
        for mine, theirs, n in places:
            total[8 * mine : 8 * (mine + n), :] += got_side[k, 8 * theirs : 8 * (theirs + n), :]
    for k, mine in enumerate((16, 24, 8, 0)):
        total[8 * mine : 8 * mine + 16, :] += got_corner[k, 0:16, :]
    numbers = []
    for par in range(2):
        number = own_axis[par, 0:BORDER, :]
        at = 112 + 16 * par
        gap = jnp.zeros((16, 128), F32)
        number = number + jnp.concatenate([gap, got_side[0, at : at + 16, :]], 0)
        number = number + jnp.concatenate([gap[0:8], got_side[2, at : at + 16, :], gap[0:8]], 0)
        pair = got_corner[0, 20 + 2 * par : 22 + 2 * par, :]
        number = number + jnp.concatenate([gap, pair, gap[0:14]], 0)
        numbers.append(number)
    groups = [None] * 7
    most = [jnp.maximum(total[pl.ds(par, BORDER, stride=8), :], 1.0) for par in range(2)]
    border_mean = []
    for c in range(3):
        halves = [total[pl.ds(2 + 2 * c + par, BORDER, stride=8), :] / most[par] for par in range(2)]
        mean = jnp.concatenate(halves, 1)
        border_mean.append(mean)
        groups[c] = high_part(mean)
        groups[4 + c] = mean - groups[c]
    groups[3] = jnp.concatenate(numbers, 1)
    table = jnp.concatenate(groups, 0).astype(BF16)
    choices = axis_table()

    def turn(at, live, v, looked):
        mean = looked[:3]
        number = looked[3].astype(jnp.int32)
        bits = [(number & (1 << k)) != 0 for k in range(4)]
        a = []
        for c in range(3):
            level = [entry[c] for entry in choices]
            for k in range(4):
                level = [jnp.where(bits[k], level[2 * m + 1], level[2 * m]) for m in range(len(level) // 2)]
            a.append(level[0])
        w = [v[c] - mean[c] for c in range(3)]
        cross = [
            a[1] * w[2] - a[2] * w[1],
            a[2] * w[0] - a[0] * w[2],
            a[0] * w[1] - a[1] * w[0],
        ]
        along = (a[0] * w[0] + a[1] * w[1] + a[2] * w[2]) * (1.0 - COS_TURN)
        for c in range(3):
            turned = mean[c] + COS_TURN * w[c] + SIN_TURN * cross[c] + along * a[c]
            out[c, at, :] = jnp.where(live, turned, 0.0)

    slot = iota((8, 128), 0) * 128 + iota((8, 128), 1)
    arrived = []
    for k in (1, 0, 3, 2):
        v = [got_side[k, 80 + 8 * c : 88 + 8 * c, :] for c in range(4)]
        if k > 1:
            first, second = ((2, 0), (3, 1))[k - 2]
            n0 = jnp.sum((v[3] >= 0.0).astype(jnp.int32))
            n1 = jnp.sum((got_corner[first, 19:20, :] >= 0.0).astype(jnp.int32))
            in_first = (slot >= n0) & (slot < n0 + n1)
            in_second = (slot >= n0 + n1) & (slot < n0 + n1 + 128)
            by1, by2 = lax.rem(n0, 128), lax.rem(n0 + n1, 128)
            for c in range(4):
                at = slice(16 + c, 17 + c)
                one = pltpu.roll(jnp.broadcast_to(got_corner[first, at, :], (8, 128)), by1, 1)
                two = pltpu.roll(jnp.broadcast_to(got_corner[second, at, :], (8, 128)), by2, 1)
                v[c] = jnp.where(in_first, one, jnp.where(in_second, two, v[c]))
        arrived.append(v)

    stores = []

    def store(source, target):
        copy = pltpu.make_async_copy(source, target, store_sem.at[len(stores)])
        copy.start()
        stores.append(copy)

    out[:, 0:8, :] = jnp.zeros((3, 8, 128), F32)
    for b in range(1, 8):
        at = slice(8 * b, 8 * b + 8)
        block = ids[at, :]
        rows = jnp.floor(block * (1.0 / 256.0))
        looked = look_up_block(table, BORDER, block - rows * 256.0, rows)
        turn(at, block >= 0.0, [vel[c, at, :] for c in range(3)], [looked[c] + found[c, at, :] for c in range(4)])

    for v, at, window in zip(arrived, (64, 72, 80, 88), (0, 16, 24, 8)):
        rows = jnp.floor(v[3] * (1.0 / 256.0))
        cols = v[3] - rows * 256.0
        if window == 24:
            part = [jnp.concatenate([g[24:32], g[0:8]], 0) for g in groups]
            local = jnp.where(rows < 2.0, rows + 8.0, rows - 24.0)
        else:
            part = [g[window : window + 16] for g in groups]
            local = rows - float(window)
        looked = look_up_block(jnp.concatenate(part, 0).astype(BF16), 16, cols, local)
        turn(slice(at, at + 8), v[3] >= 0.0, v, looked)
    store(out, out_hbm)

    for c in range(3):
        for par in range(2):
            lanes = slice(par * 128, par * 128 + 128)
            for first, n, cx, cx_step, half_y, half_step in PIECES:
                if first < BORDER:
                    piece = border_mean[c][first : first + n, lanes]
                else:
                    piece = inner_mean[c, first - BORDER : first - BORDER + n, lanes]
                start = cx * 10 + 2 * half_y + par
                means[c, pl.ds(start, n, stride=10 * cx_step + 2 * half_step), :] = piece
    load.wait()
    low_x = (shift[0] == 1).astype(jnp.int32)
    low_y = (shift[1] == 1).astype(jnp.int32)
    for c in range(3):
        for cx in range(CXL):
            flow[c, cx * 8 : cx * 8 + 8, :] = means[c, pl.ds((cx + low_x) * 10 + low_y, 8), :]
    store(flow, flow_hbm)
    for copy in stores:
        copy.wait()


def shape(*dims):
    return jax.ShapeDtypeStruct(dims, F32)


def per_device(velocity, position, leaving, grid_shift, axis_index):
    vel = velocity.reshape(3, ROWS, 128)
    pos = position.reshape(3, ROWS, 128)
    axis = axis_index.reshape(64, 128)
    leaving = leaving.reshape(4)
    vel, pos, axis, leaving, grid_shift = [
        pltpu.with_memory_space_constraint(v, pltpu.HBM) for v in (vel, pos, axis, leaving, grid_shift)
    ]
    vmem = pl.BlockSpec(memory_space=pltpu.VMEM)
    hbm = pl.BlockSpec(memory_space=pltpu.HBM)
    parts = pl.pallas_call(
        prep_kernel,
        name="prep",
        out_shape=(
            shape(8 * BORDER, 128),
            shape(2, 56, 128),
            shape(ROWS, 128),
            shape(3, 24, 256),
            shape(4, ROWS, 128),
            shape(3, ROWS, 128),
            shape(4, 144, 128),
            shape(4, 24, 128),
        ),
        in_specs=[hbm] * 5,
        out_specs=(vmem,) * 8,
        scratch_shapes=[
            pltpu.SMEM((4,), jnp.int32),
            pltpu.SMEM((3,), jnp.int32),
            pltpu.VMEM((3, ROWS, 128), F32),
            pltpu.VMEM((64, 128), jnp.int32),
            pltpu.VMEM((ROWS, 128), F32),
            pltpu.VMEM((ROWS, 128), F32),
            pltpu.VMEM((7 * MAIN + 16, 256), F32),
            pltpu.VMEM((2, 128, 128), F32),
            pltpu.VMEM((32, 128), F32),
            pltpu.VMEM((128, 128), F32),
            pltpu.VMEM((4, 144, 128), F32),
            pltpu.VMEM((4, 24, 128), F32),
            pltpu.SemaphoreType.DMA((5,)),
            pltpu.SemaphoreType.DMA((8,)),
            pltpu.SemaphoreType.DMA((8,)),
        ],
        compiler_params=pltpu.CompilerParams(
            collective_id=0, has_side_effects=True, vmem_limit_bytes=32 << 20
        ),
    )(leaving, grid_shift, vel, pos, axis)
    out, flow = pl.pallas_call(
        collide_kernel,
        name="collide",
        out_shape=(shape(3, SLOTS, 128), shape(3, 64, 128)),
        in_specs=[hbm] + [vmem] * 8,
        out_specs=(hbm, hbm),
        scratch_shapes=[
            pltpu.SMEM((3,), jnp.int32),
            pltpu.VMEM((3, SLOTS, 128), F32),
            pltpu.VMEM((3, 64, 128), F32),
            pltpu.VMEM((8 * BORDER, 128), F32),
            pltpu.VMEM((3, 104, 128), F32),
            pltpu.SemaphoreType.DMA,
            pltpu.SemaphoreType.DMA((3,)),
        ],
        compiler_params=pltpu.CompilerParams(vmem_limit_bytes=32 << 20),
    )(grid_shift, *parts)
    return out.reshape(3, 1, 1, SLOTS * 128), flow.reshape(3, 1, 1, 64 * 128)


def solution(mesh):
    return jax.shard_map(
        per_device,
        mesh=mesh,
        in_specs=(
            P(None, "gx", "gy", None),
            P(None, "gx", "gy", None),
            P("gx", "gy", None),
            P(),
            P("gx", "gy", None),
        ),
        out_specs=(P(None, "gx", "gy", None), P(None, "gx", "gy", None)),
        check_vma=False,
    )
```

```python
import math

import jax
import jax.numpy as jnp
from jax import lax
from jax.experimental import pallas as pl
from jax.experimental.pallas import tpu as pltpu
from jax.sharding import PartitionSpec as P

CXL = 8
CYL = 8
CZ = 128
NAX = 16
ROWS = 64
SLOTS = 96
BORDER = 32
INNER = 18
MAIN = 48

COS_TURN = -0.6427876096865393
SIN_TURN = 0.766044443118978
GOLDEN_TURN = 2.399963229728653

F32 = jnp.float32
BF16 = jnp.bfloat16
MESH = pl.DeviceIdType.MESH


def axis_table():
    table = []
    for number in range(NAX):
        height = 1.0 - (2.0 * number + 1.0) / NAX
        radius = math.sqrt(1.0 - height * height)
        phase = number * GOLDEN_TURN
        table.append((radius * math.cos(phase), radius * math.sin(phase), height))
    return table


def dot_nt(a, b):
    return lax.dot_general(a, b, (((1,), (1,)), ((), ())), preferred_element_type=F32)


def iota(shape, dim):
    return lax.broadcasted_iota(jnp.int32, shape, dim)


def iota16(shape, dim):
    return iota(shape, dim).astype(F32).astype(BF16)


def spread(row, height):
    return jnp.broadcast_to(row, (height, 128)).astype(BF16)


def one_hot(hit):
    return jnp.where(hit, jnp.ones(hit.shape, BF16), jnp.zeros(hit.shape, BF16))


def high_part(value):
    return value.astype(BF16).astype(F32)


PIECES = (
    [(0, 2, 0, 1, 0, 0), (8, 2, 0, 1, 4, 0), (16, 2, 8, 1, 4, 0), (24, 2, 8, 1, 0, 0)]
    + [(10, 6, 2, 1, 4, 0), (26, 6, 2, 1, 0, 0)]
    + [(2 + 3 * u, 3, u, 0, 1, 1) for u in range(2)]
    + [(18 + 3 * u, 3, 8 + u, 0, 1, 1) for u in range(2)]
    + [(32 + 3 * w, 3, 2 + w, 0, 1, 1) for w in range(6)]
)


def look_up(table, heights, groups, cols, local, j):
    col_of = iota16((256, 128), 0)
    row_of = iota((heights, 128), 0).astype(F32)
    hits = [one_hot(col_of == spread(cols[i : i + 1, :], 256)) for i in (j, j + 1)]
    both = jnp.dot(table, jnp.concatenate(hits, 1), preferred_element_type=F32)
    found = []
    for i in (0, 1):
        lanes = slice(i * 128, i * 128 + 128)
        hit = row_of == jnp.broadcast_to(local[j + i : j + i + 1, :], (heights, 128))
        row = []
        for c in range(4):
            part = both[heights * c : heights * (c + 1), lanes]
            if c < 3:
                part = part + both[heights * (4 + c) : heights * (5 + c), lanes]
            row.append(jnp.sum(jnp.where(hit, part, 0.0), axis=0, keepdims=True))
        found.append(row)
    return found


def look_up_block(table, heights, cols, local):
    found = []
    for j in range(0, 8, 2):
        found += look_up(table, heights, 7, cols, local, j)
    return [jnp.concatenate([row[c] for row in found], 0) for c in range(4)]


def neighbours():
    x, y = lax.axis_index("gx"), lax.axis_index("gy")
    nx, ny = lax.axis_size("gx"), lax.axis_size("gy")
    left, right = lax.rem(x + nx - 1, nx), lax.rem(x + 1, nx)
    down, up = lax.rem(y + ny - 1, ny), lax.rem(y + 1, ny)
    sides = [(left, y), (right, y), (x, down), (x, up)]
    corners = [(left, down), (left, up), (right, down), (right, up)]
    return sides + corners


def prep_kernel(
    leaving_in, shift_in, vel_in, pos_in, axis_in,
    border, own_axis, ids, inner_mean, found, vel, got_side, got_corner,
    leaving, shift, pos, axis, row_s, col_s, sums, run_s, prep_s, axis_s, side, corner,
    load_sem, send_sem, recv_sem,
):
    targets = neighbours()
    barrier = pltpu.get_barrier_semaphore()
    for target in targets:
        pl.semaphore_signal(barrier, inc=1, device_id=target, device_id_type=MESH)
    loads = [
        pltpu.make_async_copy(source, target, load_sem.at[k])
        for k, (source, target) in enumerate(
            ((pos_in, pos), (shift_in, shift), (axis_in, axis), (vel_in, vel), (leaving_in, leaving))
        )
    ]
    for load in loads:
        load.start()
    axis_s[...] = jnp.zeros(axis_s.shape, F32)
    for k in (0, 2):
        side[k, 112:144, :] = jnp.zeros((32, 128), F32)
    corner[:, 20:24, :] = jnp.zeros((4, 4, 128), F32)
    for load in loads:
        load.wait()

    low_x = (shift[0] == 1).astype(jnp.int32)
    low_y = (shift[1] == 1).astype(jnp.int32)
    shifts = [shift[k].astype(F32) * 0.25 for k in range(3)]
    cell_x = jnp.floor(pos[0] + shifts[0]) + low_x.astype(F32)
    cell_y = jnp.floor(pos[1] + shifts[1]) + low_y.astype(F32)
    cell_z = jnp.floor(pos[2] + shifts[2])
    cell_z = jnp.where(cell_z >= float(CZ), cell_z - float(CZ), cell_z)
    half = jnp.floor(cell_y * 0.5)
    is_left = cell_x < 2.0
    is_right = cell_x > 7.0
    bottom = cell_x + jnp.where(is_left, 0.0, jnp.where(is_right, 16.0, 24.0))
    middle = 3.0 * cell_x + half + jnp.where(is_left, 1.0, jnp.where(is_right, -7.0, 25.0))
    row = jnp.where(half < 1.0, bottom, jnp.where(half > 3.0, cell_x + 8.0, middle))
    col = (cell_y - 2.0 * half) * float(CZ) + cell_z
    row_s[...] = row
    col_s[...] = col
    ids[...] = row * 256.0 + col

    row_of = iota16((MAIN, 128), 0)
    col_of = iota16((256, 128), 0)
    rest = iota((16, 128), 0)
    rest_row = (MAIN + rest % 2).astype(F32).astype(BF16)
    rest_is = [rest // 2 == g for g in range(7)]
    for chunk in range(8):
        left_parts = [[] for _ in range(8)]
        right_parts = []
        for j in range(8):
            r = chunk * 8 + j
            values = [jnp.ones((1, 128), F32)]
            for c in range(3):
                high = high_part(vel[c, r : r + 1, :])
                values += [high, vel[c, r : r + 1, :] - high]
            hit = row_of == spread(row_s[r : r + 1, :], MAIN)
            tail = jnp.broadcast_to(values[0], (16, 128))
            for g in range(7):
                wide = spread(values[g], MAIN)
                left_parts[g].append(jnp.where(hit, wide, jnp.zeros((MAIN, 128), BF16)))
                if g:
                    tail = jnp.where(rest_is[g], jnp.broadcast_to(values[g], (16, 128)), tail)
            hit = rest_row == spread(row_s[r : r + 1, :], 16)
            left_parts[7].append(jnp.where(hit, tail.astype(BF16), jnp.zeros((16, 128), BF16)))
            right_parts.append(one_hot(col_of == spread(col_s[r : r + 1, :], 256)))
        part = dot_nt(
            jnp.concatenate([jnp.concatenate(p, 1) for p in left_parts], 0),
            jnp.concatenate(right_parts, 1),
        )
        if chunk == 0:
            sums[...] = part
        else:
            sums[...] += part
    for c in range(4):
        if c == 0:
            group = sums[0:BORDER, :]
        else:
            at = (2 * c - 1) * MAIN
            group = sums[at : at + BORDER, :] + sums[at + MAIN : at + MAIN + BORDER, :]
        for par in range(2):
            lanes = slice(par * 128, par * 128 + 128)
            border[pl.ds(2 * c + par, BORDER, stride=8), :] = group[:, lanes]
    for k, start in enumerate((0, 16, 24, 8)):
        if start == 24:
            side[k, 0:64, :] = border[192:256, :]
            side[k, 64:80, :] = border[0:16, :]
        else:
            side[k, 0:80, :] = border[8 * start : 8 * start + 80, :]
    for k, start in enumerate((0, 8, 24, 16)):
        corner[k, 0:16, :] = border[8 * start : 8 * start + 16, :]

    for cx in range(CXL):
        at = (cx + 1) * 11 + 1
        axis_s[at : at + 8, :] = axis[cx * 8 : cx * 8 + 8, :].astype(F32)
    for par in range(2):
        for first, n, cx, cx_step, half_y, half_step in PIECES:
            start = (cx + 1 - low_x) * 11 + 2 * half_y + par + 1 - low_y
            step = 11 * cx_step + 2 * half_step
            own_axis[par, first : first + n, :] = axis_s[pl.ds(start, n, stride=step), :]
        own_axis[par, 50:56, :] = jnp.zeros((6, 128), F32)
        base = 112 + 16 * par
        for k, order in ((0, ((8, 2), (2, 6), (0, 2))), (2, ((0, 2), (26, 6), (24, 2)))):
            at = base
            for first, n in order:
                side[k, at : at + n, :] = own_axis[par, first : first + n, :]
                at += n
        corner[0, 20 + 2 * par : 22 + 2 * par, :] = own_axis[par, 0:2, :]

    slot = iota((8, 128), 0) * 128 + iota((8, 128), 1)
    lane = iota((8, 128), 1)
    counts = [leaving[k] for k in range(4)]
    starts = [jnp.int32(0), counts[0], counts[0] + counts[1], counts[0] + counts[1] + counts[2]]

    def run(load, d):
        if d == 0:
            return load(0)
        q = starts[d] // 128
        r = starts[d] - q * 128
        back = jnp.where(r == 0, 0, 128 - r)
        here = pltpu.roll(load(q), back, 1)
        after = pltpu.roll(load(q + 1), back, 1)
        return jnp.where(lane < 128 - r, here, after)

    def moved(d, run_row):
        if d == 0:
            return run_row + jnp.where(run_row < 2.0, 24.0, jnp.where(run_row < 8.0, 16.0, 8.0))
        if d == 1:
            return run_row - jnp.where(run_row < 18.0, 8.0, jnp.where(run_row < 24.0, 16.0, 24.0))
        if d == 2:
            return run_row + jnp.where(run_row < 2.0, 8.0, jnp.where(run_row < 26.0, -8.0, -16.0))
        return run_row + jnp.where(run_row < 10.0, -8.0, jnp.where(run_row < 16.0, 16.0, 8.0))

    flags = []
    for d in range(4):
        live = slot < counts[d]
        values = [run(lambda q, c=c: vel[c, pl.ds(q, 8), :], d) for c in range(3)]
        run_row = run(lambda q: row_s[pl.ds(q, 8), :], d)
        run_col = run(lambda q: col_s[pl.ds(q, 8), :], d)
        kept = live
        if d < 2:
            y = run(lambda q: pos[1, pl.ds(q, 8), :], d)
            down = live & (y < 0.0)
            up = live & (y >= float(CYL))
            kept = live & (y >= 0.0) & (y < float(CYL))
            flags += [down, up]
            for c in range(3):
                high = high_part(values[c])
                run_s[d, 16 * c : 16 * c + 8, :] = high
                run_s[d, 16 * c + 8 : 16 * c + 16, :] = values[c] - high
            run_s[d, 48:56, :] = run_row
            run_s[d, 56:64, :] = run_col
            run_s[d, 64:72, :] = jnp.ones((8, 128), F32)
            run_s[d, 72:128, :] = jnp.zeros((56, 128), F32)
        for c in range(3):
            side[d, 80 + 8 * c : 88 + 8 * c, :] = values[c]
        side[d, 104:112, :] = jnp.where(kept, moved(d, run_row) * 256.0 + run_col, -1.0)

    flag = jnp.concatenate([f.astype(F32) for f in flags], 0)
    flag16 = flag.astype(BF16)
    before = (iota((128, 128), 0) < iota((128, 128), 1)).astype(F32).astype(BF16)
    inside = jnp.dot(flag16, before, preferred_element_type=F32)
    total = jnp.dot(flag16, jnp.ones((128, 128), BF16), preferred_element_type=F32)
    r0, r1 = iota((32, 32), 0), iota((32, 32), 1)
    earlier = ((r1 < r0) & (r0 // 8 == r1 // 8)).astype(F32).astype(BF16)
    offset = jnp.dot(earlier, total.astype(BF16), preferred_element_type=F32)
    prep_s[...] = jnp.where(flag > 0.0, inside + offset, -1.0)
    rank_of = iota16((128, 128), 0)
    for d in range(2):
        rows = jnp.concatenate([run_s[d, pl.ds(r, 16, stride=8), :] for r in range(8)], 1).astype(BF16)
        for s in range(2):
            at = d * 16 + s * 8
            hits = [one_hot(rank_of == spread(prep_s[at + r : at + r + 1, :], 128)) for r in range(8)]
            packed = dot_nt(rows, jnp.concatenate(hits, 1))
            k = d * 2 + s
            for c in range(3):
                corner[k, 16 + c : 17 + c, :] = packed[2 * c : 2 * c + 1] + packed[2 * c + 1 : 2 * c + 2]
            there = (packed[6:7] + (16.0 - 32.0 * d)) * 256.0 + packed[7:8]
            corner[k, 19:20, :] = jnp.where(packed[8:9] > 0.5, there, -1.0)

    pl.semaphore_wait(barrier, 8)
    copies = []
    for k in range(8):
        if k < 4:
            size = 144 if k in (0, 2) else 112
            source, target = side.at[k, pl.ds(0, size), :], got_side.at[k, pl.ds(0, size), :]
        else:
            source, target = corner.at[k - 4], got_corner.at[k - 4]
        copies.append(
            pltpu.make_async_remote_copy(
                src_ref=source,
                dst_ref=target,
                send_sem=send_sem.at[k],
                recv_sem=recv_sem.at[k],
                device_id=targets[k],
                device_id_type=MESH,
            )
        )
    for k in (4, 5, 6, 7, 0, 1, 2, 3):
        copies[k].start()

    def inner(group):
        at = group * MAIN + BORDER
        end = 7 * MAIN + 2 * group
        return jnp.concatenate([sums[at : at + 16, :], sums[end : end + 2, :], jnp.zeros((6, 256), F32)], 0)

    most = jnp.maximum(inner(0), 1.0)
    high_rows, low_rows = [], []
    for c in range(3):
        mean = (inner(1 + 2 * c) + inner(2 + 2 * c)) / most
        inner_mean[c] = mean
        high = high_part(mean)
        high_rows.append(high)
        low_rows.append(mean - high)
    high_rows.append(jnp.concatenate([own_axis[0, BORDER:56, :], own_axis[1, BORDER:56, :]], 1))
    table = jnp.concatenate(high_rows + low_rows, 0).astype(BF16)
    for b in range(1, 8):
        at = slice(8 * b, 8 * b + 8)
        looked = look_up_block(table, 24, col_s[at, :], row_s[at, :] - float(BORDER))
        for c in range(4):
            found[c, at, :] = looked[c]
    gone = starts[3] + counts[3]
    place = iota((ROWS, 128), 0) * 128 + iota((ROWS, 128), 1)
    ids[...] = jnp.where(place >= gone, ids[...], -1.0)
    for copy in copies:
        copy.wait()


def collide_kernel(
    shift_in, border, own_axis, ids, inner_mean, found, vel, got_side, got_corner,
    out_hbm, flow_hbm,
    shift, out, flow, total, means, load_sem, store_sem,
):
    load = pltpu.make_async_copy(shift_in, shift, load_sem)
    load.start()
    for first, n, parts in (
        (0, 2, ((1, 8), (3, 0), (None, 3))),
        (2, 6, ((1, 2),)),
        (8, 2, ((1, 0), (2, 8), (None, 2))),
        (10, 6, ((2, 2),)),
        (16, 2, ((0, 8), (2, 0), (None, 0))),
        (18, 6, ((0, 2),)),
        (24, 2, ((0, 0), (3, 8), (None, 1))),
        (26, 6, ((3, 2),)),
    ):
        value = border[8 * first : 8 * (first + n), :]
        for k, at in parts:
            if k is None:
                value = value + got_corner[at, 0:16, :]
            else:
                value = value + got_side[k, 8 * at : 8 * (at + n), :]
        total[8 * first : 8 * (first + n), :] = value
    numbers = []
    for par in range(2):
        number = own_axis[par, 0:BORDER, :]
        at = 112 + 16 * par
        gap = jnp.zeros((16, 128), F32)
        number = number + jnp.concatenate([gap, got_side[0, at : at + 16, :]], 0)
        number = number + jnp.concatenate([gap[0:8], got_side[2, at : at + 16, :], gap[0:8]], 0)
        pair = got_corner[0, 20 + 2 * par : 22 + 2 * par, :]
        number = number + jnp.concatenate([gap, pair, gap[0:14]], 0)
        numbers.append(number)
    groups = [None] * 7
    most = [jnp.maximum(total[pl.ds(par, BORDER, stride=8), :], 1.0) for par in range(2)]
    border_mean = []
    for c in range(3):
        halves = [total[pl.ds(2 + 2 * c + par, BORDER, stride=8), :] / most[par] for par in range(2)]
        mean = jnp.concatenate(halves, 1)
        border_mean.append(mean)
        groups[c] = high_part(mean)
        groups[4 + c] = mean - groups[c]
    groups[3] = jnp.concatenate(numbers, 1)
    table = jnp.concatenate(groups, 0).astype(BF16)
    choices = axis_table()

    def turn(at, live, v, looked):
        mean = looked[:3]
        number = looked[3].astype(jnp.int32)
        bits = [(number & (1 << k)) != 0 for k in range(4)]
        a = []
        for c in range(3):
            level = [entry[c] for entry in choices]
            for k in range(4):
                level = [jnp.where(bits[k], level[2 * m + 1], level[2 * m]) for m in range(len(level) // 2)]
            a.append(level[0])
        w = [v[c] - mean[c] for c in range(3)]
        cross = [
            a[1] * w[2] - a[2] * w[1],
            a[2] * w[0] - a[0] * w[2],
            a[0] * w[1] - a[1] * w[0],
        ]
        along = (a[0] * w[0] + a[1] * w[1] + a[2] * w[2]) * (1.0 - COS_TURN)
        for c in range(3):
            turned = mean[c] + COS_TURN * w[c] + SIN_TURN * cross[c] + along * a[c]
            out[c, at, :] = jnp.where(live, turned, 0.0)

    slot = iota((8, 128), 0) * 128 + iota((8, 128), 1)
    arrived = []
    for k in (1, 0, 3, 2):
        v = [got_side[k, 80 + 8 * c : 88 + 8 * c, :] for c in range(4)]
        if k > 1:
            first, second = ((2, 0), (3, 1))[k - 2]
            n0 = jnp.sum((v[3] >= 0.0).astype(jnp.int32))
            n1 = jnp.sum((got_corner[first, 19:20, :] >= 0.0).astype(jnp.int32))
            in_first = (slot >= n0) & (slot < n0 + n1)
            in_second = (slot >= n0 + n1) & (slot < n0 + n1 + 128)
            by1, by2 = lax.rem(n0, 128), lax.rem(n0 + n1, 128)
            for c in range(4):
                at = slice(16 + c, 17 + c)
                one = pltpu.roll(jnp.broadcast_to(got_corner[first, at, :], (8, 128)), by1, 1)
                two = pltpu.roll(jnp.broadcast_to(got_corner[second, at, :], (8, 128)), by2, 1)
                v[c] = jnp.where(in_first, one, jnp.where(in_second, two, v[c]))
        arrived.append(v)

    stores = []

    def store(source, target):
        copy = pltpu.make_async_copy(source, target, store_sem.at[len(stores)])
        copy.start()
        stores.append(copy)

    for v, at, window in zip(arrived, (64, 72, 80, 88), (0, 16, 24, 8)):
        rows = jnp.floor(v[3] * (1.0 / 256.0))
        cols = v[3] - rows * 256.0
        if window == 24:
            part = [jnp.concatenate([g[24:32], g[0:8]], 0) for g in groups]
            local = jnp.where(rows < 2.0, rows + 8.0, rows - 24.0)
        else:
            part = [g[window : window + 16] for g in groups]
            local = rows - float(window)
        looked = look_up_block(jnp.concatenate(part, 0).astype(BF16), 16, cols, local)
        turn(slice(at, at + 8), v[3] >= 0.0, v, looked)

    out[:, 0:8, :] = jnp.zeros((3, 8, 128), F32)
    for b in range(1, 8):
        at = slice(8 * b, 8 * b + 8)
        block = ids[at, :]
        rows = jnp.floor(block * (1.0 / 256.0))
        looked = look_up_block(table, BORDER, block - rows * 256.0, rows)
        turn(at, block >= 0.0, [vel[c, at, :] for c in range(3)], [looked[c] + found[c, at, :] for c in range(4)])
    store(out, out_hbm)

    for c in range(3):
        for par in range(2):
            lanes = slice(par * 128, par * 128 + 128)
            for first, n, cx, cx_step, half_y, half_step in PIECES:
                if first < BORDER:
                    piece = border_mean[c][first : first + n, lanes]
                else:
                    piece = inner_mean[c, first - BORDER : first - BORDER + n, lanes]
                start = cx * 10 + 2 * half_y + par
                means[c, pl.ds(start, n, stride=10 * cx_step + 2 * half_step), :] = piece
    load.wait()
    low_x = (shift[0] == 1).astype(jnp.int32)
    low_y = (shift[1] == 1).astype(jnp.int32)
    for c in range(3):
        for cx in range(CXL):
            flow[c, cx * 8 : cx * 8 + 8, :] = means[c, pl.ds((cx + low_x) * 10 + low_y, 8), :]
    store(flow, flow_hbm)
    for copy in stores:
        copy.wait()


def shape(*dims):
    return jax.ShapeDtypeStruct(dims, F32)


def per_device(velocity, position, leaving, grid_shift, axis_index):
    vel = velocity.reshape(3, ROWS, 128)
    pos = position.reshape(3, ROWS, 128)
    axis = axis_index.reshape(64, 128)
    leaving = leaving.reshape(4)
    vel, pos, axis, leaving, grid_shift = [
        pltpu.with_memory_space_constraint(v, pltpu.HBM) for v in (vel, pos, axis, leaving, grid_shift)
    ]
    vmem = pl.BlockSpec(memory_space=pltpu.VMEM)
    hbm = pl.BlockSpec(memory_space=pltpu.HBM)
    parts = pl.pallas_call(
        prep_kernel,
        name="prep",
        out_shape=(
            shape(8 * BORDER + 8, 128),
            shape(2, 56, 128),
            shape(ROWS, 128),
            shape(3, 24, 256),
            shape(4, ROWS, 128),
            shape(3, ROWS, 128),
            shape(4, 144, 128),
            shape(4, 24, 128),
        ),
        in_specs=[hbm] * 5,
        out_specs=(vmem,) * 8,
        scratch_shapes=[
            pltpu.SMEM((4,), jnp.int32),
            pltpu.SMEM((3,), jnp.int32),
            pltpu.VMEM((3, ROWS, 128), F32),
            pltpu.VMEM((64, 128), jnp.int32),
            pltpu.VMEM((ROWS, 128), F32),
            pltpu.VMEM((ROWS, 128), F32),
            pltpu.VMEM((7 * MAIN + 16, 256), F32),
            pltpu.VMEM((2, 136, 128), F32),
            pltpu.VMEM((32, 128), F32),
            pltpu.VMEM((144, 128), F32),
            pltpu.VMEM((4, 144, 128), F32),
            pltpu.VMEM((4, 24, 128), F32),
            pltpu.SemaphoreType.DMA((5,)),
            pltpu.SemaphoreType.DMA((8,)),
            pltpu.SemaphoreType.DMA((8,)),
        ],
        compiler_params=pltpu.CompilerParams(
            collective_id=0, has_side_effects=True, vmem_limit_bytes=32 << 20
        ),
    )(leaving, grid_shift, vel, pos, axis)
    out, flow = pl.pallas_call(
        collide_kernel,
        name="collide",
        out_shape=(shape(3, SLOTS, 128), shape(3, 64, 128)),
        in_specs=[hbm] + [vmem] * 8,
        out_specs=(hbm, hbm),
        scratch_shapes=[
            pltpu.SMEM((3,), jnp.int32),
            pltpu.VMEM((3, SLOTS, 128), F32),
            pltpu.VMEM((3, 64, 128), F32),
            pltpu.VMEM((8 * BORDER + 8, 128), F32),
            pltpu.VMEM((3, 112, 128), F32),
            pltpu.SemaphoreType.DMA,
            pltpu.SemaphoreType.DMA((3,)),
        ],
        compiler_params=pltpu.CompilerParams(vmem_limit_bytes=32 << 20),
    )(grid_shift, *parts)
    return out.reshape(3, 1, 1, SLOTS * 128), flow.reshape(3, 1, 1, 64 * 128)


def solution(mesh):
    return jax.shard_map(
        per_device,
        mesh=mesh,
        in_specs=(
            P(None, "gx", "gy", None),
            P(None, "gx", "gy", None),
            P("gx", "gy", None),
            P(),
            P("gx", "gy", None),
        ),
        out_specs=(P(None, "gx", "gy", None), P(None, "gx", "gy", None)),
        check_vma=False,
    )
```

```python
import math

import jax
import jax.numpy as jnp
from jax import lax
from jax.experimental import pallas as pl
from jax.experimental.pallas import tpu as pltpu
from jax.sharding import PartitionSpec as P

CXL = 8
CYL = 8
CZ = 128
NAX = 16
ROWS = 64
SLOTS = 96
BORDER = 32
INNER = 18
MAIN = 48

COS_TURN = -0.6427876096865393
SIN_TURN = 0.766044443118978
GOLDEN_TURN = 2.399963229728653

F32 = jnp.float32
BF16 = jnp.bfloat16
MESH = pl.DeviceIdType.MESH


def axis_table():
    table = []
    for number in range(NAX):
        height = 1.0 - (2.0 * number + 1.0) / NAX
        radius = math.sqrt(1.0 - height * height)
        phase = number * GOLDEN_TURN
        table.append((radius * math.cos(phase), radius * math.sin(phase), height))
    return table


def dot_nt(a, b):
    return lax.dot_general(a, b, (((1,), (1,)), ((), ())), preferred_element_type=F32)


def iota(shape, dim):
    return lax.broadcasted_iota(jnp.int32, shape, dim)


def iota16(shape, dim):
    return iota(shape, dim).astype(F32).astype(BF16)


def spread(row, height):
    return jnp.broadcast_to(row, (height, 128)).astype(BF16)


def one_hot(hit):
    return jnp.where(hit, jnp.ones(hit.shape, BF16), jnp.zeros(hit.shape, BF16))


def high_part(value):
    return value.astype(BF16).astype(F32)


PIECES = (
    [(0, 2, 0, 1, 0, 0), (8, 2, 0, 1, 4, 0), (16, 2, 8, 1, 4, 0), (24, 2, 8, 1, 0, 0)]
    + [(10, 6, 2, 1, 4, 0), (26, 6, 2, 1, 0, 0)]
    + [(2 + 3 * u, 3, u, 0, 1, 1) for u in range(2)]
    + [(18 + 3 * u, 3, 8 + u, 0, 1, 1) for u in range(2)]
    + [(32 + 3 * w, 3, 2 + w, 0, 1, 1) for w in range(6)]
)


def look_up(table, heights, groups, cols, local, j):
    col_of = iota16((256, 128), 0)
    row_of = iota((heights, 128), 0).astype(F32)
    hits = [one_hot(col_of == spread(cols[i : i + 1, :], 256)) for i in (j, j + 1)]
    both = jnp.dot(table, jnp.concatenate(hits, 1), preferred_element_type=F32)
    found = []
    for i in (0, 1):
        lanes = slice(i * 128, i * 128 + 128)
        hit = row_of == jnp.broadcast_to(local[j + i : j + i + 1, :], (heights, 128))
        row = []
        for c in range(4):
            part = both[heights * c : heights * (c + 1), lanes]
            if c < 3:
                part = part + both[heights * (4 + c) : heights * (5 + c), lanes]
            row.append(jnp.sum(jnp.where(hit, part, 0.0), axis=0, keepdims=True))
        found.append(row)
    return found


def look_up_block(table, heights, cols, local):
    found = []
    for j in range(0, 8, 2):
        found += look_up(table, heights, 7, cols, local, j)
    return [jnp.concatenate([row[c] for row in found], 0) for c in range(4)]


def neighbours():
    x, y = lax.axis_index("gx"), lax.axis_index("gy")
    nx, ny = lax.axis_size("gx"), lax.axis_size("gy")
    left, right = lax.rem(x + nx - 1, nx), lax.rem(x + 1, nx)
    down, up = lax.rem(y + ny - 1, ny), lax.rem(y + 1, ny)
    sides = [(left, y), (right, y), (x, down), (x, up)]
    corners = [(left, down), (left, up), (right, down), (right, up)]
    return sides + corners


def prep_kernel(
    leaving_in, shift_in, vel_in, pos_in, axis_in,
    border, own_axis, ids, inner_mean, found, vel, got_side, got_corner,
    leaving, shift, pos, axis, row_s, col_s, sums, run_s, prep_s, axis_s, side, corner,
    load_sem, send_sem, recv_sem,
):
    loads = [
        pltpu.make_async_copy(source, target, load_sem.at[k])
        for k, (source, target) in enumerate(
            ((pos_in, pos), (shift_in, shift), (axis_in, axis), (vel_in, vel), (leaving_in, leaving))
        )
    ]
    for load in loads:
        load.start()
    targets = neighbours()
    barrier = pltpu.get_barrier_semaphore()
    for target in targets:
        pl.semaphore_signal(barrier, inc=1, device_id=target, device_id_type=MESH)
    axis_s[...] = jnp.zeros(axis_s.shape, F32)
    side[:, 112:144, :] = jnp.zeros((4, 32, 128), F32)
    for load in loads:
        load.wait()

    low_x = (shift[0] == 1).astype(jnp.int32)
    low_y = (shift[1] == 1).astype(jnp.int32)
    shifts = [shift[k].astype(F32) * 0.25 for k in range(3)]
    cell_x = jnp.floor(pos[0] + shifts[0]) + low_x.astype(F32)
    cell_y = jnp.floor(pos[1] + shifts[1]) + low_y.astype(F32)
    cell_z = jnp.floor(pos[2] + shifts[2])
    cell_z = jnp.where(cell_z >= float(CZ), cell_z - float(CZ), cell_z)
    half = jnp.floor(cell_y * 0.5)
    is_left = cell_x < 2.0
    is_right = cell_x > 7.0
    bottom = cell_x + jnp.where(is_left, 0.0, jnp.where(is_right, 16.0, 24.0))
    middle = 3.0 * cell_x + half + jnp.where(is_left, 1.0, jnp.where(is_right, -7.0, 25.0))
    row = jnp.where(half < 1.0, bottom, jnp.where(half > 3.0, cell_x + 8.0, middle))
    col = (cell_y - 2.0 * half) * float(CZ) + cell_z
    row_s[...] = row
    col_s[...] = col
    ids[...] = row * 256.0 + col

    row_of = iota16((MAIN, 128), 0)
    col_of = iota16((256, 128), 0)
    rest = iota((16, 128), 0)
    rest_row = (MAIN + rest % 2).astype(F32).astype(BF16)
    rest_is = [rest // 2 == g for g in range(7)]
    for chunk in range(8):
        left_parts = [[] for _ in range(8)]
        right_parts = []
        for j in range(8):
            r = chunk * 8 + j
            values = [jnp.ones((1, 128), F32)]
            for c in range(3):
                high = high_part(vel[c, r : r + 1, :])
                values += [high, vel[c, r : r + 1, :] - high]
            hit = row_of == spread(row_s[r : r + 1, :], MAIN)
            tail = jnp.broadcast_to(values[0], (16, 128))
            for g in range(7):
                wide = spread(values[g], MAIN)
                left_parts[g].append(jnp.where(hit, wide, jnp.zeros((MAIN, 128), BF16)))
                if g:
                    tail = jnp.where(rest_is[g], jnp.broadcast_to(values[g], (16, 128)), tail)
            hit = rest_row == spread(row_s[r : r + 1, :], 16)
            left_parts[7].append(jnp.where(hit, tail.astype(BF16), jnp.zeros((16, 128), BF16)))
            right_parts.append(one_hot(col_of == spread(col_s[r : r + 1, :], 256)))
        part = dot_nt(
            jnp.concatenate([jnp.concatenate(p, 1) for p in left_parts], 0),
            jnp.concatenate(right_parts, 1),
        )
        if chunk == 0:
            sums[...] = part
        else:
            sums[...] += part
    for c in range(4):
        if c == 0:
            group = sums[0:BORDER, :]
        else:
            at = (2 * c - 1) * MAIN
            group = sums[at : at + BORDER, :] + sums[at + MAIN : at + MAIN + BORDER, :]
        for par in range(2):
            lanes = slice(par * 128, par * 128 + 128)
            border[pl.ds(2 * c + par, BORDER, stride=8), :] = group[:, lanes]
    for k, start in enumerate((0, 16, 24, 8)):
        if start == 24:
            side[k, 0:64, :] = border[192:256, :]
            side[k, 64:80, :] = border[0:16, :]
        else:
            side[k, 0:80, :] = border[8 * start : 8 * start + 80, :]
    for k, start in enumerate((0, 8, 24, 16)):
        corner[k, 0:16, :] = border[8 * start : 8 * start + 16, :]

    for cx in range(CXL):
        at = (cx + 1) * 11 + 1
        axis_s[at : at + 8, :] = axis[cx * 8 : cx * 8 + 8, :].astype(F32)
    for par in range(2):
        for first, n, cx, cx_step, half_y, half_step in PIECES:
            start = (cx + 1 - low_x) * 11 + 2 * half_y + par + 1 - low_y
            step = 11 * cx_step + 2 * half_step
            own_axis[par, first : first + n, :] = axis_s[pl.ds(start, n, stride=step), :]
        own_axis[par, 50:56, :] = jnp.zeros((6, 128), F32)
        base = 112 + 16 * par
        for k, order in enumerate(
            (((8, 2), (2, 6), (0, 2)), ((24, 2), (18, 6), (16, 2)), ((0, 2), (26, 6), (24, 2)), ((16, 2), (10, 6), (8, 2)))
        ):
            at = base
            for first, n in order:
                side[k, at : at + n, :] = own_axis[par, first : first + n, :]
                at += n
        for k, first in enumerate((0, 8, 24, 16)):
            corner[k, 20 + 2 * par : 22 + 2 * par, :] = own_axis[par, first : first + 2, :]

    slot = iota((8, 128), 0) * 128 + iota((8, 128), 1)
    lane = iota((8, 128), 1)
    counts = [leaving[k] for k in range(4)]
    starts = [jnp.int32(0), counts[0], counts[0] + counts[1], counts[0] + counts[1] + counts[2]]

    def run(load, d):
        if d == 0:
            return load(0)
        q = starts[d] // 128
        r = starts[d] - q * 128
        back = jnp.where(r == 0, 0, 128 - r)
        here = pltpu.roll(load(q), back, 1)
        after = pltpu.roll(load(q + 1), back, 1)
        return jnp.where(lane < 128 - r, here, after)

    def moved(d, run_row):
        if d == 0:
            return run_row + jnp.where(run_row < 2.0, 24.0, jnp.where(run_row < 8.0, 16.0, 8.0))
        if d == 1:
            return run_row - jnp.where(run_row < 18.0, 8.0, jnp.where(run_row < 24.0, 16.0, 24.0))
        if d == 2:
            return run_row + jnp.where(run_row < 2.0, 8.0, jnp.where(run_row < 26.0, -8.0, -16.0))
        return run_row + jnp.where(run_row < 10.0, -8.0, jnp.where(run_row < 16.0, 16.0, 8.0))

    flags = []
    for d in range(4):
        live = slot < counts[d]
        values = [run(lambda q, c=c: vel[c, pl.ds(q, 8), :], d) for c in range(3)]
        run_row = run(lambda q: row_s[pl.ds(q, 8), :], d)
        run_col = run(lambda q: col_s[pl.ds(q, 8), :], d)
        kept = live
        if d < 2:
            y = run(lambda q: pos[1, pl.ds(q, 8), :], d)
            down = live & (y < 0.0)
            up = live & (y >= float(CYL))
            kept = live & (y >= 0.0) & (y < float(CYL))
            flags += [down, up]
            for c in range(3):
                high = high_part(values[c])
                run_s[d, 16 * c : 16 * c + 8, :] = high
                run_s[d, 16 * c + 8 : 16 * c + 16, :] = values[c] - high
            run_s[d, 48:56, :] = run_row
            run_s[d, 56:64, :] = run_col
            run_s[d, 64:72, :] = jnp.ones((8, 128), F32)
            run_s[d, 72:128, :] = jnp.zeros((56, 128), F32)
        for c in range(3):
            side[d, 80 + 8 * c : 88 + 8 * c, :] = values[c]
        side[d, 104:112, :] = jnp.where(kept, moved(d, run_row) * 256.0 + run_col, -1.0)

    flag = jnp.concatenate([f.astype(F32) for f in flags], 0)
    flag16 = flag.astype(BF16)
    before = (iota((128, 128), 0) < iota((128, 128), 1)).astype(F32).astype(BF16)
    inside = jnp.dot(flag16, before, preferred_element_type=F32)
    total = jnp.dot(flag16, jnp.ones((128, 128), BF16), preferred_element_type=F32)
    r0, r1 = iota((32, 32), 0), iota((32, 32), 1)
    earlier = ((r1 < r0) & (r0 // 8 == r1 // 8)).astype(F32).astype(BF16)
    offset = jnp.dot(earlier, total.astype(BF16), preferred_element_type=F32)
    prep_s[...] = jnp.where(flag > 0.0, inside + offset, -1.0)
    rank_of = iota16((128, 128), 0)
    for d in range(2):
        rows = jnp.concatenate([run_s[d, pl.ds(r, 16, stride=8), :] for r in range(8)], 1).astype(BF16)
        for s in range(2):
            at = d * 16 + s * 8
            hits = [one_hot(rank_of == spread(prep_s[at + r : at + r + 1, :], 128)) for r in range(8)]
            packed = dot_nt(rows, jnp.concatenate(hits, 1))
            k = d * 2 + s
            for c in range(3):
                corner[k, 16 + c : 17 + c, :] = packed[2 * c : 2 * c + 1] + packed[2 * c + 1 : 2 * c + 2]
            there = (packed[6:7] + (16.0 - 32.0 * d)) * 256.0 + packed[7:8]
            corner[k, 19:20, :] = jnp.where(packed[8:9] > 0.5, there, -1.0)

    pl.semaphore_wait(barrier, 8)
    copies = []
    for k in (4, 5, 6, 7, 0, 1, 2, 3):
        source, target = (side.at[k], got_side.at[k]) if k < 4 else (corner.at[k - 4], got_corner.at[k - 4])
        copy = pltpu.make_async_remote_copy(
            src_ref=source,
            dst_ref=target,
            send_sem=send_sem.at[k],
            recv_sem=recv_sem.at[k],
            device_id=targets[k],
            device_id_type=MESH,
        )
        copy.start()
        copies.append(copy)

    def inner(group):
        at = group * MAIN + BORDER
        end = 7 * MAIN + 2 * group
        return jnp.concatenate([sums[at : at + 16, :], sums[end : end + 2, :], jnp.zeros((6, 256), F32)], 0)

    most = jnp.maximum(inner(0), 1.0)
    high_rows, low_rows = [], []
    for c in range(3):
        mean = (inner(1 + 2 * c) + inner(2 + 2 * c)) / most
        inner_mean[c] = mean
        high = high_part(mean)
        high_rows.append(high)
        low_rows.append(mean - high)
    high_rows.append(jnp.concatenate([own_axis[0, BORDER:56, :], own_axis[1, BORDER:56, :]], 1))
    table = jnp.concatenate(high_rows + low_rows, 0).astype(BF16)
    for b in range(1, 8):
        at = slice(8 * b, 8 * b + 8)
        looked = look_up_block(table, 24, col_s[at, :], row_s[at, :] - float(BORDER))
        for c in range(4):
            found[c, at, :] = looked[c]
    gone = starts[3] + counts[3]
    place = iota((ROWS, 128), 0) * 128 + iota((ROWS, 128), 1)
    ids[...] = jnp.where(place >= gone, ids[...], -1.0)
    for copy in copies:
        copy.wait()


def collide_kernel(
    shift_in, border, own_axis, ids, inner_mean, found, vel, got_side, got_corner,
    out_hbm, flow_hbm,
    shift, out, flow, total, means, load_sem, store_sem,
):
    load = pltpu.make_async_copy(shift_in, shift, load_sem)
    load.start()
    total[0 : 8 * BORDER, :] = border[0 : 8 * BORDER, :]
    for k, places in enumerate(
        (
            ((24, 0, 2), (18, 2, 6), (16, 8, 2)),
            ((8, 0, 2), (2, 2, 6), (0, 8, 2)),
            ((16, 0, 2), (10, 2, 6), (8, 8, 2)),
            ((0, 0, 2), (26, 2, 6), (24, 8, 2)),
        )
    ):
        for mine, theirs, n in places:
            total[8 * mine : 8 * (mine + n), :] += got_side[k, 8 * theirs : 8 * (theirs + n), :]
    for k, mine in enumerate((16, 24, 8, 0)):
        total[8 * mine : 8 * mine + 16, :] += got_corner[k, 0:16, :]
    numbers = []
    for par in range(2):
        number = own_axis[par, 0:BORDER, :]
        at = 112 + 16 * par
        zero = jnp.zeros((16, 128), F32)
        for k, (before, after) in enumerate(((16, 0), (0, 16), (8, 8))):
            strip = got_side[k, at : at + 16, :]
            parts = [jnp.zeros((before, 128), F32)] * (before > 0) + [strip]
            parts += [jnp.zeros((after, 128), F32)] * (after > 0)
            number = number + jnp.concatenate(parts, 0)
        strip = got_side[3, at : at + 16, :]
        number = number + jnp.concatenate([strip[8:16], zero, strip[0:8]], 0)
        pair = [got_corner[k, 20 + 2 * par : 22 + 2 * par, :] for k in range(4)]
        gap = jnp.zeros((6, 128), F32)
        number = number + jnp.concatenate([pair[3], gap, pair[2], gap, pair[0], gap, pair[1], gap], 0)
        numbers.append(number)
    groups = [None] * 7
    most = [jnp.maximum(total[pl.ds(par, BORDER, stride=8), :], 1.0) for par in range(2)]
    border_mean = []
    for c in range(3):
        halves = [total[pl.ds(2 + 2 * c + par, BORDER, stride=8), :] / most[par] for par in range(2)]
        mean = jnp.concatenate(halves, 1)
        border_mean.append(mean)
        groups[c] = high_part(mean)
        groups[4 + c] = mean - groups[c]
    groups[3] = jnp.concatenate(numbers, 1)
    table = jnp.concatenate(groups, 0).astype(BF16)
    choices = axis_table()

    def turn(at, live, v, looked):
        mean = looked[:3]
        number = looked[3].astype(jnp.int32)
        bits = [(number & (1 << k)) != 0 for k in range(4)]
        a = []
        for c in range(2):
            level = [entry[c] for entry in choices]
            for k in range(4):
                level = [jnp.where(bits[k], level[2 * m + 1], level[2 * m]) for m in range(len(level) // 2)]
            a.append(level[0])
        a.append((1.0 - 1.0 / NAX) - (2.0 / NAX) * looked[3])
        w = [v[c] - mean[c] for c in range(3)]
        cross = [
            a[1] * w[2] - a[2] * w[1],
            a[2] * w[0] - a[0] * w[2],
            a[0] * w[1] - a[1] * w[0],
        ]
        along = (a[0] * w[0] + a[1] * w[1] + a[2] * w[2]) * (1.0 - COS_TURN)
        for c in range(3):
            turned = mean[c] + COS_TURN * w[c] + SIN_TURN * cross[c] + along * a[c]
            out[c, at, :] = jnp.where(live, turned, 0.0)

    slot = iota((8, 128), 0) * 128 + iota((8, 128), 1)
    arrived = []
    for k in (1, 0, 3, 2):
        v = [got_side[k, 80 + 8 * c : 88 + 8 * c, :] for c in range(4)]
        if k > 1:
            first, second = ((2, 0), (3, 1))[k - 2]
            n0 = jnp.sum((v[3] >= 0.0).astype(jnp.int32))
            n1 = jnp.sum((got_corner[first, 19:20, :] >= 0.0).astype(jnp.int32))
            in_first = (slot >= n0) & (slot < n0 + n1)
            in_second = (slot >= n0 + n1) & (slot < n0 + n1 + 128)
            by1, by2 = lax.rem(n0, 128), lax.rem(n0 + n1, 128)
            for c in range(4):
                at = slice(16 + c, 17 + c)
                one = pltpu.roll(jnp.broadcast_to(got_corner[first, at, :], (8, 128)), by1, 1)
                two = pltpu.roll(jnp.broadcast_to(got_corner[second, at, :], (8, 128)), by2, 1)
                v[c] = jnp.where(in_first, one, jnp.where(in_second, two, v[c]))
        arrived.append(v)

    out[:, 0:8, :] = jnp.zeros((3, 8, 128), F32)
    for b in range(1, 8):
        at = slice(8 * b, 8 * b + 8)
        block = ids[at, :]
        rows = jnp.floor(block * (1.0 / 256.0))
        looked = look_up_block(table, BORDER, block - rows * 256.0, rows)
        turn(at, block >= 0.0, [vel[c, at, :] for c in range(3)], [looked[c] + found[c, at, :] for c in range(4)])
    stores = []

    def store(source, target):
        copy = pltpu.make_async_copy(source, target, store_sem.at[len(stores)])
        copy.start()
        stores.append(copy)

    for v, at, window in zip(arrived, (64, 72, 80, 88), (0, 16, 24, 8)):
        rows = jnp.floor(v[3] * (1.0 / 256.0))
        cols = v[3] - rows * 256.0
        if window == 24:
            part = [jnp.concatenate([g[24:32], g[0:8]], 0) for g in groups]
            local = jnp.where(rows < 2.0, rows + 8.0, rows - 24.0)
        else:
            part = [g[window : window + 16] for g in groups]
            local = rows - float(window)
        looked = look_up_block(jnp.concatenate(part, 0).astype(BF16), 16, cols, local)
        turn(slice(at, at + 8), v[3] >= 0.0, v, looked)
    store(out, out_hbm)

    for c in range(3):
        for par in range(2):
            lanes = slice(par * 128, par * 128 + 128)
            for first, n, cx, cx_step, half_y, half_step in PIECES:
                if first < BORDER:
                    piece = border_mean[c][first : first + n, lanes]
                else:
                    piece = inner_mean[c, first - BORDER : first - BORDER + n, lanes]
                start = cx * 10 + 2 * half_y + par
                means[c, pl.ds(start, n, stride=10 * cx_step + 2 * half_step), :] = piece
    load.wait()
    low_x = (shift[0] == 1).astype(jnp.int32)
    low_y = (shift[1] == 1).astype(jnp.int32)
    for c in range(3):
        for cx in range(CXL):
            flow[c, cx * 8 : cx * 8 + 8, :] = means[c, pl.ds((cx + low_x) * 10 + low_y, 8), :]
    store(flow, flow_hbm)
    for copy in stores:
        copy.wait()


def shape(*dims):
    return jax.ShapeDtypeStruct(dims, F32)


def per_device(velocity, position, leaving, grid_shift, axis_index):
    vel = velocity.reshape(3, ROWS, 128)
    pos = position.reshape(3, ROWS, 128)
    axis = axis_index.reshape(64, 128)
    leaving = leaving.reshape(4)
    vel, pos, axis, leaving, grid_shift = [
        pltpu.with_memory_space_constraint(v, pltpu.HBM) for v in (vel, pos, axis, leaving, grid_shift)
    ]
    vmem = pl.BlockSpec(memory_space=pltpu.VMEM)
    hbm = pl.BlockSpec(memory_space=pltpu.HBM)
    parts = pl.pallas_call(
        prep_kernel,
        name="prep",
        out_shape=(
            shape(8 * BORDER + 8, 128),
            shape(2, 56, 128),
            shape(ROWS, 128),
            shape(3, 24, 256),
            shape(4, ROWS, 128),
            shape(3, ROWS, 128),
            shape(4, 144, 128),
            shape(4, 24, 128),
        ),
        in_specs=[hbm] * 5,
        out_specs=(vmem,) * 8,
        scratch_shapes=[
            pltpu.SMEM((4,), jnp.int32),
            pltpu.SMEM((3,), jnp.int32),
            pltpu.VMEM((3, ROWS, 128), F32),
            pltpu.VMEM((64, 128), jnp.int32),
            pltpu.VMEM((ROWS, 128), F32),
            pltpu.VMEM((ROWS, 128), F32),
            pltpu.VMEM((7 * MAIN + 16, 256), F32),
            pltpu.VMEM((2, 136, 128), F32),
            pltpu.VMEM((32, 128), F32),
            pltpu.VMEM((144, 128), F32),
            pltpu.VMEM((4, 144, 128), F32),
            pltpu.VMEM((4, 24, 128), F32),
            pltpu.SemaphoreType.DMA((5,)),
            pltpu.SemaphoreType.DMA((8,)),
            pltpu.SemaphoreType.DMA((8,)),
        ],
        compiler_params=pltpu.CompilerParams(
            collective_id=0, has_side_effects=True, vmem_limit_bytes=32 << 20
        ),
    )(leaving, grid_shift, vel, pos, axis)
    out, flow = pl.pallas_call(
        collide_kernel,
        name="collide",
        out_shape=(shape(3, SLOTS, 128), shape(3, 64, 128)),
        in_specs=[hbm] + [vmem] * 8,
        out_specs=(hbm, hbm),
        scratch_shapes=[
            pltpu.SMEM((3,), jnp.int32),
            pltpu.VMEM((3, SLOTS, 128), F32),
            pltpu.VMEM((3, 64, 128), F32),
            pltpu.VMEM((8 * BORDER + 8, 128), F32),
            pltpu.VMEM((3, 112, 128), F32),
            pltpu.SemaphoreType.DMA,
            pltpu.SemaphoreType.DMA((3,)),
        ],
        compiler_params=pltpu.CompilerParams(vmem_limit_bytes=32 << 20),
    )(grid_shift, *parts)
    return out.reshape(3, 1, 1, SLOTS * 128), flow.reshape(3, 1, 1, 64 * 128)


def solution(mesh):
    return jax.shard_map(
        per_device,
        mesh=mesh,
        in_specs=(
            P(None, "gx", "gy", None),
            P(None, "gx", "gy", None),
            P("gx", "gy", None),
            P(),
            P("gx", "gy", None),
        ),
        out_specs=(P(None, "gx", "gy", None), P(None, "gx", "gy", None)),
        check_vma=False,
    )
```

```python
import math

import jax
import jax.numpy as jnp
from jax import lax
from jax.experimental import pallas as pl
from jax.experimental.pallas import tpu as pltpu
from jax.sharding import PartitionSpec as P

CXL = 8
CYL = 8
CZ = 128
NAX = 16
ROWS = 64
SLOTS = 96
BORDER = 32
INNER = 18
MAIN = 48

COS_TURN = -0.6427876096865393
SIN_TURN = 0.766044443118978
GOLDEN_TURN = 2.399963229728653

F32 = jnp.float32
BF16 = jnp.bfloat16
MESH = pl.DeviceIdType.MESH


def axis_table():
    table = []
    for number in range(NAX):
        height = 1.0 - (2.0 * number + 1.0) / NAX
        radius = math.sqrt(1.0 - height * height)
        phase = number * GOLDEN_TURN
        table.append((radius * math.cos(phase), radius * math.sin(phase), height))
    return table


def dot_nt(a, b):
    return lax.dot_general(a, b, (((1,), (1,)), ((), ())), preferred_element_type=F32)


def iota(shape, dim):
    return lax.broadcasted_iota(jnp.int32, shape, dim)


def iota16(shape, dim):
    return iota(shape, dim).astype(F32).astype(BF16)


def spread(row, height):
    return jnp.broadcast_to(row, (height, 128)).astype(BF16)


def one_hot(hit):
    return jnp.where(hit, jnp.ones(hit.shape, BF16), jnp.zeros(hit.shape, BF16))


def high_part(value):
    return value.astype(BF16).astype(F32)


PIECES = (
    [(0, 2, 0, 1, 0, 0), (8, 2, 0, 1, 4, 0), (16, 2, 8, 1, 4, 0), (24, 2, 8, 1, 0, 0)]
    + [(10, 6, 2, 1, 4, 0), (26, 6, 2, 1, 0, 0)]
    + [(2 + 3 * u, 3, u, 0, 1, 1) for u in range(2)]
    + [(18 + 3 * u, 3, 8 + u, 0, 1, 1) for u in range(2)]
    + [(32 + 3 * w, 3, 2 + w, 0, 1, 1) for w in range(6)]
)


def look_up(table, heights, groups, cols, local, j):
    col_of = iota16((256, 128), 0)
    row_of = iota((heights, 128), 0).astype(F32)
    hits = [one_hot(col_of == spread(cols[i : i + 1, :], 256)) for i in (j, j + 1)]
    both = jnp.dot(table, jnp.concatenate(hits, 1), preferred_element_type=F32)
    found = []
    for i in (0, 1):
        lanes = slice(i * 128, i * 128 + 128)
        hit = row_of == jnp.broadcast_to(local[j + i : j + i + 1, :], (heights, 128))
        row = []
        for c in range(4):
            part = both[heights * c : heights * (c + 1), lanes]
            if c < 3:
                part = part + both[heights * (4 + c) : heights * (5 + c), lanes]
            row.append(jnp.sum(jnp.where(hit, part, 0.0), axis=0, keepdims=True))
        found.append(row)
    return found


def look_up_block(table, heights, cols, local):
    found = []
    for j in range(0, 8, 2):
        found += look_up(table, heights, 7, cols, local, j)
    return [jnp.concatenate([row[c] for row in found], 0) for c in range(4)]


def neighbours():
    x, y = lax.axis_index("gx"), lax.axis_index("gy")
    nx, ny = lax.axis_size("gx"), lax.axis_size("gy")
    left, right = lax.rem(x + nx - 1, nx), lax.rem(x + 1, nx)
    down, up = lax.rem(y + ny - 1, ny), lax.rem(y + 1, ny)
    sides = [(left, y), (right, y), (x, down), (x, up)]
    corners = [(left, down), (left, up), (right, down), (right, up)]
    return sides + corners


def prep_kernel(
    leaving_in, shift_in, vel_in, pos_in, axis_in,
    border, own_axis, ids, inner_mean, found, vel, got_side, got_corner,
    leaving, shift, pos, axis, row_s, col_s, sums, run_s, prep_s, axis_s, side, corner,
    load_sem, send_sem, recv_sem,
):
    loads = [
        pltpu.make_async_copy(source, target, load_sem.at[k])
        for k, (source, target) in enumerate(
            ((pos_in, pos), (shift_in, shift), (axis_in, axis), (vel_in, vel), (leaving_in, leaving))
        )
    ]
    for load in loads:
        load.start()
    targets = neighbours()
    barrier = pltpu.get_barrier_semaphore()
    for target in targets:
        pl.semaphore_signal(barrier, inc=1, device_id=target, device_id_type=MESH)
    axis_s[...] = jnp.zeros(axis_s.shape, F32)
    for k in (0, 2):
        side[k, 112:144, :] = jnp.zeros((32, 128), F32)
    corner[:, 20:24, :] = jnp.zeros((4, 4, 128), F32)
    for load in loads:
        load.wait()

    low_x = (shift[0] == 1).astype(jnp.int32)
    low_y = (shift[1] == 1).astype(jnp.int32)
    shifts = [shift[k].astype(F32) * 0.25 for k in range(3)]
    cell_x = jnp.floor(pos[0] + shifts[0]) + low_x.astype(F32)
    cell_y = jnp.floor(pos[1] + shifts[1]) + low_y.astype(F32)
    cell_z = jnp.floor(pos[2] + shifts[2])
    cell_z = jnp.where(cell_z >= float(CZ), cell_z - float(CZ), cell_z)
    half = jnp.floor(cell_y * 0.5)
    is_left = cell_x < 2.0
    is_right = cell_x > 7.0
    bottom = cell_x + jnp.where(is_left, 0.0, jnp.where(is_right, 16.0, 24.0))
    middle = 3.0 * cell_x + half + jnp.where(is_left, 1.0, jnp.where(is_right, -7.0, 25.0))
    row = jnp.where(half < 1.0, bottom, jnp.where(half > 3.0, cell_x + 8.0, middle))
    col = (cell_y - 2.0 * half) * float(CZ) + cell_z
    row_s[...] = row
    col_s[...] = col
    ids[...] = row * 256.0 + col

    row_of = iota16((MAIN, 128), 0)
    col_of = iota16((256, 128), 0)
    rest = iota((16, 128), 0)
    rest_row = (MAIN + rest % 2).astype(F32).astype(BF16)
    rest_is = [rest // 2 == g for g in range(7)]
    for chunk in range(8):
        left_parts = [[] for _ in range(8)]
        right_parts = []
        for j in range(8):
            r = chunk * 8 + j
            values = [jnp.ones((1, 128), F32)]
            for c in range(3):
                high = high_part(vel[c, r : r + 1, :])
                values += [high, vel[c, r : r + 1, :] - high]
            hit = row_of == spread(row_s[r : r + 1, :], MAIN)
            tail = jnp.broadcast_to(values[0], (16, 128))
            for g in range(7):
                wide = spread(values[g], MAIN)
                left_parts[g].append(jnp.where(hit, wide, jnp.zeros((MAIN, 128), BF16)))
                if g:
                    tail = jnp.where(rest_is[g], jnp.broadcast_to(values[g], (16, 128)), tail)
            hit = rest_row == spread(row_s[r : r + 1, :], 16)
            left_parts[7].append(jnp.where(hit, tail.astype(BF16), jnp.zeros((16, 128), BF16)))
            right_parts.append(one_hot(col_of == spread(col_s[r : r + 1, :], 256)))
        part = dot_nt(
            jnp.concatenate([jnp.concatenate(p, 1) for p in left_parts], 0),
            jnp.concatenate(right_parts, 1),
        )
        if chunk == 0:
            sums[...] = part
        else:
            sums[...] += part
    for c in range(4):
        if c == 0:
            group = sums[0:BORDER, :]
        else:
            at = (2 * c - 1) * MAIN
            group = sums[at : at + BORDER, :] + sums[at + MAIN : at + MAIN + BORDER, :]
        for par in range(2):
            lanes = slice(par * 128, par * 128 + 128)
            border[pl.ds(2 * c + par, BORDER, stride=8), :] = group[:, lanes]
    for k, start in enumerate((0, 16, 24, 8)):
        if start == 24:
            side[k, 0:64, :] = border[192:256, :]
            side[k, 64:80, :] = border[0:16, :]
        else:
            side[k, 0:80, :] = border[8 * start : 8 * start + 80, :]
    for k, start in enumerate((0, 8, 24, 16)):
        corner[k, 0:16, :] = border[8 * start : 8 * start + 16, :]

    for cx in range(CXL):
        at = (cx + 1) * 11 + 1
        axis_s[at : at + 8, :] = axis[cx * 8 : cx * 8 + 8, :].astype(F32)
    for par in range(2):
        for first, n, cx, cx_step, half_y, half_step in PIECES:
            start = (cx + 1 - low_x) * 11 + 2 * half_y + par + 1 - low_y
            step = 11 * cx_step + 2 * half_step
            own_axis[par, first : first + n, :] = axis_s[pl.ds(start, n, stride=step), :]
        own_axis[par, 50:56, :] = jnp.zeros((6, 128), F32)
        base = 112 + 16 * par
        for k, order in ((0, ((8, 2), (2, 6), (0, 2))), (2, ((0, 2), (26, 6), (24, 2)))):
            at = base
            for first, n in order:
                side[k, at : at + n, :] = own_axis[par, first : first + n, :]
                at += n
        corner[0, 20 + 2 * par : 22 + 2 * par, :] = own_axis[par, 0:2, :]

    slot = iota((8, 128), 0) * 128 + iota((8, 128), 1)
    lane = iota((8, 128), 1)
    counts = [leaving[k] for k in range(4)]
    starts = [jnp.int32(0), counts[0], counts[0] + counts[1], counts[0] + counts[1] + counts[2]]

    def run(load, d):
        if d == 0:
            return load(0)
        q = starts[d] // 128
        r = starts[d] - q * 128
        back = jnp.where(r == 0, 0, 128 - r)
        here = pltpu.roll(load(q), back, 1)
        after = pltpu.roll(load(q + 1), back, 1)
        return jnp.where(lane < 128 - r, here, after)

    def moved(d, run_row):
        if d == 0:
            return run_row + jnp.where(run_row < 2.0, 24.0, jnp.where(run_row < 8.0, 16.0, 8.0))
        if d == 1:
            return run_row - jnp.where(run_row < 18.0, 8.0, jnp.where(run_row < 24.0, 16.0, 24.0))
        if d == 2:
            return run_row + jnp.where(run_row < 2.0, 8.0, jnp.where(run_row < 26.0, -8.0, -16.0))
        return run_row + jnp.where(run_row < 10.0, -8.0, jnp.where(run_row < 16.0, 16.0, 8.0))

    flags = []
    for d in range(4):
        live = slot < counts[d]
        values = [run(lambda q, c=c: vel[c, pl.ds(q, 8), :], d) for c in range(3)]
        run_row = run(lambda q: row_s[pl.ds(q, 8), :], d)
        run_col = run(lambda q: col_s[pl.ds(q, 8), :], d)
        kept = live
        if d < 2:
            y = run(lambda q: pos[1, pl.ds(q, 8), :], d)
            down = live & (y < 0.0)
            up = live & (y >= float(CYL))
            kept = live & (y >= 0.0) & (y < float(CYL))
            flags += [down, up]
            for c in range(3):
                high = high_part(values[c])
                run_s[d, 16 * c : 16 * c + 8, :] = high
                run_s[d, 16 * c + 8 : 16 * c + 16, :] = values[c] - high
            run_s[d, 48:56, :] = run_row
            run_s[d, 56:64, :] = run_col
            run_s[d, 64:72, :] = jnp.ones((8, 128), F32)
            run_s[d, 72:128, :] = jnp.zeros((56, 128), F32)
        for c in range(3):
            side[d, 80 + 8 * c : 88 + 8 * c, :] = values[c]
        side[d, 104:112, :] = jnp.where(kept, moved(d, run_row) * 256.0 + run_col, -1.0)

    flag = jnp.concatenate([f.astype(F32) for f in flags], 0)
    flag16 = flag.astype(BF16)
    before = (iota((128, 128), 0) < iota((128, 128), 1)).astype(F32).astype(BF16)
    inside = jnp.dot(flag16, before, preferred_element_type=F32)
    total = jnp.dot(flag16, jnp.ones((128, 128), BF16), preferred_element_type=F32)
    r0, r1 = iota((32, 32), 0), iota((32, 32), 1)
    earlier = ((r1 < r0) & (r0 // 8 == r1 // 8)).astype(F32).astype(BF16)
    offset = jnp.dot(earlier, total.astype(BF16), preferred_element_type=F32)
    prep_s[...] = jnp.where(flag > 0.0, inside + offset, -1.0)
    rank_of = iota16((128, 128), 0)
    for d in range(2):
        rows = jnp.concatenate([run_s[d, pl.ds(r, 16, stride=8), :] for r in range(8)], 1).astype(BF16)
        for s in range(2):
            at = d * 16 + s * 8
            hits = [one_hot(rank_of == spread(prep_s[at + r : at + r + 1, :], 128)) for r in range(8)]
            packed = dot_nt(rows, jnp.concatenate(hits, 1))
            k = d * 2 + s
            for c in range(3):
                corner[k, 16 + c : 17 + c, :] = packed[2 * c : 2 * c + 1] + packed[2 * c + 1 : 2 * c + 2]
            there = (packed[6:7] + (16.0 - 32.0 * d)) * 256.0 + packed[7:8]
            corner[k, 19:20, :] = jnp.where(packed[8:9] > 0.5, there, -1.0)

    pl.semaphore_wait(barrier, 8)
    copies = []
    for k in (4, 5, 6, 7, 0, 1, 2, 3):
        if k < 4:
            size = 144 if k in (0, 2) else 112
            source, target = side.at[k, pl.ds(0, size), :], got_side.at[k, pl.ds(0, size), :]
        else:
            source, target = corner.at[k - 4], got_corner.at[k - 4]
        copy = pltpu.make_async_remote_copy(
            src_ref=source,
            dst_ref=target,
            send_sem=send_sem.at[k],
            recv_sem=recv_sem.at[k],
            device_id=targets[k],
            device_id_type=MESH,
        )
        copy.start()
        copies.append(copy)

    def inner(group):
        at = group * MAIN + BORDER
        end = 7 * MAIN + 2 * group
        return jnp.concatenate([sums[at : at + 16, :], sums[end : end + 2, :], jnp.zeros((6, 256), F32)], 0)

    most = jnp.maximum(inner(0), 1.0)
    high_rows, low_rows = [], []
    for c in range(3):
        mean = (inner(1 + 2 * c) + inner(2 + 2 * c)) / most
        inner_mean[c] = mean
        high = high_part(mean)
        high_rows.append(high)
        low_rows.append(mean - high)
    high_rows.append(jnp.concatenate([own_axis[0, BORDER:56, :], own_axis[1, BORDER:56, :]], 1))
    table = jnp.concatenate(high_rows + low_rows, 0).astype(BF16)
    for b in range(1, 8):
        at = slice(8 * b, 8 * b + 8)
        looked = look_up_block(table, 24, col_s[at, :], row_s[at, :] - float(BORDER))
        for c in range(4):
            found[c, at, :] = looked[c]
    gone = starts[3] + counts[3]
    place = iota((ROWS, 128), 0) * 128 + iota((ROWS, 128), 1)
    ids[...] = jnp.where(place >= gone, ids[...], -1.0)
    for copy in copies:
        copy.wait()


def collide_kernel(
    shift_in, border, own_axis, ids, inner_mean, found, vel, got_side, got_corner,
    out_hbm, flow_hbm,
    shift, out, flow, total, means, load_sem, store_sem,
):
    load = pltpu.make_async_copy(shift_in, shift, load_sem)
    load.start()
    total[0 : 8 * BORDER, :] = border[0 : 8 * BORDER, :]
    for k, places in enumerate(
        (
            ((24, 0, 2), (18, 2, 6), (16, 8, 2)),
            ((8, 0, 2), (2, 2, 6), (0, 8, 2)),
            ((16, 0, 2), (10, 2, 6), (8, 8, 2)),
            ((0, 0, 2), (26, 2, 6), (24, 8, 2)),
        )
    ):
        for mine, theirs, n in places:
            total[8 * mine : 8 * (mine + n), :] += got_side[k, 8 * theirs : 8 * (theirs + n), :]
    for k, mine in enumerate((16, 24, 8, 0)):
        total[8 * mine : 8 * mine + 16, :] += got_corner[k, 0:16, :]
    numbers = []
    for par in range(2):
        number = own_axis[par, 0:BORDER, :]
        at = 112 + 16 * par
        gap = jnp.zeros((16, 128), F32)
        number = number + jnp.concatenate([gap, got_side[0, at : at + 16, :]], 0)
        number = number + jnp.concatenate([gap[0:8], got_side[2, at : at + 16, :], gap[0:8]], 0)
        pair = got_corner[0, 20 + 2 * par : 22 + 2 * par, :]
        number = number + jnp.concatenate([gap, pair, gap[0:14]], 0)
        numbers.append(number)
    groups = [None] * 7
    most = [jnp.maximum(total[pl.ds(par, BORDER, stride=8), :], 1.0) for par in range(2)]
    border_mean = []
    for c in range(3):
        halves = [total[pl.ds(2 + 2 * c + par, BORDER, stride=8), :] / most[par] for par in range(2)]
        mean = jnp.concatenate(halves, 1)
        border_mean.append(mean)
        groups[c] = high_part(mean)
        groups[4 + c] = mean - groups[c]
    groups[3] = jnp.concatenate(numbers, 1)
    table = jnp.concatenate(groups, 0).astype(BF16)
    choices = axis_table()

    def turn(at, live, v, looked):
        mean = looked[:3]
        number = looked[3].astype(jnp.int32)
        bits = [(number & (1 << k)) != 0 for k in range(4)]
        a = []
        for c in range(2):
            level = [entry[c] for entry in choices]
            for k in range(4):
                level = [jnp.where(bits[k], level[2 * m + 1], level[2 * m]) for m in range(len(level) // 2)]
            a.append(level[0])
        a.append((1.0 - 1.0 / NAX) - (2.0 / NAX) * looked[3])
        w = [v[c] - mean[c] for c in range(3)]
        cross = [
            a[1] * w[2] - a[2] * w[1],
            a[2] * w[0] - a[0] * w[2],
            a[0] * w[1] - a[1] * w[0],
        ]
        along = (a[0] * w[0] + a[1] * w[1] + a[2] * w[2]) * (1.0 - COS_TURN)
        for c in range(3):
            turned = mean[c] + COS_TURN * w[c] + SIN_TURN * cross[c] + along * a[c]
            out[c, at, :] = jnp.where(live, turned, 0.0)

    slot = iota((8, 128), 0) * 128 + iota((8, 128), 1)
    arrived = []
    for k in (1, 0, 3, 2):
        v = [got_side[k, 80 + 8 * c : 88 + 8 * c, :] for c in range(4)]
        if k > 1:
            first, second = ((2, 0), (3, 1))[k - 2]
            n0 = jnp.sum((v[3] >= 0.0).astype(jnp.int32))
            n1 = jnp.sum((got_corner[first, 19:20, :] >= 0.0).astype(jnp.int32))
            in_first = (slot >= n0) & (slot < n0 + n1)
            in_second = (slot >= n0 + n1) & (slot < n0 + n1 + 128)
            by1, by2 = lax.rem(n0, 128), lax.rem(n0 + n1, 128)
            for c in range(4):
                at = slice(16 + c, 17 + c)
                one = pltpu.roll(jnp.broadcast_to(got_corner[first, at, :], (8, 128)), by1, 1)
                two = pltpu.roll(jnp.broadcast_to(got_corner[second, at, :], (8, 128)), by2, 1)
                v[c] = jnp.where(in_first, one, jnp.where(in_second, two, v[c]))
        arrived.append(v)

    out[:, 0:8, :] = jnp.zeros((3, 8, 128), F32)
    for b in range(1, 8):
        at = slice(8 * b, 8 * b + 8)
        block = ids[at, :]
        rows = jnp.floor(block * (1.0 / 256.0))
        looked = look_up_block(table, BORDER, block - rows * 256.0, rows)
        turn(at, block >= 0.0, [vel[c, at, :] for c in range(3)], [looked[c] + found[c, at, :] for c in range(4)])
    stores = []

    def store(source, target):
        copy = pltpu.make_async_copy(source, target, store_sem.at[len(stores)])
        copy.start()
        stores.append(copy)

    for v, at, window in zip(arrived, (64, 72, 80, 88), (0, 16, 24, 8)):
        rows = jnp.floor(v[3] * (1.0 / 256.0))
        cols = v[3] - rows * 256.0
        if window == 24:
            part = [jnp.concatenate([g[24:32], g[0:8]], 0) for g in groups]
            local = jnp.where(rows < 2.0, rows + 8.0, rows - 24.0)
        else:
            part = [g[window : window + 16] for g in groups]
            local = rows - float(window)
        looked = look_up_block(jnp.concatenate(part, 0).astype(BF16), 16, cols, local)
        turn(slice(at, at + 8), v[3] >= 0.0, v, looked)
    store(out, out_hbm)

    for c in range(3):
        for par in range(2):
            lanes = slice(par * 128, par * 128 + 128)
            for first, n, cx, cx_step, half_y, half_step in PIECES:
                if first < BORDER:
                    piece = border_mean[c][first : first + n, lanes]
                else:
                    piece = inner_mean[c, first - BORDER : first - BORDER + n, lanes]
                start = cx * 10 + 2 * half_y + par
                means[c, pl.ds(start, n, stride=10 * cx_step + 2 * half_step), :] = piece
    load.wait()
    low_x = (shift[0] == 1).astype(jnp.int32)
    low_y = (shift[1] == 1).astype(jnp.int32)
    for c in range(3):
        for cx in range(CXL):
            flow[c, cx * 8 : cx * 8 + 8, :] = means[c, pl.ds((cx + low_x) * 10 + low_y, 8), :]
    store(flow, flow_hbm)
    for copy in stores:
        copy.wait()


def shape(*dims):
    return jax.ShapeDtypeStruct(dims, F32)


def per_device(velocity, position, leaving, grid_shift, axis_index):
    vel = velocity.reshape(3, ROWS, 128)
    pos = position.reshape(3, ROWS, 128)
    axis = axis_index.reshape(64, 128)
    leaving = leaving.reshape(4)
    vel, pos, axis, leaving, grid_shift = [
        pltpu.with_memory_space_constraint(v, pltpu.HBM) for v in (vel, pos, axis, leaving, grid_shift)
    ]
    vmem = pl.BlockSpec(memory_space=pltpu.VMEM)
    hbm = pl.BlockSpec(memory_space=pltpu.HBM)
    parts = pl.pallas_call(
        prep_kernel,
        name="prep",
        out_shape=(
            shape(8 * BORDER + 8, 128),
            shape(2, 56, 128),
            shape(ROWS, 128),
            shape(3, 24, 256),
            shape(4, ROWS, 128),
            shape(3, ROWS, 128),
            shape(4, 144, 128),
            shape(4, 24, 128),
        ),
        in_specs=[hbm] * 5,
        out_specs=(vmem,) * 8,
        scratch_shapes=[
            pltpu.SMEM((4,), jnp.int32),
            pltpu.SMEM((3,), jnp.int32),
            pltpu.VMEM((3, ROWS, 128), F32),
            pltpu.VMEM((64, 128), jnp.int32),
            pltpu.VMEM((ROWS, 128), F32),
            pltpu.VMEM((ROWS, 128), F32),
            pltpu.VMEM((7 * MAIN + 16, 256), F32),
            pltpu.VMEM((2, 136, 128), F32),
            pltpu.VMEM((32, 128), F32),
            pltpu.VMEM((144, 128), F32),
            pltpu.VMEM((4, 144, 128), F32),
            pltpu.VMEM((4, 24, 128), F32),
            pltpu.SemaphoreType.DMA((5,)),
            pltpu.SemaphoreType.DMA((8,)),
            pltpu.SemaphoreType.DMA((8,)),
        ],
        compiler_params=pltpu.CompilerParams(
            collective_id=0, has_side_effects=True, vmem_limit_bytes=32 << 20
        ),
    )(leaving, grid_shift, vel, pos, axis)
    out, flow = pl.pallas_call(
        collide_kernel,
        name="collide",
        out_shape=(shape(3, SLOTS, 128), shape(3, 64, 128)),
        in_specs=[hbm] + [vmem] * 8,
        out_specs=(hbm, hbm),
        scratch_shapes=[
            pltpu.SMEM((3,), jnp.int32),
            pltpu.VMEM((3, SLOTS, 128), F32),
            pltpu.VMEM((3, 64, 128), F32),
            pltpu.VMEM((8 * BORDER + 8, 128), F32),
            pltpu.VMEM((3, 112, 128), F32),
            pltpu.SemaphoreType.DMA,
            pltpu.SemaphoreType.DMA((3,)),
        ],
        compiler_params=pltpu.CompilerParams(vmem_limit_bytes=32 << 20),
    )(grid_shift, *parts)
    return out.reshape(3, 1, 1, SLOTS * 128), flow.reshape(3, 1, 1, 64 * 128)


def solution(mesh):
    return jax.shard_map(
        per_device,
        mesh=mesh,
        in_specs=(
            P(None, "gx", "gy", None),
            P(None, "gx", "gy", None),
            P("gx", "gy", None),
            P(),
            P("gx", "gy", None),
        ),
        out_specs=(P(None, "gx", "gy", None), P(None, "gx", "gy", None)),
        check_vma=False,
    )
```

```python
import math

import jax
import jax.numpy as jnp
from jax import lax
from jax.experimental import pallas as pl
from jax.experimental.pallas import tpu as pltpu
from jax.sharding import PartitionSpec as P

CXL = 8
CYL = 8
CZ = 128
NAX = 16
ROWS = 64
SLOTS = 96
BORDER = 32
INNER = 18
MAIN = 48

COS_TURN = -0.6427876096865393
SIN_TURN = 0.766044443118978
GOLDEN_TURN = 2.399963229728653

F32 = jnp.float32
BF16 = jnp.bfloat16
MESH = pl.DeviceIdType.MESH


def axis_table():
    table = []
    for number in range(NAX):
        height = 1.0 - (2.0 * number + 1.0) / NAX
        radius = math.sqrt(1.0 - height * height)
        phase = number * GOLDEN_TURN
        table.append((radius * math.cos(phase), radius * math.sin(phase), height))
    return table


def dot_nt(a, b):
    return lax.dot_general(a, b, (((1,), (1,)), ((), ())), preferred_element_type=F32)


def iota(shape, dim):
    return lax.broadcasted_iota(jnp.int32, shape, dim)


def iota16(shape, dim):
    return iota(shape, dim).astype(F32).astype(BF16)


def spread(row, height):
    return jnp.broadcast_to(row, (height, 128)).astype(BF16)


def one_hot(hit):
    return jnp.where(hit, jnp.ones(hit.shape, BF16), jnp.zeros(hit.shape, BF16))


def high_part(value):
    return value.astype(BF16).astype(F32)


PIECES = (
    [(0, 2, 0, 1, 0, 0), (8, 2, 0, 1, 4, 0), (16, 2, 8, 1, 4, 0), (24, 2, 8, 1, 0, 0)]
    + [(10, 6, 2, 1, 4, 0), (26, 6, 2, 1, 0, 0)]
    + [(2 + 3 * u, 3, u, 0, 1, 1) for u in range(2)]
    + [(18 + 3 * u, 3, 8 + u, 0, 1, 1) for u in range(2)]
    + [(32 + 3 * w, 3, 2 + w, 0, 1, 1) for w in range(6)]
)


def look_up(table, heights, groups, cols, local, j):
    col_of = iota16((256, 128), 0)
    row_of = iota((heights, 128), 0).astype(F32)
    hits = [one_hot(col_of == spread(cols[i : i + 1, :], 256)) for i in (j, j + 1)]
    both = jnp.dot(table, jnp.concatenate(hits, 1), preferred_element_type=F32)
    found = []
    for i in (0, 1):
        lanes = slice(i * 128, i * 128 + 128)
        hit = row_of == jnp.broadcast_to(local[j + i : j + i + 1, :], (heights, 128))
        row = []
        for c in range(4):
            part = both[heights * c : heights * (c + 1), lanes]
            if c < 3:
                part = part + both[heights * (4 + c) : heights * (5 + c), lanes]
            row.append(jnp.sum(jnp.where(hit, part, 0.0), axis=0, keepdims=True))
        found.append(row)
    return found


def look_up_block(table, heights, cols, local):
    found = []
    for j in range(0, 8, 2):
        found += look_up(table, heights, 7, cols, local, j)
    return [jnp.concatenate([row[c] for row in found], 0) for c in range(4)]


def neighbours():
    x, y = lax.axis_index("gx"), lax.axis_index("gy")
    nx, ny = lax.axis_size("gx"), lax.axis_size("gy")
    left, right = lax.rem(x + nx - 1, nx), lax.rem(x + 1, nx)
    down, up = lax.rem(y + ny - 1, ny), lax.rem(y + 1, ny)
    sides = [(left, y), (right, y), (x, down), (x, up)]
    corners = [(left, down), (left, up), (right, down), (right, up)]
    return sides + corners


def prep_kernel(
    leaving_in, shift_in, vel_in, pos_in, axis_in,
    border, own_axis, ids, inner_means, found, vel, got_side, got_corner,
    leaving, shift, pos, axis, row_s, col_s, sums, run_s, prep_s, axis_s, side, corner,
    load_sem, send_sem, recv_sem,
):
    loads = [
        pltpu.make_async_copy(source, target, load_sem.at[k])
        for k, (source, target) in enumerate(
            ((pos_in, pos), (shift_in, shift), (axis_in, axis), (vel_in, vel), (leaving_in, leaving))
        )
    ]
    for load in loads:
        load.start()
    targets = neighbours()
    barrier = pltpu.get_barrier_semaphore()
    for target in targets:
        pl.semaphore_signal(barrier, inc=1, device_id=target, device_id_type=MESH)
    axis_s[...] = jnp.zeros(axis_s.shape, F32)
    side[:, 112:144, :] = jnp.zeros((4, 32, 128), F32)
    for load in loads:
        load.wait()

    low_x = (shift[0] == 1).astype(jnp.int32)
    low_y = (shift[1] == 1).astype(jnp.int32)
    shifts = [shift[k].astype(F32) * 0.25 for k in range(3)]
    cell_x = jnp.floor(pos[0] + shifts[0]) + low_x.astype(F32)
    cell_y = jnp.floor(pos[1] + shifts[1]) + low_y.astype(F32)
    cell_z = jnp.floor(pos[2] + shifts[2])
    cell_z = jnp.where(cell_z >= float(CZ), cell_z - float(CZ), cell_z)
    half = jnp.floor(cell_y * 0.5)
    is_left = cell_x < 2.0
    is_right = cell_x > 7.0
    bottom = cell_x + jnp.where(is_left, 0.0, jnp.where(is_right, 16.0, 24.0))
    middle = 3.0 * cell_x + half + jnp.where(is_left, 1.0, jnp.where(is_right, -7.0, 25.0))
    row = jnp.where(half < 1.0, bottom, jnp.where(half > 3.0, cell_x + 8.0, middle))
    col = (cell_y - 2.0 * half) * float(CZ) + cell_z
    row_s[...] = row
    col_s[...] = col
    ids[...] = row * 256.0 + col

    row_of = iota16((MAIN, 128), 0)
    col_of = iota16((256, 128), 0)
    rest = iota((16, 128), 0)
    rest_row = (MAIN + rest % 2).astype(F32).astype(BF16)
    rest_is = [rest // 2 == g for g in range(7)]
    for chunk in range(8):
        left_parts = [[] for _ in range(8)]
        right_parts = []
        for j in range(8):
            r = chunk * 8 + j
            values = [jnp.ones((1, 128), F32)]
            for c in range(3):
                high = high_part(vel[c, r : r + 1, :])
                values += [high, vel[c, r : r + 1, :] - high]
            hit = row_of == spread(row_s[r : r + 1, :], MAIN)
            tail = jnp.broadcast_to(values[0], (16, 128))
            for g in range(7):
                wide = spread(values[g], MAIN)
                left_parts[g].append(jnp.where(hit, wide, jnp.zeros((MAIN, 128), BF16)))
                if g:
                    tail = jnp.where(rest_is[g], jnp.broadcast_to(values[g], (16, 128)), tail)
            hit = rest_row == spread(row_s[r : r + 1, :], 16)
            left_parts[7].append(jnp.where(hit, tail.astype(BF16), jnp.zeros((16, 128), BF16)))
            right_parts.append(one_hot(col_of == spread(col_s[r : r + 1, :], 256)))
        part = dot_nt(
            jnp.concatenate([jnp.concatenate(p, 1) for p in left_parts], 0),
            jnp.concatenate(right_parts, 1),
        )
        if chunk == 0:
            sums[...] = part
        else:
            sums[...] += part
    for c in range(4):
        if c == 0:
            group = sums[0:BORDER, :]
        else:
            at = (2 * c - 1) * MAIN
            group = sums[at : at + BORDER, :] + sums[at + MAIN : at + MAIN + BORDER, :]
        for par in range(2):
            lanes = slice(par * 128, par * 128 + 128)
            border[pl.ds(2 * c + par, BORDER, stride=8), :] = group[:, lanes]
    for k, start in enumerate((0, 16, 24, 8)):
        if start == 24:
            side[k, 0:64, :] = border[192:256, :]
            side[k, 64:80, :] = border[0:16, :]
        else:
            side[k, 0:80, :] = border[8 * start : 8 * start + 80, :]
    for k, start in enumerate((0, 8, 24, 16)):
        corner[k, 0:16, :] = border[8 * start : 8 * start + 16, :]

    for cx in range(CXL):
        at = (cx + 1) * 11 + 1
        axis_s[at : at + 8, :] = axis[cx * 8 : cx * 8 + 8, :].astype(F32)
    for par in range(2):
        for first, n, cx, cx_step, half_y, half_step in PIECES:
            start = (cx + 1 - low_x) * 11 + 2 * half_y + par + 1 - low_y
            step = 11 * cx_step + 2 * half_step
            own_axis[par, first : first + n, :] = axis_s[pl.ds(start, n, stride=step), :]
        own_axis[par, 50:56, :] = jnp.zeros((6, 128), F32)
        base = 112 + 16 * par
        for k, order in enumerate(
            (((8, 2), (2, 6), (0, 2)), ((24, 2), (18, 6), (16, 2)), ((0, 2), (26, 6), (24, 2)), ((16, 2), (10, 6), (8, 2)))
        ):
            at = base
            for first, n in order:
                side[k, at : at + n, :] = own_axis[par, first : first + n, :]
                at += n
        for k, first in enumerate((0, 8, 24, 16)):
            corner[k, 20 + 2 * par : 22 + 2 * par, :] = own_axis[par, first : first + 2, :]

    slot = iota((8, 128), 0) * 128 + iota((8, 128), 1)
    lane = iota((8, 128), 1)
    counts = [leaving[k] for k in range(4)]
    starts = [jnp.int32(0), counts[0], counts[0] + counts[1], counts[0] + counts[1] + counts[2]]

    def run(load, d):
        if d == 0:
            return load(0)
        q = starts[d] // 128
        r = starts[d] - q * 128
        back = jnp.where(r == 0, 0, 128 - r)
        here = pltpu.roll(load(q), back, 1)
        after = pltpu.roll(load(q + 1), back, 1)
        return jnp.where(lane < 128 - r, here, after)

    def moved(d, run_row):
        if d == 0:
            return run_row + jnp.where(run_row < 2.0, 24.0, jnp.where(run_row < 8.0, 16.0, 8.0))
        if d == 1:
            return run_row - jnp.where(run_row < 18.0, 8.0, jnp.where(run_row < 24.0, 16.0, 24.0))
        if d == 2:
            return run_row + jnp.where(run_row < 2.0, 8.0, jnp.where(run_row < 26.0, -8.0, -16.0))
        return run_row + jnp.where(run_row < 10.0, -8.0, jnp.where(run_row < 16.0, 16.0, 8.0))

    flags = []
    for d in range(4):
        live = slot < counts[d]
        values = [run(lambda q, c=c: vel[c, pl.ds(q, 8), :], d) for c in range(3)]
        run_row = run(lambda q: row_s[pl.ds(q, 8), :], d)
        run_col = run(lambda q: col_s[pl.ds(q, 8), :], d)
        kept = live
        if d < 2:
            y = run(lambda q: pos[1, pl.ds(q, 8), :], d)
            down = live & (y < 0.0)
            up = live & (y >= float(CYL))
            kept = live & (y >= 0.0) & (y < float(CYL))
            flags += [down, up]
            for c in range(3):
                high = high_part(values[c])
                run_s[d, 16 * c : 16 * c + 8, :] = high
                run_s[d, 16 * c + 8 : 16 * c + 16, :] = values[c] - high
            run_s[d, 48:56, :] = run_row
            run_s[d, 56:64, :] = run_col
            run_s[d, 64:72, :] = jnp.ones((8, 128), F32)
            run_s[d, 72:128, :] = jnp.zeros((56, 128), F32)
        for c in range(3):
            side[d, 80 + 8 * c : 88 + 8 * c, :] = values[c]
        side[d, 104:112, :] = jnp.where(kept, moved(d, run_row) * 256.0 + run_col, -1.0)

    flag = jnp.concatenate([f.astype(F32) for f in flags], 0)
    flag16 = flag.astype(BF16)
    before = (iota((128, 128), 0) < iota((128, 128), 1)).astype(F32).astype(BF16)
    inside = jnp.dot(flag16, before, preferred_element_type=F32)
    total = jnp.dot(flag16, jnp.ones((128, 128), BF16), preferred_element_type=F32)
    r0, r1 = iota((32, 32), 0), iota((32, 32), 1)
    earlier = ((r1 < r0) & (r0 // 8 == r1 // 8)).astype(F32).astype(BF16)
    offset = jnp.dot(earlier, total.astype(BF16), preferred_element_type=F32)
    prep_s[...] = jnp.where(flag > 0.0, inside + offset, -1.0)
    rank_of = iota16((128, 128), 0)
    for d in range(2):
        rows = jnp.concatenate([run_s[d, pl.ds(r, 16, stride=8), :] for r in range(8)], 1).astype(BF16)
        for s in range(2):
            at = d * 16 + s * 8
            hits = [one_hot(rank_of == spread(prep_s[at + r : at + r + 1, :], 128)) for r in range(8)]
            packed = dot_nt(rows, jnp.concatenate(hits, 1))
            k = d * 2 + s
            for c in range(3):
                corner[k, 16 + c : 17 + c, :] = packed[2 * c : 2 * c + 1] + packed[2 * c + 1 : 2 * c + 2]
            there = (packed[6:7] + (16.0 - 32.0 * d)) * 256.0 + packed[7:8]
            corner[k, 19:20, :] = jnp.where(packed[8:9] > 0.5, there, -1.0)

    pl.semaphore_wait(barrier, 8)
    copies = []
    for k in (4, 5, 6, 7, 0, 1, 2, 3):
        source, target = (side.at[k], got_side.at[k]) if k < 4 else (corner.at[k - 4], got_corner.at[k - 4])
        copy = pltpu.make_async_remote_copy(
            src_ref=source,
            dst_ref=target,
            send_sem=send_sem.at[k],
            recv_sem=recv_sem.at[k],
            device_id=targets[k],
            device_id_type=MESH,
        )
        copy.start()
        copies.append(copy)

    def inner(group):
        at = group * MAIN + BORDER
        end = 7 * MAIN + 2 * group
        return jnp.concatenate([sums[at : at + 16, :], sums[end : end + 2, :], jnp.zeros((6, 256), F32)], 0)

    most = jnp.maximum(inner(0), 1.0)
    high_rows, low_rows = [], []
    for c in range(3):
        mean = (inner(1 + 2 * c) + inner(2 + 2 * c)) / most
        inner_means[c] = jnp.zeros((112, 128), F32)
        for par in range(2):
            for w in range(6):
                start = (2 + w) * 10 + 2 + par
                piece = mean[3 * w : 3 * w + 3, 128 * par : 128 * par + 128]
                inner_means[c, pl.ds(start, 3, stride=2), :] = piece
        high = high_part(mean)
        high_rows.append(high)
        low_rows.append(mean - high)
    high_rows.append(jnp.concatenate([own_axis[0, BORDER:56, :], own_axis[1, BORDER:56, :]], 1))
    table = jnp.concatenate(high_rows + low_rows, 0).astype(BF16)
    for b in range(1, 8):
        at = slice(8 * b, 8 * b + 8)
        looked = look_up_block(table, 24, col_s[at, :], row_s[at, :] - float(BORDER))
        for c in range(4):
            found[c, at, :] = looked[c]
    gone = starts[3] + counts[3]
    place = iota((ROWS, 128), 0) * 128 + iota((ROWS, 128), 1)
    ids[...] = jnp.where(place >= gone, ids[...], -1.0)
    for copy in copies:
        copy.wait()


def collide_kernel(
    shift_in, border, own_axis, ids, inner_means, found, vel, got_side, got_corner,
    out_hbm, flow_hbm,
    shift, out, flow, total, means, load_sem, store_sem,
):
    load = pltpu.make_async_copy(shift_in, shift, load_sem)
    load.start()
    total[0 : 8 * BORDER, :] = border[0 : 8 * BORDER, :]
    for k, places in enumerate(
        (
            ((24, 0, 2), (18, 2, 6), (16, 8, 2)),
            ((8, 0, 2), (2, 2, 6), (0, 8, 2)),
            ((16, 0, 2), (10, 2, 6), (8, 8, 2)),
            ((0, 0, 2), (26, 2, 6), (24, 8, 2)),
        )
    ):
        for mine, theirs, n in places:
            total[8 * mine : 8 * (mine + n), :] += got_side[k, 8 * theirs : 8 * (theirs + n), :]
    for k, mine in enumerate((16, 24, 8, 0)):
        total[8 * mine : 8 * mine + 16, :] += got_corner[k, 0:16, :]
    numbers = []
    for par in range(2):
        number = own_axis[par, 0:BORDER, :]
        at = 112 + 16 * par
        zero = jnp.zeros((16, 128), F32)
        for k, (before, after) in enumerate(((16, 0), (0, 16), (8, 8))):
            strip = got_side[k, at : at + 16, :]
            parts = [jnp.zeros((before, 128), F32)] * (before > 0) + [strip]
            parts += [jnp.zeros((after, 128), F32)] * (after > 0)
            number = number + jnp.concatenate(parts, 0)
        strip = got_side[3, at : at + 16, :]
        number = number + jnp.concatenate([strip[8:16], zero, strip[0:8]], 0)
        pair = [got_corner[k, 20 + 2 * par : 22 + 2 * par, :] for k in range(4)]
        gap = jnp.zeros((6, 128), F32)
        number = number + jnp.concatenate([pair[3], gap, pair[2], gap, pair[0], gap, pair[1], gap], 0)
        numbers.append(number)
    groups = [None] * 7
    most = [jnp.maximum(total[pl.ds(par, BORDER, stride=8), :], 1.0) for par in range(2)]
    border_mean = []
    for c in range(3):
        halves = [total[pl.ds(2 + 2 * c + par, BORDER, stride=8), :] / most[par] for par in range(2)]
        mean = jnp.concatenate(halves, 1)
        border_mean.append(mean)
        groups[c] = high_part(mean)
        groups[4 + c] = mean - groups[c]
    groups[3] = jnp.concatenate(numbers, 1)
    table = jnp.concatenate(groups, 0).astype(BF16)
    choices = axis_table()

    def turn(at, live, v, looked):
        mean = looked[:3]
        number = looked[3].astype(jnp.int32)
        bits = [(number & (1 << k)) != 0 for k in range(4)]
        a = []
        for c in range(2):
            level = [entry[c] for entry in choices]
            for k in range(4):
                level = [jnp.where(bits[k], level[2 * m + 1], level[2 * m]) for m in range(len(level) // 2)]
            a.append(level[0])
        a.append((1.0 - 1.0 / NAX) - (2.0 / NAX) * looked[3])
        w = [v[c] - mean[c] for c in range(3)]
        cross = [
            a[1] * w[2] - a[2] * w[1],
            a[2] * w[0] - a[0] * w[2],
            a[0] * w[1] - a[1] * w[0],
        ]
        along = (a[0] * w[0] + a[1] * w[1] + a[2] * w[2]) * (1.0 - COS_TURN)
        for c in range(3):
            turned = mean[c] + COS_TURN * w[c] + SIN_TURN * cross[c] + along * a[c]
            out[c, at, :] = jnp.where(live, turned, 0.0)

    slot = iota((8, 128), 0) * 128 + iota((8, 128), 1)
    arrived = []
    for k in (1, 0, 3, 2):
        v = [got_side[k, 80 + 8 * c : 88 + 8 * c, :] for c in range(4)]
        if k > 1:
            first, second = ((2, 0), (3, 1))[k - 2]
            n0 = jnp.sum((v[3] >= 0.0).astype(jnp.int32))
            n1 = jnp.sum((got_corner[first, 19:20, :] >= 0.0).astype(jnp.int32))
            in_first = (slot >= n0) & (slot < n0 + n1)
            in_second = (slot >= n0 + n1) & (slot < n0 + n1 + 128)
            by1, by2 = lax.rem(n0, 128), lax.rem(n0 + n1, 128)
            for c in range(4):
                at = slice(16 + c, 17 + c)
                one = pltpu.roll(jnp.broadcast_to(got_corner[first, at, :], (8, 128)), by1, 1)
                two = pltpu.roll(jnp.broadcast_to(got_corner[second, at, :], (8, 128)), by2, 1)
                v[c] = jnp.where(in_first, one, jnp.where(in_second, two, v[c]))
        arrived.append(v)

    out[:, 0:8, :] = jnp.zeros((3, 8, 128), F32)
    for b in range(1, 8):
        at = slice(8 * b, 8 * b + 8)
        block = ids[at, :]
        rows = jnp.floor(block * (1.0 / 256.0))
        looked = look_up_block(table, BORDER, block - rows * 256.0, rows)
        turn(at, block >= 0.0, [vel[c, at, :] for c in range(3)], [looked[c] + found[c, at, :] for c in range(4)])
    stores = []

    def store(source, target):
        copy = pltpu.make_async_copy(source, target, store_sem.at[len(stores)])
        copy.start()
        stores.append(copy)

    for v, at, window in zip(arrived, (64, 72, 80, 88), (0, 16, 24, 8)):
        rows = jnp.floor(v[3] * (1.0 / 256.0))
        cols = v[3] - rows * 256.0
        if window == 24:
            part = [jnp.concatenate([g[24:32], g[0:8]], 0) for g in groups]
            local = jnp.where(rows < 2.0, rows + 8.0, rows - 24.0)
        else:
            part = [g[window : window + 16] for g in groups]
            local = rows - float(window)
        looked = look_up_block(jnp.concatenate(part, 0).astype(BF16), 16, cols, local)
        turn(slice(at, at + 8), v[3] >= 0.0, v, looked)
    store(out, out_hbm)

    means[...] = inner_means[...]
    for c in range(3):
        for par in range(2):
            lanes = slice(par * 128, par * 128 + 128)
            for first, n, cx, cx_step, half_y, half_step in PIECES:
                if first >= BORDER:
                    continue
                piece = border_mean[c][first : first + n, lanes]
                start = cx * 10 + 2 * half_y + par
                means[c, pl.ds(start, n, stride=10 * cx_step + 2 * half_step), :] = piece
    load.wait()
    low_x = (shift[0] == 1).astype(jnp.int32)
    low_y = (shift[1] == 1).astype(jnp.int32)
    for c in range(3):
        for cx in range(CXL):
            flow[c, cx * 8 : cx * 8 + 8, :] = means[c, pl.ds((cx + low_x) * 10 + low_y, 8), :]
    store(flow, flow_hbm)
    for copy in stores:
        copy.wait()


def shape(*dims):
    return jax.ShapeDtypeStruct(dims, F32)


def per_device(velocity, position, leaving, grid_shift, axis_index):
    vel = velocity.reshape(3, ROWS, 128)
    pos = position.reshape(3, ROWS, 128)
    axis = axis_index.reshape(64, 128)
    leaving = leaving.reshape(4)
    vel, pos, axis, leaving, grid_shift = [
        pltpu.with_memory_space_constraint(v, pltpu.HBM) for v in (vel, pos, axis, leaving, grid_shift)
    ]
    vmem = pl.BlockSpec(memory_space=pltpu.VMEM)
    hbm = pl.BlockSpec(memory_space=pltpu.HBM)
    parts = pl.pallas_call(
        prep_kernel,
        name="prep",
        out_shape=(
            shape(8 * BORDER + 8, 128),
            shape(2, 56, 128),
            shape(ROWS, 128),
            shape(3, 112, 128),
            shape(4, ROWS, 128),
            shape(3, ROWS, 128),
            shape(4, 144, 128),
            shape(4, 24, 128),
        ),
        in_specs=[hbm] * 5,
        out_specs=(vmem,) * 8,
        scratch_shapes=[
            pltpu.SMEM((4,), jnp.int32),
            pltpu.SMEM((3,), jnp.int32),
            pltpu.VMEM((3, ROWS, 128), F32),
            pltpu.VMEM((64, 128), jnp.int32),
            pltpu.VMEM((ROWS, 128), F32),
            pltpu.VMEM((ROWS, 128), F32),
            pltpu.VMEM((7 * MAIN + 16, 256), F32),
            pltpu.VMEM((2, 136, 128), F32),
            pltpu.VMEM((32, 128), F32),
            pltpu.VMEM((144, 128), F32),
            pltpu.VMEM((4, 144, 128), F32),
            pltpu.VMEM((4, 24, 128), F32),
            pltpu.SemaphoreType.DMA((5,)),
            pltpu.SemaphoreType.DMA((8,)),
            pltpu.SemaphoreType.DMA((8,)),
        ],
        compiler_params=pltpu.CompilerParams(
            collective_id=0, has_side_effects=True, vmem_limit_bytes=32 << 20
        ),
    )(leaving, grid_shift, vel, pos, axis)
    out, flow = pl.pallas_call(
        collide_kernel,
        name="collide",
        out_shape=(shape(3, SLOTS, 128), shape(3, 64, 128)),
        in_specs=[hbm] + [vmem] * 8,
        out_specs=(hbm, hbm),
        scratch_shapes=[
            pltpu.SMEM((3,), jnp.int32),
            pltpu.VMEM((3, SLOTS, 128), F32),
            pltpu.VMEM((3, 64, 128), F32),
            pltpu.VMEM((8 * BORDER + 8, 128), F32),
            pltpu.VMEM((3, 112, 128), F32),
            pltpu.SemaphoreType.DMA,
            pltpu.SemaphoreType.DMA((3,)),
        ],
        compiler_params=pltpu.CompilerParams(vmem_limit_bytes=32 << 20),
    )(grid_shift, *parts)
    return out.reshape(3, 1, 1, SLOTS * 128), flow.reshape(3, 1, 1, 64 * 128)


def solution(mesh):
    return jax.shard_map(
        per_device,
        mesh=mesh,
        in_specs=(
            P(None, "gx", "gy", None),
            P(None, "gx", "gy", None),
            P("gx", "gy", None),
            P(),
            P("gx", "gy", None),
        ),
        out_specs=(P(None, "gx", "gy", None), P(None, "gx", "gy", None)),
        check_vma=False,
    )
```

```python
import math

import jax
import jax.numpy as jnp
from jax import lax
from jax.experimental import pallas as pl
from jax.experimental.pallas import tpu as pltpu
from jax.sharding import PartitionSpec as P

CXL = 8
CYL = 8
CZ = 128
NAX = 16
ROWS = 64
SLOTS = 96
BORDER = 32
INNER = 18
MAIN = 48

COS_TURN = -0.6427876096865393
SIN_TURN = 0.766044443118978
GOLDEN_TURN = 2.399963229728653

F32 = jnp.float32
BF16 = jnp.bfloat16
MESH = pl.DeviceIdType.MESH


def axis_table():
    table = []
    for number in range(NAX):
        height = 1.0 - (2.0 * number + 1.0) / NAX
        radius = math.sqrt(1.0 - height * height)
        phase = number * GOLDEN_TURN
        table.append((radius * math.cos(phase), radius * math.sin(phase), height))
    return table


def dot_nt(a, b):
    return lax.dot_general(a, b, (((1,), (1,)), ((), ())), preferred_element_type=F32)


def iota(shape, dim):
    return lax.broadcasted_iota(jnp.int32, shape, dim)


def iota16(shape, dim):
    return iota(shape, dim).astype(F32).astype(BF16)


def spread(row, height):
    return jnp.broadcast_to(row, (height, 128)).astype(BF16)


def one_hot(hit):
    return jnp.where(hit, jnp.ones(hit.shape, BF16), jnp.zeros(hit.shape, BF16))


def high_part(value):
    return value.astype(BF16).astype(F32)


PIECES = (
    [(0, 2, 0, 1, 0, 0), (8, 2, 0, 1, 4, 0), (16, 2, 8, 1, 4, 0), (24, 2, 8, 1, 0, 0)]
    + [(10, 6, 2, 1, 4, 0), (26, 6, 2, 1, 0, 0)]
    + [(2 + 3 * u, 3, u, 0, 1, 1) for u in range(2)]
    + [(18 + 3 * u, 3, 8 + u, 0, 1, 1) for u in range(2)]
    + [(32 + 3 * w, 3, 2 + w, 0, 1, 1) for w in range(6)]
)


def look_up(table, heights, groups, cols, local, j):
    col_of = iota16((256, 128), 0)
    row_of = iota((heights, 128), 0).astype(F32)
    hits = [one_hot(col_of == spread(cols[i : i + 1, :], 256)) for i in (j, j + 1)]
    both = jnp.dot(table, jnp.concatenate(hits, 1), preferred_element_type=F32)
    found = []
    for i in (0, 1):
        lanes = slice(i * 128, i * 128 + 128)
        hit = row_of == jnp.broadcast_to(local[j + i : j + i + 1, :], (heights, 128))
        row = []
        for c in range(4):
            part = both[heights * c : heights * (c + 1), lanes]
            if c < 3:
                part = part + both[heights * (4 + c) : heights * (5 + c), lanes]
            row.append(jnp.sum(jnp.where(hit, part, 0.0), axis=0, keepdims=True))
        found.append(row)
    return found


def look_up_block(table, heights, cols, local):
    found = []
    for j in range(0, 8, 2):
        found += look_up(table, heights, 7, cols, local, j)
    return [jnp.concatenate([row[c] for row in found], 0) for c in range(4)]


def neighbours():
    x, y = lax.axis_index("gx"), lax.axis_index("gy")
    nx, ny = lax.axis_size("gx"), lax.axis_size("gy")
    left, right = lax.rem(x + nx - 1, nx), lax.rem(x + 1, nx)
    down, up = lax.rem(y + ny - 1, ny), lax.rem(y + 1, ny)
    sides = [(left, y), (right, y), (x, down), (x, up)]
    corners = [(left, down), (left, up), (right, down), (right, up)]
    return sides + corners


def prep_kernel(
    leaving_in, shift_in, vel_in, pos_in, axis_in,
    border, own_axis, ids, inner_means, found, vel, got_side, got_corner,
    leaving, shift, pos, axis, row_s, col_s, sums, run_s, prep_s, axis_s, side, corner,
    load_sem, send_sem, recv_sem,
):
    loads = [
        pltpu.make_async_copy(source, target, load_sem.at[k])
        for k, (source, target) in enumerate(
            ((pos_in, pos), (shift_in, shift), (axis_in, axis), (vel_in, vel), (leaving_in, leaving))
        )
    ]
    for load in loads:
        load.start()
    targets = neighbours()
    barrier = pltpu.get_barrier_semaphore()
    for target in targets:
        pl.semaphore_signal(barrier, inc=1, device_id=target, device_id_type=MESH)
    axis_s[...] = jnp.zeros(axis_s.shape, F32)
    side[:, 112:144, :] = jnp.zeros((4, 32, 128), F32)
    for load in loads:
        load.wait()

    low_x = (shift[0] == 1).astype(jnp.int32)
    low_y = (shift[1] == 1).astype(jnp.int32)
    shifts = [shift[k].astype(F32) * 0.25 for k in range(3)]
    cell_x = jnp.floor(pos[0] + shifts[0]) + low_x.astype(F32)
    cell_y = jnp.floor(pos[1] + shifts[1]) + low_y.astype(F32)
    cell_z = jnp.floor(pos[2] + shifts[2])
    cell_z = jnp.where(cell_z >= float(CZ), cell_z - float(CZ), cell_z)
    half = jnp.floor(cell_y * 0.5)
    is_left = cell_x < 2.0
    is_right = cell_x > 7.0
    bottom = cell_x + jnp.where(is_left, 0.0, jnp.where(is_right, 16.0, 24.0))
    middle = 3.0 * cell_x + half + jnp.where(is_left, 1.0, jnp.where(is_right, -7.0, 25.0))
    row = jnp.where(half < 1.0, bottom, jnp.where(half > 3.0, cell_x + 8.0, middle))
    col = (cell_y - 2.0 * half) * float(CZ) + cell_z
    row_s[...] = row
    col_s[...] = col
    ids[...] = row * 256.0 + col

    row_of = iota16((MAIN, 128), 0)
    col_of = iota16((256, 128), 0)
    rest = iota((16, 128), 0)
    rest_row = (MAIN + rest % 2).astype(F32).astype(BF16)
    rest_is = [rest // 2 == g for g in range(7)]
    for chunk in range(8):
        left_parts = [[] for _ in range(8)]
        right_parts = []
        for j in range(8):
            r = chunk * 8 + j
            values = [jnp.ones((1, 128), F32)]
            for c in range(3):
                high = high_part(vel[c, r : r + 1, :])
                values += [high, vel[c, r : r + 1, :] - high]
            hit = row_of == spread(row_s[r : r + 1, :], MAIN)
            tail = jnp.broadcast_to(values[0], (16, 128))
            for g in range(7):
                wide = spread(values[g], MAIN)
                left_parts[g].append(jnp.where(hit, wide, jnp.zeros((MAIN, 128), BF16)))
                if g:
                    tail = jnp.where(rest_is[g], jnp.broadcast_to(values[g], (16, 128)), tail)
            hit = rest_row == spread(row_s[r : r + 1, :], 16)
            left_parts[7].append(jnp.where(hit, tail.astype(BF16), jnp.zeros((16, 128), BF16)))
            right_parts.append(one_hot(col_of == spread(col_s[r : r + 1, :], 256)))
        part = dot_nt(
            jnp.concatenate([jnp.concatenate(p, 1) for p in left_parts], 0),
            jnp.concatenate(right_parts, 1),
        )
        if chunk == 0:
            sums[...] = part
        else:
            sums[...] += part
    for c in range(4):
        if c == 0:
            group = sums[0:BORDER, :]
        else:
            at = (2 * c - 1) * MAIN
            group = sums[at : at + BORDER, :] + sums[at + MAIN : at + MAIN + BORDER, :]
        for par in range(2):
            lanes = slice(par * 128, par * 128 + 128)
            border[pl.ds(2 * c + par, BORDER, stride=8), :] = group[:, lanes]
    for k, start in enumerate((0, 16, 24, 8)):
        if start == 24:
            side[k, 0:64, :] = border[192:256, :]
            side[k, 64:80, :] = border[0:16, :]
        else:
            side[k, 0:80, :] = border[8 * start : 8 * start + 80, :]
    for k, start in enumerate((0, 8, 24, 16)):
        corner[k, 0:16, :] = border[8 * start : 8 * start + 16, :]

    for cx in range(CXL):
        at = (cx + 1) * 11 + 1
        axis_s[at : at + 8, :] = axis[cx * 8 : cx * 8 + 8, :].astype(F32)
    for par in range(2):
        for first, n, cx, cx_step, half_y, half_step in PIECES:
            start = (cx + 1 - low_x) * 11 + 2 * half_y + par + 1 - low_y
            step = 11 * cx_step + 2 * half_step
            own_axis[par, first : first + n, :] = axis_s[pl.ds(start, n, stride=step), :]
        own_axis[par, 50:56, :] = jnp.zeros((6, 128), F32)
        base = 112 + 16 * par
        for k, order in enumerate(
            (((8, 2), (2, 6), (0, 2)), ((24, 2), (18, 6), (16, 2)), ((0, 2), (26, 6), (24, 2)), ((16, 2), (10, 6), (8, 2)))
        ):
            at = base
            for first, n in order:
                side[k, at : at + n, :] = own_axis[par, first : first + n, :]
                at += n
        for k, first in enumerate((0, 8, 24, 16)):
            corner[k, 20 + 2 * par : 22 + 2 * par, :] = own_axis[par, first : first + 2, :]

    slot = iota((8, 128), 0) * 128 + iota((8, 128), 1)
    lane = iota((8, 128), 1)
    counts = [leaving[k] for k in range(4)]
    starts = [jnp.int32(0), counts[0], counts[0] + counts[1], counts[0] + counts[1] + counts[2]]

    def run(load, d):
        if d == 0:
            return load(0)
        q = starts[d] // 128
        r = starts[d] - q * 128
        back = jnp.where(r == 0, 0, 128 - r)
        here = pltpu.roll(load(q), back, 1)
        after = pltpu.roll(load(q + 1), back, 1)
        return jnp.where(lane < 128 - r, here, after)

    def moved(d, run_row):
        if d == 0:
            return run_row + jnp.where(run_row < 2.0, 24.0, jnp.where(run_row < 8.0, 16.0, 8.0))
        if d == 1:
            return run_row - jnp.where(run_row < 18.0, 8.0, jnp.where(run_row < 24.0, 16.0, 24.0))
        if d == 2:
            return run_row + jnp.where(run_row < 2.0, 8.0, jnp.where(run_row < 26.0, -8.0, -16.0))
        return run_row + jnp.where(run_row < 10.0, -8.0, jnp.where(run_row < 16.0, 16.0, 8.0))

    flags = []
    for d in range(4):
        live = slot < counts[d]
        values = [run(lambda q, c=c: vel[c, pl.ds(q, 8), :], d) for c in range(3)]
        run_row = run(lambda q: row_s[pl.ds(q, 8), :], d)
        run_col = run(lambda q: col_s[pl.ds(q, 8), :], d)
        kept = live
        if d < 2:
            y = run(lambda q: pos[1, pl.ds(q, 8), :], d)
            down = live & (y < 0.0)
            up = live & (y >= float(CYL))
            kept = live & (y >= 0.0) & (y < float(CYL))
            flags += [down, up]
            for c in range(3):
                high = high_part(values[c])
                run_s[d, 16 * c : 16 * c + 8, :] = high
                run_s[d, 16 * c + 8 : 16 * c + 16, :] = values[c] - high
            run_s[d, 48:56, :] = run_row
            run_s[d, 56:64, :] = run_col
            run_s[d, 64:72, :] = jnp.ones((8, 128), F32)
            run_s[d, 72:128, :] = jnp.zeros((56, 128), F32)
        for c in range(3):
            side[d, 80 + 8 * c : 88 + 8 * c, :] = values[c]
        side[d, 104:112, :] = jnp.where(kept, moved(d, run_row) * 256.0 + run_col, -1.0)

    flag = jnp.concatenate([f.astype(F32) for f in flags], 0)
    flag16 = flag.astype(BF16)
    before = (iota((128, 128), 0) < iota((128, 128), 1)).astype(F32).astype(BF16)
    inside = jnp.dot(flag16, before, preferred_element_type=F32)
    total = jnp.dot(flag16, jnp.ones((128, 128), BF16), preferred_element_type=F32)
    r0, r1 = iota((32, 32), 0), iota((32, 32), 1)
    earlier = ((r1 < r0) & (r0 // 8 == r1 // 8)).astype(F32).astype(BF16)
    offset = jnp.dot(earlier, total.astype(BF16), preferred_element_type=F32)
    prep_s[...] = jnp.where(flag > 0.0, inside + offset, -1.0)
    rank_of = iota16((128, 128), 0)
    for d in range(2):
        rows = jnp.concatenate([run_s[d, pl.ds(r, 16, stride=8), :] for r in range(8)], 1).astype(BF16)
        for s in range(2):
            at = d * 16 + s * 8
            hits = [one_hot(rank_of == spread(prep_s[at + r : at + r + 1, :], 128)) for r in range(8)]
            packed = dot_nt(rows, jnp.concatenate(hits, 1))
            k = d * 2 + s
            for c in range(3):
                corner[k, 16 + c : 17 + c, :] = packed[2 * c : 2 * c + 1] + packed[2 * c + 1 : 2 * c + 2]
            there = (packed[6:7] + (16.0 - 32.0 * d)) * 256.0 + packed[7:8]
            corner[k, 19:20, :] = jnp.where(packed[8:9] > 0.5, there, -1.0)

    pl.semaphore_wait(barrier, 8)
    copies = []
    for k in (4, 5, 6, 7, 0, 1, 2, 3):
        source, target = (side.at[k], got_side.at[k]) if k < 4 else (corner.at[k - 4], got_corner.at[k - 4])
        copy = pltpu.make_async_remote_copy(
            src_ref=source,
            dst_ref=target,
            send_sem=send_sem.at[k],
            recv_sem=recv_sem.at[k],
            device_id=targets[k],
            device_id_type=MESH,
        )
        copy.start()
        copies.append(copy)

    def inner(group):
        at = group * MAIN + BORDER
        end = 7 * MAIN + 2 * group
        return jnp.concatenate([sums[at : at + 16, :], sums[end : end + 2, :], jnp.zeros((6, 256), F32)], 0)

    most = jnp.maximum(inner(0), 1.0)
    high_rows, low_rows = [], []
    for c in range(3):
        mean = (inner(1 + 2 * c) + inner(2 + 2 * c)) / most
        inner_means[c] = jnp.zeros((112, 128), F32)
        for par in range(2):
            for w in range(6):
                start = (2 + w) * 10 + 2 + par
                piece = mean[3 * w : 3 * w + 3, 128 * par : 128 * par + 128]
                inner_means[c, pl.ds(start, 3, stride=2), :] = piece
        high = high_part(mean)
        high_rows.append(high)
        low_rows.append(mean - high)
    high_rows.append(jnp.concatenate([own_axis[0, BORDER:56, :], own_axis[1, BORDER:56, :]], 1))
    table = jnp.concatenate(high_rows + low_rows, 0).astype(BF16)
    for b in range(1, 8):
        at = slice(8 * b, 8 * b + 8)
        looked = look_up_block(table, 24, col_s[at, :], row_s[at, :] - float(BORDER))
        for c in range(4):
            found[c, at, :] = looked[c]
    gone = starts[3] + counts[3]
    place = iota((ROWS, 128), 0) * 128 + iota((ROWS, 128), 1)
    ids[...] = jnp.where(place >= gone, ids[...], -1.0)
    for copy in copies:
        copy.wait_send()
    for copy in copies[4:] + copies[:4]:
        copy.wait_recv()


def collide_kernel(
    shift_in, border, own_axis, ids, inner_means, found, vel, got_side, got_corner,
    out_hbm, flow_hbm,
    shift, out, flow, total, means, load_sem, store_sem,
):
    load = pltpu.make_async_copy(shift_in, shift, load_sem)
    load.start()
    total[0 : 8 * BORDER, :] = border[0 : 8 * BORDER, :]
    for k, places in enumerate(
        (
            ((24, 0, 2), (18, 2, 6), (16, 8, 2)),
            ((8, 0, 2), (2, 2, 6), (0, 8, 2)),
            ((16, 0, 2), (10, 2, 6), (8, 8, 2)),
            ((0, 0, 2), (26, 2, 6), (24, 8, 2)),
        )
    ):
        for mine, theirs, n in places:
            total[8 * mine : 8 * (mine + n), :] += got_side[k, 8 * theirs : 8 * (theirs + n), :]
    for k, mine in enumerate((16, 24, 8, 0)):
        total[8 * mine : 8 * mine + 16, :] += got_corner[k, 0:16, :]
    numbers = []
    for par in range(2):
        number = own_axis[par, 0:BORDER, :]
        at = 112 + 16 * par
        zero = jnp.zeros((16, 128), F32)
        for k, (before, after) in enumerate(((16, 0), (0, 16), (8, 8))):
            strip = got_side[k, at : at + 16, :]
            parts = [jnp.zeros((before, 128), F32)] * (before > 0) + [strip]
            parts += [jnp.zeros((after, 128), F32)] * (after > 0)
            number = number + jnp.concatenate(parts, 0)
        strip = got_side[3, at : at + 16, :]
        number = number + jnp.concatenate([strip[8:16], zero, strip[0:8]], 0)
        pair = [got_corner[k, 20 + 2 * par : 22 + 2 * par, :] for k in range(4)]
        gap = jnp.zeros((6, 128), F32)
        number = number + jnp.concatenate([pair[3], gap, pair[2], gap, pair[0], gap, pair[1], gap], 0)
        numbers.append(number)
    groups = [None] * 7
    most = [jnp.maximum(total[pl.ds(par, BORDER, stride=8), :], 1.0) for par in range(2)]
    border_mean = []
    for c in range(3):
        halves = [total[pl.ds(2 + 2 * c + par, BORDER, stride=8), :] / most[par] for par in range(2)]
        mean = jnp.concatenate(halves, 1)
        border_mean.append(mean)
        groups[c] = high_part(mean)
        groups[4 + c] = mean - groups[c]
    groups[3] = jnp.concatenate(numbers, 1)
    table = jnp.concatenate(groups, 0).astype(BF16)
    choices = axis_table()

    def turn(at, live, v, looked):
        mean = looked[:3]
        number = looked[3].astype(jnp.int32)
        bits = [(number & (1 << k)) != 0 for k in range(4)]
        a = []
        for c in range(2):
            level = [entry[c] for entry in choices]
            for k in range(4):
                level = [jnp.where(bits[k], level[2 * m + 1], level[2 * m]) for m in range(len(level) // 2)]
            a.append(level[0])
        a.append((1.0 - 1.0 / NAX) - (2.0 / NAX) * looked[3])
        w = [v[c] - mean[c] for c in range(3)]
        cross = [
            a[1] * w[2] - a[2] * w[1],
            a[2] * w[0] - a[0] * w[2],
            a[0] * w[1] - a[1] * w[0],
        ]
        along = (a[0] * w[0] + a[1] * w[1] + a[2] * w[2]) * (1.0 - COS_TURN)
        for c in range(3):
            turned = mean[c] + COS_TURN * w[c] + SIN_TURN * cross[c] + along * a[c]
            out[c, at, :] = jnp.where(live, turned, 0.0)

    slot = iota((8, 128), 0) * 128 + iota((8, 128), 1)
    arrived = []
    for k in (1, 0, 3, 2):
        v = [got_side[k, 80 + 8 * c : 88 + 8 * c, :] for c in range(4)]
        if k > 1:
            first, second = ((2, 0), (3, 1))[k - 2]
            n0 = jnp.sum((v[3] >= 0.0).astype(jnp.int32))
            n1 = jnp.sum((got_corner[first, 19:20, :] >= 0.0).astype(jnp.int32))
            in_first = (slot >= n0) & (slot < n0 + n1)
            in_second = (slot >= n0 + n1) & (slot < n0 + n1 + 128)
            by1, by2 = lax.rem(n0, 128), lax.rem(n0 + n1, 128)
            for c in range(4):
                at = slice(16 + c, 17 + c)
                one = pltpu.roll(jnp.broadcast_to(got_corner[first, at, :], (8, 128)), by1, 1)
                two = pltpu.roll(jnp.broadcast_to(got_corner[second, at, :], (8, 128)), by2, 1)
                v[c] = jnp.where(in_first, one, jnp.where(in_second, two, v[c]))
        arrived.append(v)

    out[:, 0:8, :] = jnp.zeros((3, 8, 128), F32)
    for b in range(1, 8):
        at = slice(8 * b, 8 * b + 8)
        block = ids[at, :]
        rows = jnp.floor(block * (1.0 / 256.0))
        looked = look_up_block(table, BORDER, block - rows * 256.0, rows)
        turn(at, block >= 0.0, [vel[c, at, :] for c in range(3)], [looked[c] + found[c, at, :] for c in range(4)])
    stores = []

    def store(source, target):
        copy = pltpu.make_async_copy(source, target, store_sem.at[len(stores)])
        copy.start()
        stores.append(copy)

    for v, at, window in zip(arrived, (64, 72, 80, 88), (0, 16, 24, 8)):
        rows = jnp.floor(v[3] * (1.0 / 256.0))
        cols = v[3] - rows * 256.0
        if window == 24:
            part = [jnp.concatenate([g[24:32], g[0:8]], 0) for g in groups]
            local = jnp.where(rows < 2.0, rows + 8.0, rows - 24.0)
        else:
            part = [g[window : window + 16] for g in groups]
            local = rows - float(window)
        looked = look_up_block(jnp.concatenate(part, 0).astype(BF16), 16, cols, local)
        turn(slice(at, at + 8), v[3] >= 0.0, v, looked)
    store(out, out_hbm)

    means[...] = inner_means[...]
    for c in range(3):
        for par in range(2):
            lanes = slice(par * 128, par * 128 + 128)
            for first, n, cx, cx_step, half_y, half_step in PIECES:
                if first >= BORDER:
                    continue
                piece = border_mean[c][first : first + n, lanes]
                start = cx * 10 + 2 * half_y + par
                means[c, pl.ds(start, n, stride=10 * cx_step + 2 * half_step), :] = piece
    load.wait()
    low_x = (shift[0] == 1).astype(jnp.int32)
    low_y = (shift[1] == 1).astype(jnp.int32)
    for c in range(3):
        for cx in range(CXL):
            flow[c, cx * 8 : cx * 8 + 8, :] = means[c, pl.ds((cx + low_x) * 10 + low_y, 8), :]
    store(flow, flow_hbm)
    for copy in stores:
        copy.wait()


def shape(*dims):
    return jax.ShapeDtypeStruct(dims, F32)


def per_device(velocity, position, leaving, grid_shift, axis_index):
    vel = velocity.reshape(3, ROWS, 128)
    pos = position.reshape(3, ROWS, 128)
    axis = axis_index.reshape(64, 128)
    leaving = leaving.reshape(4)
    vel, pos, axis, leaving, grid_shift = [
        pltpu.with_memory_space_constraint(v, pltpu.HBM) for v in (vel, pos, axis, leaving, grid_shift)
    ]
    vmem = pl.BlockSpec(memory_space=pltpu.VMEM)
    hbm = pl.BlockSpec(memory_space=pltpu.HBM)
    parts = pl.pallas_call(
        prep_kernel,
        name="prep",
        out_shape=(
            shape(8 * BORDER + 8, 128),
            shape(2, 56, 128),
            shape(ROWS, 128),
            shape(3, 112, 128),
            shape(4, ROWS, 128),
            shape(3, ROWS, 128),
            shape(4, 144, 128),
            shape(4, 24, 128),
        ),
        in_specs=[hbm] * 5,
        out_specs=(vmem,) * 8,
        scratch_shapes=[
            pltpu.SMEM((4,), jnp.int32),
            pltpu.SMEM((3,), jnp.int32),
            pltpu.VMEM((3, ROWS, 128), F32),
            pltpu.VMEM((64, 128), jnp.int32),
            pltpu.VMEM((ROWS, 128), F32),
            pltpu.VMEM((ROWS, 128), F32),
            pltpu.VMEM((7 * MAIN + 16, 256), F32),
            pltpu.VMEM((2, 136, 128), F32),
            pltpu.VMEM((32, 128), F32),
            pltpu.VMEM((144, 128), F32),
            pltpu.VMEM((4, 144, 128), F32),
            pltpu.VMEM((4, 24, 128), F32),
            pltpu.SemaphoreType.DMA((5,)),
            pltpu.SemaphoreType.DMA((8,)),
            pltpu.SemaphoreType.DMA((8,)),
        ],
        compiler_params=pltpu.CompilerParams(
            collective_id=0, has_side_effects=True, vmem_limit_bytes=32 << 20
        ),
    )(leaving, grid_shift, vel, pos, axis)
    out, flow = pl.pallas_call(
        collide_kernel,
        name="collide",
        out_shape=(shape(3, SLOTS, 128), shape(3, 64, 128)),
        in_specs=[hbm] + [vmem] * 8,
        out_specs=(hbm, hbm),
        scratch_shapes=[
            pltpu.SMEM((3,), jnp.int32),
            pltpu.VMEM((3, SLOTS, 128), F32),
            pltpu.VMEM((3, 64, 128), F32),
            pltpu.VMEM((8 * BORDER + 8, 128), F32),
            pltpu.VMEM((3, 112, 128), F32),
            pltpu.SemaphoreType.DMA,
            pltpu.SemaphoreType.DMA((3,)),
        ],
        compiler_params=pltpu.CompilerParams(vmem_limit_bytes=32 << 20),
    )(grid_shift, *parts)
    return out.reshape(3, 1, 1, SLOTS * 128), flow.reshape(3, 1, 1, 64 * 128)


def solution(mesh):
    return jax.shard_map(
        per_device,
        mesh=mesh,
        in_specs=(
            P(None, "gx", "gy", None),
            P(None, "gx", "gy", None),
            P("gx", "gy", None),
            P(),
            P("gx", "gy", None),
        ),
        out_specs=(P(None, "gx", "gy", None), P(None, "gx", "gy", None)),
        check_vma=False,
    )
```

```python
import math

import jax
import jax.numpy as jnp
from jax import lax
from jax.experimental import pallas as pl
from jax.experimental.pallas import tpu as pltpu
from jax.sharding import PartitionSpec as P

CXL = 8
CYL = 8
CZ = 128
NAX = 16
ROWS = 64
SLOTS = 96
BORDER = 32
INNER = 18
MAIN = 48

COS_TURN = -0.6427876096865393
SIN_TURN = 0.766044443118978
GOLDEN_TURN = 2.399963229728653

F32 = jnp.float32
BF16 = jnp.bfloat16
MESH = pl.DeviceIdType.MESH


def axis_table():
    table = []
    for number in range(NAX):
        height = 1.0 - (2.0 * number + 1.0) / NAX
        radius = math.sqrt(1.0 - height * height)
        phase = number * GOLDEN_TURN
        table.append((radius * math.cos(phase), radius * math.sin(phase), height))
    return table


def dot_nt(a, b):
    return lax.dot_general(a, b, (((1,), (1,)), ((), ())), preferred_element_type=F32)


def iota(shape, dim):
    return lax.broadcasted_iota(jnp.int32, shape, dim)


def iota16(shape, dim):
    return iota(shape, dim).astype(F32).astype(BF16)


def spread(row, height):
    return jnp.broadcast_to(row, (height, 128)).astype(BF16)


def one_hot(hit):
    return jnp.where(hit, jnp.ones(hit.shape, BF16), jnp.zeros(hit.shape, BF16))


def high_part(value):
    return value.astype(BF16).astype(F32)


PIECES = (
    [(0, 2, 0, 1, 0, 0), (8, 2, 0, 1, 4, 0), (16, 2, 8, 1, 4, 0), (24, 2, 8, 1, 0, 0)]
    + [(10, 6, 2, 1, 4, 0), (26, 6, 2, 1, 0, 0)]
    + [(2 + 3 * u, 3, u, 0, 1, 1) for u in range(2)]
    + [(18 + 3 * u, 3, 8 + u, 0, 1, 1) for u in range(2)]
    + [(32 + 3 * w, 3, 2 + w, 0, 1, 1) for w in range(6)]
)


def look_up(table, heights, groups, cols, local, j):
    col_of = iota16((256, 128), 0)
    row_of = iota((heights, 128), 0).astype(F32)
    hits = [one_hot(col_of == spread(cols[i : i + 1, :], 256)) for i in (j, j + 1)]
    both = jnp.dot(table, jnp.concatenate(hits, 1), preferred_element_type=F32)
    found = []
    for i in (0, 1):
        lanes = slice(i * 128, i * 128 + 128)
        hit = row_of == jnp.broadcast_to(local[j + i : j + i + 1, :], (heights, 128))
        row = []
        for c in range(4):
            part = both[heights * c : heights * (c + 1), lanes]
            if c < 3:
                part = part + both[heights * (4 + c) : heights * (5 + c), lanes]
            row.append(jnp.sum(jnp.where(hit, part, 0.0), axis=0, keepdims=True))
        found.append(row)
    return found


def look_up_block(table, heights, cols, local):
    found = []
    for j in range(0, 8, 2):
        found += look_up(table, heights, 7, cols, local, j)
    return [jnp.concatenate([row[c] for row in found], 0) for c in range(4)]


def neighbours():
    x, y = lax.axis_index("gx"), lax.axis_index("gy")
    nx, ny = lax.axis_size("gx"), lax.axis_size("gy")
    left, right = lax.rem(x + nx - 1, nx), lax.rem(x + 1, nx)
    down, up = lax.rem(y + ny - 1, ny), lax.rem(y + 1, ny)
    sides = [(left, y), (right, y), (x, down), (x, up)]
    corners = [(left, down), (left, up), (right, down), (right, up)]
    return sides + corners


def prep_kernel(
    leaving_in, shift_in, vel_in, pos_in, axis_in,
    border, own_axis, ids, inner_means, found, vel, got_side, got_corner,
    leaving, shift, pos, axis, row_s, col_s, sums, run_s, prep_s, axis_s, side, corner,
    load_sem, send_sem, recv_sem,
):
    loads = [
        pltpu.make_async_copy(source, target, load_sem.at[k])
        for k, (source, target) in enumerate(
            ((pos_in, pos), (shift_in, shift), (axis_in, axis), (vel_in, vel), (leaving_in, leaving))
        )
    ]
    for load in loads:
        load.start()
    targets = neighbours()
    barrier = pltpu.get_barrier_semaphore()
    for target in targets:
        pl.semaphore_signal(barrier, inc=1, device_id=target, device_id_type=MESH)
    axis_s[...] = jnp.zeros(axis_s.shape, F32)
    for k in (0, 2):
        side[k, 112:144, :] = jnp.zeros((32, 128), F32)
    corner[:, 20:24, :] = jnp.zeros((4, 4, 128), F32)
    for load in loads:
        load.wait()

    low_x = (shift[0] == 1).astype(jnp.int32)
    low_y = (shift[1] == 1).astype(jnp.int32)
    shifts = [shift[k].astype(F32) * 0.25 for k in range(3)]
    cell_x = jnp.floor(pos[0] + shifts[0]) + low_x.astype(F32)
    cell_y = jnp.floor(pos[1] + shifts[1]) + low_y.astype(F32)
    cell_z = jnp.floor(pos[2] + shifts[2])
    cell_z = jnp.where(cell_z >= float(CZ), cell_z - float(CZ), cell_z)
    half = jnp.floor(cell_y * 0.5)
    is_left = cell_x < 2.0
    is_right = cell_x > 7.0
    bottom = cell_x + jnp.where(is_left, 0.0, jnp.where(is_right, 16.0, 24.0))
    middle = 3.0 * cell_x + half + jnp.where(is_left, 1.0, jnp.where(is_right, -7.0, 25.0))
    row = jnp.where(half < 1.0, bottom, jnp.where(half > 3.0, cell_x + 8.0, middle))
    col = (cell_y - 2.0 * half) * float(CZ) + cell_z
    row_s[...] = row
    col_s[...] = col
    ids[...] = row * 256.0 + col

    row_of = iota16((MAIN, 128), 0)
    col_of = iota16((256, 128), 0)
    rest = iota((16, 128), 0)
    rest_row = (MAIN + rest % 2).astype(F32).astype(BF16)
    rest_is = [rest // 2 == g for g in range(7)]
    for chunk in range(8):
        left_parts = [[] for _ in range(8)]
        right_parts = []
        for j in range(8):
            r = chunk * 8 + j
            values = [jnp.ones((1, 128), F32)]
            for c in range(3):
                high = high_part(vel[c, r : r + 1, :])
                values += [high, vel[c, r : r + 1, :] - high]
            hit = row_of == spread(row_s[r : r + 1, :], MAIN)
            tail = jnp.broadcast_to(values[0], (16, 128))
            for g in range(7):
                wide = spread(values[g], MAIN)
                left_parts[g].append(jnp.where(hit, wide, jnp.zeros((MAIN, 128), BF16)))
                if g:
                    tail = jnp.where(rest_is[g], jnp.broadcast_to(values[g], (16, 128)), tail)
            hit = rest_row == spread(row_s[r : r + 1, :], 16)
            left_parts[7].append(jnp.where(hit, tail.astype(BF16), jnp.zeros((16, 128), BF16)))
            right_parts.append(one_hot(col_of == spread(col_s[r : r + 1, :], 256)))
        part = dot_nt(
            jnp.concatenate([jnp.concatenate(p, 1) for p in left_parts], 0),
            jnp.concatenate(right_parts, 1),
        )
        if chunk == 0:
            sums[...] = part
        else:
            sums[...] += part
    for c in range(4):
        if c == 0:
            group = sums[0:BORDER, :]
        else:
            at = (2 * c - 1) * MAIN
            group = sums[at : at + BORDER, :] + sums[at + MAIN : at + MAIN + BORDER, :]
        for par in range(2):
            lanes = slice(par * 128, par * 128 + 128)
            border[pl.ds(2 * c + par, BORDER, stride=8), :] = group[:, lanes]
    for k, start in enumerate((0, 16, 24, 8)):
        if start == 24:
            side[k, 0:64, :] = border[192:256, :]
            side[k, 64:80, :] = border[0:16, :]
        else:
            side[k, 0:80, :] = border[8 * start : 8 * start + 80, :]
    for k, start in enumerate((0, 8, 24, 16)):
        corner[k, 0:16, :] = border[8 * start : 8 * start + 16, :]

    for cx in range(CXL):
        at = (cx + 1) * 11 + 1
        axis_s[at : at + 8, :] = axis[cx * 8 : cx * 8 + 8, :].astype(F32)
    for par in range(2):
        for first, n, cx, cx_step, half_y, half_step in PIECES:
            start = (cx + 1 - low_x) * 11 + 2 * half_y + par + 1 - low_y
            step = 11 * cx_step + 2 * half_step
            own_axis[par, first : first + n, :] = axis_s[pl.ds(start, n, stride=step), :]
        own_axis[par, 50:56, :] = jnp.zeros((6, 128), F32)
        base = 112 + 16 * par
        for k, order in ((0, ((8, 2), (2, 6), (0, 2))), (2, ((0, 2), (26, 6), (24, 2)))):
            at = base
            for first, n in order:
                side[k, at : at + n, :] = own_axis[par, first : first + n, :]
                at += n
        corner[0, 20 + 2 * par : 22 + 2 * par, :] = own_axis[par, 0:2, :]

    slot = iota((8, 128), 0) * 128 + iota((8, 128), 1)
    lane = iota((8, 128), 1)
    counts = [leaving[k] for k in range(4)]
    starts = [jnp.int32(0), counts[0], counts[0] + counts[1], counts[0] + counts[1] + counts[2]]

    def run(load, d):
        if d == 0:
            return load(0)
        q = starts[d] // 128
        r = starts[d] - q * 128
        back = jnp.where(r == 0, 0, 128 - r)
        here = pltpu.roll(load(q), back, 1)
        after = pltpu.roll(load(q + 1), back, 1)
        return jnp.where(lane < 128 - r, here, after)

    def moved(d, run_row):
        if d == 0:
            return run_row + jnp.where(run_row < 2.0, 24.0, jnp.where(run_row < 8.0, 16.0, 8.0))
        if d == 1:
            return run_row - jnp.where(run_row < 18.0, 8.0, jnp.where(run_row < 24.0, 16.0, 24.0))
        if d == 2:
            return run_row + jnp.where(run_row < 2.0, 8.0, jnp.where(run_row < 26.0, -8.0, -16.0))
        return run_row + jnp.where(run_row < 10.0, -8.0, jnp.where(run_row < 16.0, 16.0, 8.0))

    flags = []
    for d in range(4):
        live = slot < counts[d]
        values = [run(lambda q, c=c: vel[c, pl.ds(q, 8), :], d) for c in range(3)]
        run_row = run(lambda q: row_s[pl.ds(q, 8), :], d)
        run_col = run(lambda q: col_s[pl.ds(q, 8), :], d)
        kept = live
        if d < 2:
            y = run(lambda q: pos[1, pl.ds(q, 8), :], d)
            down = live & (y < 0.0)
            up = live & (y >= float(CYL))
            kept = live & (y >= 0.0) & (y < float(CYL))
            flags += [down, up]
            for c in range(3):
                high = high_part(values[c])
                run_s[d, 16 * c : 16 * c + 8, :] = high
                run_s[d, 16 * c + 8 : 16 * c + 16, :] = values[c] - high
            run_s[d, 48:56, :] = run_row
            run_s[d, 56:64, :] = run_col
            run_s[d, 64:72, :] = jnp.ones((8, 128), F32)
            run_s[d, 72:128, :] = jnp.zeros((56, 128), F32)
        for c in range(3):
            side[d, 80 + 8 * c : 88 + 8 * c, :] = values[c]
        side[d, 104:112, :] = jnp.where(kept, moved(d, run_row) * 256.0 + run_col, -1.0)

    flag = jnp.concatenate([f.astype(F32) for f in flags], 0)
    flag16 = flag.astype(BF16)
    before = (iota((128, 128), 0) < iota((128, 128), 1)).astype(F32).astype(BF16)
    inside = jnp.dot(flag16, before, preferred_element_type=F32)
    total = jnp.dot(flag16, jnp.ones((128, 128), BF16), preferred_element_type=F32)
    r0, r1 = iota((32, 32), 0), iota((32, 32), 1)
    earlier = ((r1 < r0) & (r0 // 8 == r1 // 8)).astype(F32).astype(BF16)
    offset = jnp.dot(earlier, total.astype(BF16), preferred_element_type=F32)
    prep_s[...] = jnp.where(flag > 0.0, inside + offset, -1.0)
    rank_of = iota16((128, 128), 0)
    for d in range(2):
        rows = jnp.concatenate([run_s[d, pl.ds(r, 16, stride=8), :] for r in range(8)], 1).astype(BF16)
        for s in range(2):
            at = d * 16 + s * 8
            hits = [one_hot(rank_of == spread(prep_s[at + r : at + r + 1, :], 128)) for r in range(8)]
            packed = dot_nt(rows, jnp.concatenate(hits, 1))
            k = d * 2 + s
            for c in range(3):
                corner[k, 16 + c : 17 + c, :] = packed[2 * c : 2 * c + 1] + packed[2 * c + 1 : 2 * c + 2]
            there = (packed[6:7] + (16.0 - 32.0 * d)) * 256.0 + packed[7:8]
            corner[k, 19:20, :] = jnp.where(packed[8:9] > 0.5, there, -1.0)

    pl.semaphore_wait(barrier, 8)
    copies = []
    for k in (4, 5, 6, 7, 0, 1, 2, 3):
        if k < 4:
            size = 144 if k in (0, 2) else 112
            source, target = side.at[k, pl.ds(0, size), :], got_side.at[k, pl.ds(0, size), :]
        else:
            source, target = corner.at[k - 4], got_corner.at[k - 4]
        copy = pltpu.make_async_remote_copy(
            src_ref=source,
            dst_ref=target,
            send_sem=send_sem.at[k],
            recv_sem=recv_sem.at[k],
            device_id=targets[k],
            device_id_type=MESH,
        )
        copy.start()
        copies.append(copy)

    def inner(group):
        at = group * MAIN + BORDER
        end = 7 * MAIN + 2 * group
        return jnp.concatenate([sums[at : at + 16, :], sums[end : end + 2, :], jnp.zeros((6, 256), F32)], 0)

    most = jnp.maximum(inner(0), 1.0)
    high_rows, low_rows = [], []
    for c in range(3):
        mean = (inner(1 + 2 * c) + inner(2 + 2 * c)) / most
        inner_means[c] = jnp.zeros((112, 128), F32)
        for par in range(2):
            for w in range(6):
                start = (2 + w) * 10 + 2 + par
                piece = mean[3 * w : 3 * w + 3, 128 * par : 128 * par + 128]
                inner_means[c, pl.ds(start, 3, stride=2), :] = piece
        high = high_part(mean)
        high_rows.append(high)
        low_rows.append(mean - high)
    high_rows.append(jnp.concatenate([own_axis[0, BORDER:56, :], own_axis[1, BORDER:56, :]], 1))
    table = jnp.concatenate(high_rows + low_rows, 0).astype(BF16)
    for b in range(1, 8):
        at = slice(8 * b, 8 * b + 8)
        looked = look_up_block(table, 24, col_s[at, :], row_s[at, :] - float(BORDER))
        for c in range(4):
            found[c, at, :] = looked[c]
    gone = starts[3] + counts[3]
    place = iota((ROWS, 128), 0) * 128 + iota((ROWS, 128), 1)
    ids[...] = jnp.where(place >= gone, ids[...], -1.0)
    for copy in copies:
        copy.wait()


def collide_kernel(
    shift_in, border, own_axis, ids, inner_means, found, vel, got_side, got_corner,
    out_hbm, flow_hbm,
    shift, out, flow, total, means, load_sem, store_sem,
):
    load = pltpu.make_async_copy(shift_in, shift, load_sem)
    load.start()
    total[0 : 8 * BORDER, :] = border[0 : 8 * BORDER, :]
    for k, places in enumerate(
        (
            ((24, 0, 2), (18, 2, 6), (16, 8, 2)),
            ((8, 0, 2), (2, 2, 6), (0, 8, 2)),
            ((16, 0, 2), (10, 2, 6), (8, 8, 2)),
            ((0, 0, 2), (26, 2, 6), (24, 8, 2)),
        )
    ):
        for mine, theirs, n in places:
            total[8 * mine : 8 * (mine + n), :] += got_side[k, 8 * theirs : 8 * (theirs + n), :]
    for k, mine in enumerate((16, 24, 8, 0)):
        total[8 * mine : 8 * mine + 16, :] += got_corner[k, 0:16, :]
    numbers = []
    for par in range(2):
        number = own_axis[par, 0:BORDER, :]
        at = 112 + 16 * par
        gap = jnp.zeros((16, 128), F32)
        number = number + jnp.concatenate([gap, got_side[0, at : at + 16, :]], 0)
        number = number + jnp.concatenate([gap[0:8], got_side[2, at : at + 16, :], gap[0:8]], 0)
        pair = got_corner[0, 20 + 2 * par : 22 + 2 * par, :]
        number = number + jnp.concatenate([gap, pair, gap[0:14]], 0)
        numbers.append(number)
    groups = [None] * 7
    most = [jnp.maximum(total[pl.ds(par, BORDER, stride=8), :], 1.0) for par in range(2)]
    border_mean = []
    for c in range(3):
        halves = [total[pl.ds(2 + 2 * c + par, BORDER, stride=8), :] / most[par] for par in range(2)]
        mean = jnp.concatenate(halves, 1)
        border_mean.append(mean)
        groups[c] = high_part(mean)
        groups[4 + c] = mean - groups[c]
    groups[3] = jnp.concatenate(numbers, 1)
    table = jnp.concatenate(groups, 0).astype(BF16)
    choices = axis_table()

    def turn(at, live, v, looked):
        mean = looked[:3]
        number = looked[3].astype(jnp.int32)
        bits = [(number & (1 << k)) != 0 for k in range(4)]
        a = []
        for c in range(2):
            level = [entry[c] for entry in choices]
            for k in range(4):
                level = [jnp.where(bits[k], level[2 * m + 1], level[2 * m]) for m in range(len(level) // 2)]
            a.append(level[0])
        a.append((1.0 - 1.0 / NAX) - (2.0 / NAX) * looked[3])
        w = [v[c] - mean[c] for c in range(3)]
        cross = [
            a[1] * w[2] - a[2] * w[1],
            a[2] * w[0] - a[0] * w[2],
            a[0] * w[1] - a[1] * w[0],
        ]
        along = (a[0] * w[0] + a[1] * w[1] + a[2] * w[2]) * (1.0 - COS_TURN)
        for c in range(3):
            turned = mean[c] + COS_TURN * w[c] + SIN_TURN * cross[c] + along * a[c]
            out[c, at, :] = jnp.where(live, turned, 0.0)

    slot = iota((8, 128), 0) * 128 + iota((8, 128), 1)
    arrived = []
    for k in (1, 0, 3, 2):
        v = [got_side[k, 80 + 8 * c : 88 + 8 * c, :] for c in range(4)]
        if k > 1:
            first, second = ((2, 0), (3, 1))[k - 2]
            n0 = jnp.sum((v[3] >= 0.0).astype(jnp.int32))
            n1 = jnp.sum((got_corner[first, 19:20, :] >= 0.0).astype(jnp.int32))
            in_first = (slot >= n0) & (slot < n0 + n1)
            in_second = (slot >= n0 + n1) & (slot < n0 + n1 + 128)
            by1, by2 = lax.rem(n0, 128), lax.rem(n0 + n1, 128)
            for c in range(4):
                at = slice(16 + c, 17 + c)
                one = pltpu.roll(jnp.broadcast_to(got_corner[first, at, :], (8, 128)), by1, 1)
                two = pltpu.roll(jnp.broadcast_to(got_corner[second, at, :], (8, 128)), by2, 1)
                v[c] = jnp.where(in_first, one, jnp.where(in_second, two, v[c]))
        arrived.append(v)

    out[:, 0:8, :] = jnp.zeros((3, 8, 128), F32)
    for b in range(1, 8):
        at = slice(8 * b, 8 * b + 8)
        block = ids[at, :]
        rows = jnp.floor(block * (1.0 / 256.0))
        looked = look_up_block(table, BORDER, block - rows * 256.0, rows)
        turn(at, block >= 0.0, [vel[c, at, :] for c in range(3)], [looked[c] + found[c, at, :] for c in range(4)])
    stores = []

    def store(source, target):
        copy = pltpu.make_async_copy(source, target, store_sem.at[len(stores)])
        copy.start()
        stores.append(copy)

    for v, at, window in zip(arrived, (64, 72, 80, 88), (0, 16, 24, 8)):
        rows = jnp.floor(v[3] * (1.0 / 256.0))
        cols = v[3] - rows * 256.0
        if window == 24:
            part = [jnp.concatenate([g[24:32], g[0:8]], 0) for g in groups]
            local = jnp.where(rows < 2.0, rows + 8.0, rows - 24.0)
        else:
            part = [g[window : window + 16] for g in groups]
            local = rows - float(window)
        looked = look_up_block(jnp.concatenate(part, 0).astype(BF16), 16, cols, local)
        turn(slice(at, at + 8), v[3] >= 0.0, v, looked)
    store(out, out_hbm)

    means[...] = inner_means[...]
    for c in range(3):
        for par in range(2):
            lanes = slice(par * 128, par * 128 + 128)
            for first, n, cx, cx_step, half_y, half_step in PIECES:
                if first >= BORDER:
                    continue
                piece = border_mean[c][first : first + n, lanes]
                start = cx * 10 + 2 * half_y + par
                means[c, pl.ds(start, n, stride=10 * cx_step + 2 * half_step), :] = piece
    load.wait()
    low_x = (shift[0] == 1).astype(jnp.int32)
    low_y = (shift[1] == 1).astype(jnp.int32)
    for c in range(3):
        for cx in range(CXL):
            flow[c, cx * 8 : cx * 8 + 8, :] = means[c, pl.ds((cx + low_x) * 10 + low_y, 8), :]
    store(flow, flow_hbm)
    for copy in stores:
        copy.wait()


def shape(*dims):
    return jax.ShapeDtypeStruct(dims, F32)


def per_device(velocity, position, leaving, grid_shift, axis_index):
    vel = velocity.reshape(3, ROWS, 128)
    pos = position.reshape(3, ROWS, 128)
    axis = axis_index.reshape(64, 128)
    leaving = leaving.reshape(4)
    vel, pos, axis, leaving, grid_shift = [
        pltpu.with_memory_space_constraint(v, pltpu.HBM) for v in (vel, pos, axis, leaving, grid_shift)
    ]
    vmem = pl.BlockSpec(memory_space=pltpu.VMEM)
    hbm = pl.BlockSpec(memory_space=pltpu.HBM)
    parts = pl.pallas_call(
        prep_kernel,
        name="prep",
        out_shape=(
            shape(8 * BORDER + 8, 128),
            shape(2, 56, 128),
            shape(ROWS, 128),
            shape(3, 112, 128),
            shape(4, ROWS, 128),
            shape(3, ROWS, 128),
            shape(4, 144, 128),
            shape(4, 24, 128),
        ),
        in_specs=[hbm] * 5,
        out_specs=(vmem,) * 8,
        scratch_shapes=[
            pltpu.SMEM((4,), jnp.int32),
            pltpu.SMEM((3,), jnp.int32),
            pltpu.VMEM((3, ROWS, 128), F32),
            pltpu.VMEM((64, 128), jnp.int32),
            pltpu.VMEM((ROWS, 128), F32),
            pltpu.VMEM((ROWS, 128), F32),
            pltpu.VMEM((7 * MAIN + 16, 256), F32),
            pltpu.VMEM((2, 136, 128), F32),
            pltpu.VMEM((32, 128), F32),
            pltpu.VMEM((144, 128), F32),
            pltpu.VMEM((4, 144, 128), F32),
            pltpu.VMEM((4, 24, 128), F32),
            pltpu.SemaphoreType.DMA((5,)),
            pltpu.SemaphoreType.DMA((8,)),
            pltpu.SemaphoreType.DMA((8,)),
        ],
        compiler_params=pltpu.CompilerParams(
            collective_id=0, has_side_effects=True, vmem_limit_bytes=32 << 20
        ),
    )(leaving, grid_shift, vel, pos, axis)
    out, flow = pl.pallas_call(
        collide_kernel,
        name="collide",
        out_shape=(shape(3, SLOTS, 128), shape(3, 64, 128)),
        in_specs=[hbm] + [vmem] * 8,
        out_specs=(hbm, hbm),
        scratch_shapes=[
            pltpu.SMEM((3,), jnp.int32),
            pltpu.VMEM((3, SLOTS, 128), F32),
            pltpu.VMEM((3, 64, 128), F32),
            pltpu.VMEM((8 * BORDER + 8, 128), F32),
            pltpu.VMEM((3, 112, 128), F32),
            pltpu.SemaphoreType.DMA,
            pltpu.SemaphoreType.DMA((3,)),
        ],
        compiler_params=pltpu.CompilerParams(vmem_limit_bytes=32 << 20),
    )(grid_shift, *parts)
    return out.reshape(3, 1, 1, SLOTS * 128), flow.reshape(3, 1, 1, 64 * 128)


def solution(mesh):
    return jax.shard_map(
        per_device,
        mesh=mesh,
        in_specs=(
            P(None, "gx", "gy", None),
            P(None, "gx", "gy", None),
            P("gx", "gy", None),
            P(),
            P("gx", "gy", None),
        ),
        out_specs=(P(None, "gx", "gy", None), P(None, "gx", "gy", None)),
        check_vma=False,
    )
```
